256 devices in a mesh: dp: 32 (over y_lo, z, core), seq: 8 (over y_hi, x).
Axes of the slice: x: 4, y: 4 (y_hi: 2, y_lo: 2; y = y_hi * 2 + y_lo), z: 8, core: 2. Of those that a mesh axis runs over, the one named last changes fastest.
Arguments:
- inputs: bfloat16 [32, 2048, 1024], P('dp', 'seq'), may hold values from -6 to 6
- d_output: bfloat16 [32, 2048, 1024], P('dp', 'seq'), may hold values from -0.046875 to 0.046875
- loss_mask: int32 [32, 2048], P('dp', 'seq'), may hold values 0 or 1
- queries: bfloat16 [32, 2048, 8, 128], P('dp', None, 'seq'), may hold values from -10 to 10
- keys: bfloat16 [32, 2048, 8, 128], P('dp', None, 'seq'), may hold values from -10 to 10
- values: bfloat16 [32, 2048, 8, 128], P('dp', None, 'seq'), may hold values from -6 to 6
- out_weight: bfloat16 [1024, 1024], P('dp'), may hold values from -0.1875 to 0.1875
- block_mask: int32 [32, 8, 16, 16], P('dp', 'seq'), may hold values from 0 to 1, as said below
Outputs:
- grad_query: float32 [128, 8, 1024], P('dp', 'seq')
- grad_key: float32 [128, 8, 1024], P('dp', 'seq')
- grad_value: float32 [128, 8, 1024], P('dp', 'seq')
- grad_out: float32 [128, 8, 1024], P('dp', 'seq')
The draws below stay inside these ranges and needn't reach their ends.
Inputs may be any that keep to these rules, and one draw needn't show every extreme that they name: `block_mask`: every block on the diagonal is 1.
All inputs are finite; a program needn't handle non-finite values. No bound on the sum of `loss_mask` on one device may be relied on, other than what follows from the above.
Results may differ from the reference program's by a relative error of at most 0.025.
Values may be sent and summed in bfloat16 or wider, within the bound.
A program may use at most 128 MiB of HBM per device.

```python
import jax
import jax.numpy as jnp
from jax import lax

DW = 1024
HW = 8
HD = 128
BLOCK = 128
TOK_DEV = 256
SEQS = 32
LEN = 2048
NBLK = 16
N_DP = 32
N_SEQ = 8


def drawn_pair(key):
    query_draw = jnp.clip(1.5 * jax.random.normal(jax.random.fold_in(key, 11), (SEQS, LEN, HW, HD), jnp.float32), -9.0, 9.0)
    key_draw = jnp.clip(1.5 * jax.random.normal(jax.random.fold_in(key, 12), (SEQS, LEN, HW, HD), jnp.float32), -9.0, 9.0)
    return (query_draw, key_draw)


def draw_queries(key, part):
    return drawn_pair(key)[0].astype(jnp.bfloat16)


def draw_keys(key, part):
    return drawn_pair(key)[1].astype(jnp.bfloat16)


def draw_block_mask(key, part):
    band_width = jax.random.randint(jax.random.fold_in(key, 21), (SEQS, HW, 1, 1), 1, NBLK + 1)
    extra_block = jax.random.randint(jax.random.fold_in(key, 22), (SEQS, HW, NBLK, NBLK), 0, 8) == 0
    row_ids = jnp.arange(NBLK)[:, None]
    col_ids = jnp.arange(NBLK)[None, :]
    in_band = jnp.abs(row_ids - col_ids) < band_width
    return jnp.logical_or(in_band, extra_block).astype(jnp.int32)


def with_ends(entries, key, smallest, top_value):
    spot = [jax.random.randint(jax.random.fold_in(key, axis), (), 0, length) for axis, length in enumerate(entries.shape)]
    main_axis = entries.shape.index(max(entries.shape))
    next_to = spot[:main_axis] + [(spot[main_axis] + 1) % entries.shape[main_axis]] + spot[main_axis + 1:]
    return entries.at[tuple(spot)].set(smallest).at[tuple(next_to)].set(top_value)


def steps_of(own_key, shape, shards, least, largest):
    loudness, own = 1.0, jax.random.fold_in(own_key, 6)
    for axis_at, parts in shards:
        draws = jnp.exp(jax.random.uniform(jax.random.fold_in(own, axis_at), (parts,), jnp.float32, least / len(shards), largest / len(shards)))
        loudness = loudness * jnp.repeat(draws, shape[axis_at] // parts).reshape([-1 if axis == axis_at else 1 for axis in range(len(shape))])
    return loudness


def centred(own_key, shape, spread, limit, pieces=(), held_as=jnp.bfloat16):
    drawn = jax.random.normal(own_key, shape, jnp.float32) * spread
    if len(pieces) > 0:
        drawn = steps_of(own_key, shape, pieces, -0.22, 0.18) * drawn
    return jnp.clip(drawn, min=-limit, max=limit).astype(held_as)


def setup_inputs(seed: int = 0) -> dict:
    seeds = jax.random.split(jax.random.key(seed), 9)
    inputs = centred(seeds[0], (SEQS, LEN, DW), 1.0, 6.0, ((0, 32), (1, 8)))
    d_output = centred(seeds[1], (SEQS, LEN, DW), (2.0 * (TOK_DEV * N_SEQ * N_DP) ** -0.5), 0.046875, ((0, 32), (1, 8)))
    loss_mask = with_ends((jax.random.randint(seeds[2], (SEQS, LEN), 0, 2) < 1).astype(jnp.int32), jax.random.fold_in(seeds[2], 1), 0, 1)
    queries = draw_queries(jax.random.fold_in(seeds[8], 71), 0)
    keys = draw_keys(jax.random.fold_in(seeds[8], 71), 0)
    values = centred(seeds[5], (SEQS, LEN, HW, HD), 1.0, 6.0, ((0, 32), (2, 8)))
    out_weight = centred(seeds[6], (HW * HD, DW), DW ** -0.5, 0.1875, ((0, 32),))
    block_mask = draw_block_mask(jax.random.fold_in(seeds[8], 71), 0)
    return dict(inputs=inputs, d_output=d_output, loss_mask=loss_mask, queries=queries, keys=keys, values=values, out_weight=out_weight, block_mask=block_mask)


masked_score = -1.0e30


def expand_blocks(blocks, block_size):
    block_count = blocks.shape[0]
    live_blocks = blocks[:, None, :, None] > 0
    return jnp.broadcast_to(live_blocks, (block_count, block_size, block_count, block_size)).reshape(block_count * block_size, block_count * block_size)


def head_backward(query_rows, key_rows, value_rows, grad_rows, blocks):
    softmax_scale = HD ** -0.5
    allowed = expand_blocks(blocks, BLOCK)
    scores = jnp.dot(query_rows, key_rows.T, preferred_element_type=jnp.float32) * softmax_scale
    scores = jnp.where(allowed, scores, masked_score)
    row_max = jnp.max(scores, axis=1, keepdims=True)
    weights = jnp.exp(scores - row_max)
    row_total = jnp.sum(weights, axis=1, keepdims=True)
    prob_full = weights / row_total
    prob_low = prob_full.astype(jnp.bfloat16)
    attended = jnp.dot(prob_low, value_rows, preferred_element_type=jnp.float32).astype(jnp.bfloat16)
    row_delta = jnp.sum(grad_rows.astype(jnp.float32) * attended.astype(jnp.float32), axis=1, keepdims=True)
    d_prob = jnp.dot(grad_rows, value_rows.T, preferred_element_type=jnp.float32)
    d_score = (prob_full * (d_prob - row_delta)).astype(jnp.bfloat16)
    d_value = jnp.dot(prob_low.T, grad_rows, preferred_element_type=jnp.float32).astype(jnp.bfloat16)
    d_query = (jnp.dot(d_score, key_rows, preferred_element_type=jnp.float32) * softmax_scale).astype(jnp.bfloat16)
    d_key = (jnp.dot(d_score.T, query_rows, preferred_element_type=jnp.float32) * softmax_scale).astype(jnp.bfloat16)
    return d_query, d_key, d_value, attended


def reference(inputs, d_output, loss_mask, queries, keys, values, out_weight, block_mask):
    def one_sequence(grad_sum, seq_index):
        layer_in = inputs[seq_index]
        masked = d_output[seq_index] * loss_mask[seq_index][:, None].astype(jnp.bfloat16)
        d_attn = jnp.dot(masked, out_weight.T, preferred_element_type=jnp.float32).astype(jnp.bfloat16).reshape(LEN, HW, HD)
        seq_queries = queries[seq_index]
        seq_keys = keys[seq_index]
        seq_values = values[seq_index]
        seq_blocks = block_mask[seq_index]

        def one_head(head_index):
            return head_backward(seq_queries[:, head_index], seq_keys[:, head_index], seq_values[:, head_index], d_attn[:, head_index], seq_blocks[head_index])

        d_query, d_key, d_value, attended = lax.map(one_head, jnp.arange(HW))
        inputs_wide = layer_in.astype(jnp.float32)
        masked_wide = masked.astype(jnp.float32)
        contributions = jnp.stack([
            jnp.einsum('htd,tf->dhf', d_query.astype(jnp.float32), inputs_wide),
            jnp.einsum('htd,tf->dhf', d_key.astype(jnp.float32), inputs_wide),
            jnp.einsum('htd,tf->dhf', d_value.astype(jnp.float32), inputs_wide),
            jnp.einsum('htd,tf->dhf', attended.astype(jnp.float32), masked_wide)], axis=0)
        return grad_sum + contributions, None

    initial = jnp.zeros((4, HD, HW, DW), jnp.float32)
    grad_sum, unused = lax.scan(one_sequence, initial, jnp.arange(SEQS))
    return grad_sum[0], grad_sum[1], grad_sum[2], grad_sum[3]
```

```python
import functools

import jax
import jax.numpy as jnp
from jax import lax
from jax.experimental import pallas as pl
from jax.experimental.pallas import tpu as pltpu
from jax.sharding import PartitionSpec as P

HD = 128
BLOCK = 128
ROWS = 256

masked_score = -1e30


def attention_kernel(q_ref, k_ref, v_ref, g_ref, m_ref, dq_ref, att_ref, dk_ref, dv_ref, dk_acc, dv_acc):
    step = pl.program_id(0)
    steps = pl.num_programs(0)
    scale = HD ** (-0.5)
    groups = ROWS // BLOCK

    @pl.when(step == 0)
    def _():
        dk_acc[...] = jnp.zeros_like(dk_acc)
        dv_acc[...] = jnp.zeros_like(dv_acc)

    q = q_ref[...]
    k = k_ref[...]
    v = v_ref[...]
    g = g_ref[...]
    length = k.shape[0]
    nt = (((1,), (1,)), ((), ()))
    tn = (((0,), (0,)), ((), ()))
    scores = lax.dot_general(q, k, nt, preferred_element_type=jnp.float32) * scale
    live = m_ref[...]
    scores = scores.reshape(groups, BLOCK, length)
    scores = jnp.where(live > 0, scores, masked_score).reshape(ROWS, length)
    row_max = jnp.max(scores, axis=1, keepdims=True)
    weights = jnp.exp(scores - row_max)
    row_total = jnp.sum(weights, axis=1, keepdims=True)
    prob = weights / row_total
    prob_low = prob.astype(jnp.bfloat16)
    attended = jnp.dot(prob_low, v, preferred_element_type=jnp.float32).astype(jnp.bfloat16)
    row_delta = jnp.sum(g.astype(jnp.float32) * attended.astype(jnp.float32), axis=1, keepdims=True)
    d_prob = lax.dot_general(g, v, nt, preferred_element_type=jnp.float32)
    d_score = (prob * (d_prob - row_delta)).astype(jnp.bfloat16)
    dq_ref[...] = (jnp.dot(d_score, k, preferred_element_type=jnp.float32) * scale).astype(jnp.bfloat16)
    att_ref[...] = attended
    dk_acc[...] += lax.dot_general(d_score, q, tn, preferred_element_type=jnp.float32)
    dv_acc[...] += lax.dot_general(prob_low, g, tn, preferred_element_type=jnp.float32)

    @pl.when(step == steps - 1)
    def _():
        dk_ref[...] = (dk_acc[...] * scale).astype(jnp.bfloat16)
        dv_ref[...] = dv_acc[...].astype(jnp.bfloat16)


def attention_backward(q, k, v, g, live_cols):
    length = q.shape[0]
    row_spec = pl.BlockSpec((ROWS, HD), lambda i: (i, 0))
    full_spec = pl.BlockSpec((length, HD), lambda i: (0, 0))
    mask_spec = pl.BlockSpec((ROWS // BLOCK, 1, length), lambda i: (i, 0, 0))
    out = jax.ShapeDtypeStruct((length, HD), jnp.bfloat16)
    flops = 12 * length * length * HD
    return pl.pallas_call(
        attention_kernel,
        grid=(length // ROWS,),
        in_specs=[row_spec, full_spec, full_spec, row_spec, mask_spec],
        out_specs=[row_spec, row_spec, full_spec, full_spec],
        out_shape=[out, out, out, out],
        scratch_shapes=[pltpu.VMEM((length, HD), jnp.float32), pltpu.VMEM((length, HD), jnp.float32)],
        compiler_params=pltpu.CompilerParams(vmem_limit_bytes=48 * 1024 * 1024),
        cost_estimate=pl.CostEstimate(
            flops=flops, transcendentals=length * length, bytes_accessed=8 * length * HD * 2
        ),
    )(q, k, v, g, live_cols)


def local(inputs, d_output, loss_mask, queries, keys, values, out_weight, block_mask):
    head = lax.axis_index("seq")
    row_owner = lax.axis_index("dp")
    masked = d_output[0] * loss_mask[0][:, None].astype(jnp.bfloat16)
    own_rows = out_weight.shape[0]
    per_head = HD // own_rows
    placed = jnp.zeros((per_head, own_rows, out_weight.shape[1]), out_weight.dtype)
    placed = lax.dynamic_update_index_in_dim(placed, out_weight, row_owner % per_head, 0)
    placed = jnp.where(row_owner // per_head == head, placed, jnp.zeros_like(placed))
    head_weight = lax.psum(placed.reshape(HD, out_weight.shape[1]), "dp")
    masked_all = lax.all_gather(masked, "seq", axis=0, tiled=True)
    inputs_all = lax.all_gather(inputs[0], "seq", axis=0, tiled=True)
    d_attn = lax.dot_general(
        masked_all, head_weight, (((1,), (1,)), ((), ())), preferred_element_type=jnp.float32
    ).astype(jnp.bfloat16)
    blocks = block_mask[0, 0]
    live_cols = jnp.repeat(blocks, BLOCK, axis=1)[:, None, :]
    d_query, attended, d_key, d_value = attention_backward(
        queries[0, :, 0], keys[0, :, 0], values[0, :, 0], d_attn, live_cols
    )
    tn = (((0,), (0,)), ((), ()))
    terms = jnp.stack(
        [
            lax.dot_general(d_query, inputs_all, tn, preferred_element_type=jnp.float32),
            lax.dot_general(d_key, inputs_all, tn, preferred_element_type=jnp.float32),
            lax.dot_general(d_value, inputs_all, tn, preferred_element_type=jnp.float32),
            lax.dot_general(attended, masked_all, tn, preferred_element_type=jnp.float32),
        ],
        axis=1,
    )
    owned = lax.psum_scatter(terms, "dp", scatter_dimension=0, tiled=True)
    return tuple(owned[:, part][:, None, :] for part in range(4))


def solution(mesh):
    in_specs = (
        P("dp", "seq", None),
        P("dp", "seq", None),
        P("dp", "seq"),
        P("dp", None, "seq", None),
        P("dp", None, "seq", None),
        P("dp", None, "seq", None),
        P("dp", None),
        P("dp", "seq", None, None),
    )
    out_specs = (
        P("dp", "seq", None),
        P("dp", "seq", None),
        P("dp", "seq", None),
        P("dp", "seq", None),
    )
    return jax.shard_map(local, mesh=mesh, in_specs=in_specs, out_specs=out_specs, check_vma=False)
```

```python
import functools

import jax
import jax.numpy as jnp
from jax import lax
from jax.experimental import pallas as pl
from jax.experimental.pallas import tpu as pltpu
from jax.sharding import PartitionSpec as P

HD = 128
BLOCK = 128
ROWS = 256

masked_score = -1e30


def attention_kernel(q_ref, k_ref, v_ref, g_ref, m_ref, dq_ref, att_ref, dk_ref, dv_ref, dk_acc, dv_acc):
    step = pl.program_id(0)
    steps = pl.num_programs(0)
    scale = HD ** (-0.5)
    groups = ROWS // BLOCK

    @pl.when(step == 0)
    def _():
        dk_acc[...] = jnp.zeros_like(dk_acc)
        dv_acc[...] = jnp.zeros_like(dv_acc)

    q = q_ref[...]
    k = k_ref[...]
    v = v_ref[...]
    g = g_ref[...]
    length = k.shape[0]
    nt = (((1,), (1,)), ((), ()))
    tn = (((0,), (0,)), ((), ()))
    scores = lax.dot_general(q, k, nt, preferred_element_type=jnp.float32) * scale
    live = m_ref[...]
    scores = scores.reshape(groups, BLOCK, length)
    scores = jnp.where(live > 0, scores, masked_score).reshape(ROWS, length)
    row_max = jnp.max(scores, axis=1, keepdims=True)
    weights = jnp.exp(scores - row_max)
    row_total = jnp.sum(weights, axis=1, keepdims=True)
    prob = weights / row_total
    prob_low = prob.astype(jnp.bfloat16)
    attended = jnp.dot(prob_low, v, preferred_element_type=jnp.float32).astype(jnp.bfloat16)
    row_delta = jnp.sum(g.astype(jnp.float32) * attended.astype(jnp.float32), axis=1, keepdims=True)
    d_prob = lax.dot_general(g, v, nt, preferred_element_type=jnp.float32)
    d_score = (prob * (d_prob - row_delta)).astype(jnp.bfloat16)
    dq_ref[...] = (jnp.dot(d_score, k, preferred_element_type=jnp.float32) * scale).astype(jnp.bfloat16)
    att_ref[...] = attended
    dk_acc[...] += lax.dot_general(d_score, q, tn, preferred_element_type=jnp.float32)
    dv_acc[...] += lax.dot_general(prob_low, g, tn, preferred_element_type=jnp.float32)

    @pl.when(step == steps - 1)
    def _():
        dk_ref[...] = (dk_acc[...] * scale).astype(jnp.bfloat16)
        dv_ref[...] = dv_acc[...].astype(jnp.bfloat16)


def attention_backward(q, k, v, g, live_cols):
    length = q.shape[0]
    row_spec = pl.BlockSpec((ROWS, HD), lambda i: (i, 0))
    full_spec = pl.BlockSpec((length, HD), lambda i: (0, 0))
    mask_spec = pl.BlockSpec((ROWS // BLOCK, 1, length), lambda i: (i, 0, 0))
    out = jax.ShapeDtypeStruct((length, HD), jnp.bfloat16)
    flops = 12 * length * length * HD
    return pl.pallas_call(
        attention_kernel,
        grid=(length // ROWS,),
        in_specs=[row_spec, full_spec, full_spec, row_spec, mask_spec],
        out_specs=[row_spec, row_spec, full_spec, full_spec],
        out_shape=[out, out, out, out],
        scratch_shapes=[pltpu.VMEM((length, HD), jnp.float32), pltpu.VMEM((length, HD), jnp.float32)],
        compiler_params=pltpu.CompilerParams(vmem_limit_bytes=48 * 1024 * 1024),
        cost_estimate=pl.CostEstimate(
            flops=flops, transcendentals=length * length, bytes_accessed=8 * length * HD * 2
        ),
    )(q, k, v, g, live_cols)


DP = ("dpy", "dpz", "dpc")
SQ = ("sqy", "sqx")


def local(inputs, d_output, loss_mask, queries, keys, values, out_weight, block_mask):
    sizes = {name: lax.axis_size(name) for name in DP + SQ}
    head = lax.axis_index("sqy") * sizes["sqx"] + lax.axis_index("sqx")
    masked = d_output[0] * loss_mask[0][:, None].astype(jnp.bfloat16)
    own_rows, width = out_weight.shape
    gathered = lax.all_gather(out_weight, "dpc", axis=0)
    gathered = lax.all_gather(gathered, "dpy", axis=0)
    gathered = lax.all_gather(gathered, "dpz", axis=0)
    gathered = jnp.transpose(gathered, (1, 0, 2, 3, 4)).reshape(-1, width)
    head_weight = lax.dynamic_slice_in_dim(gathered, head * HD, HD, 0)
    masked_all = lax.all_gather(lax.all_gather(masked, "sqy", axis=0), "sqx", axis=0)
    inputs_all = lax.all_gather(lax.all_gather(inputs[0], "sqy", axis=0), "sqx", axis=0)
    masked_all = jnp.transpose(masked_all, (1, 0, 2, 3)).reshape(-1, width)
    inputs_all = jnp.transpose(inputs_all, (1, 0, 2, 3)).reshape(-1, width)
    d_attn = lax.dot_general(
        masked_all, head_weight, (((1,), (1,)), ((), ())), preferred_element_type=jnp.float32
    ).astype(jnp.bfloat16)
    blocks = block_mask[0, 0]
    live_cols = jnp.repeat(blocks, BLOCK, axis=1)[:, None, :]
    d_query, attended, d_key, d_value = attention_backward(
        queries[0, :, 0], keys[0, :, 0], values[0, :, 0], d_attn, live_cols
    )
    tn = (((0,), (0,)), ((), ()))
    terms = jnp.stack(
        [
            lax.dot_general(d_query, inputs_all, tn, preferred_element_type=jnp.float32),
            lax.dot_general(d_key, inputs_all, tn, preferred_element_type=jnp.float32),
            lax.dot_general(d_value, inputs_all, tn, preferred_element_type=jnp.float32),
            lax.dot_general(attended, masked_all, tn, preferred_element_type=jnp.float32),
        ],
        axis=1,
    )
    chunk = terms.shape[0] // (sizes["dpy"] * sizes["dpz"] * sizes["dpc"])
    terms = terms.reshape(sizes["dpy"], sizes["dpz"], sizes["dpc"], chunk, 4, width)
    terms = jnp.transpose(terms, (2, 0, 1, 3, 4, 5)).reshape(-1, 4 * width // 128, 128)
    owned = lax.psum_scatter(terms, "dpc", scatter_dimension=0, tiled=True)
    owned = lax.psum_scatter(owned, "dpy", scatter_dimension=0, tiled=True)
    owned = lax.psum_scatter(owned, "dpz", scatter_dimension=0, tiled=True)
    owned = owned.reshape(chunk, 4, width)
    return tuple(owned[:, part][:, None, :] for part in range(4))


def solution(mesh):
    dp, seq = mesh.devices.shape
    devices = mesh.devices.reshape(2, dp // 4, 2, 2, seq // 2)
    fine = jax.sharding.Mesh(devices, DP + SQ)
    in_specs = (
        P(DP, SQ, None),
        P(DP, SQ, None),
        P(DP, SQ),
        P(DP, None, SQ, None),
        P(DP, None, SQ, None),
        P(DP, None, SQ, None),
        P(DP, None),
        P(DP, SQ, None, None),
    )
    out_specs = (
        P(DP, SQ, None),
        P(DP, SQ, None),
        P(DP, SQ, None),
        P(DP, SQ, None),
    )
    return jax.shard_map(local, mesh=fine, in_specs=in_specs, out_specs=out_specs, check_vma=False)
```

```python
import functools

import jax
import jax.numpy as jnp
from jax import lax
from jax.experimental import pallas as pl
from jax.experimental.pallas import tpu as pltpu
from jax.sharding import PartitionSpec as P

HD = 128
BLOCK = 128
ROWS = 256

masked_score = -1e30


def attention_kernel(q_ref, k_ref, v_ref, g_ref, m_ref, dq_ref, att_ref, dk_ref, dv_ref, dk_acc, dv_acc):
    step = pl.program_id(0)
    steps = pl.num_programs(0)
    scale = HD ** (-0.5)
    groups = ROWS // BLOCK

    @pl.when(step == 0)
    def _():
        dk_acc[...] = jnp.zeros_like(dk_acc)
        dv_acc[...] = jnp.zeros_like(dv_acc)

    q = q_ref[...]
    k = k_ref[...]
    v = v_ref[...]
    g = g_ref[...]
    length = k.shape[0]
    nt = (((1,), (1,)), ((), ()))
    tn = (((0,), (0,)), ((), ()))
    scores = lax.dot_general(q, k, nt, preferred_element_type=jnp.float32) * scale
    live = m_ref[...]
    scores = scores.reshape(groups, BLOCK, length)
    scores = jnp.where(live > 0, scores, masked_score).reshape(ROWS, length)
    row_max = jnp.max(scores, axis=1, keepdims=True)
    weights = jnp.exp(scores - row_max)
    row_total = jnp.sum(weights, axis=1, keepdims=True)
    prob = weights / row_total
    prob_low = prob.astype(jnp.bfloat16)
    attended = jnp.dot(prob_low, v, preferred_element_type=jnp.float32).astype(jnp.bfloat16)
    row_delta = jnp.sum(g.astype(jnp.float32) * attended.astype(jnp.float32), axis=1, keepdims=True)
    d_prob = lax.dot_general(g, v, nt, preferred_element_type=jnp.float32)
    d_score = (prob * (d_prob - row_delta)).astype(jnp.bfloat16)
    dq_ref[...] = (jnp.dot(d_score, k, preferred_element_type=jnp.float32) * scale).astype(jnp.bfloat16)
    att_ref[...] = attended
    dk_acc[...] += lax.dot_general(d_score, q, tn, preferred_element_type=jnp.float32)
    dv_acc[...] += lax.dot_general(prob_low, g, tn, preferred_element_type=jnp.float32)

    @pl.when(step == steps - 1)
    def _():
        dk_ref[...] = (dk_acc[...] * scale).astype(jnp.bfloat16)
        dv_ref[...] = dv_acc[...].astype(jnp.bfloat16)


def attention_backward(q, k, v, g, live_cols):
    length = q.shape[0]
    row_spec = pl.BlockSpec((ROWS, HD), lambda i: (i, 0))
    full_spec = pl.BlockSpec((length, HD), lambda i: (0, 0))
    mask_spec = pl.BlockSpec((ROWS // BLOCK, 1, length), lambda i: (i, 0, 0))
    out = jax.ShapeDtypeStruct((length, HD), jnp.bfloat16)
    flops = 12 * length * length * HD
    return pl.pallas_call(
        attention_kernel,
        grid=(length // ROWS,),
        in_specs=[row_spec, full_spec, full_spec, row_spec, mask_spec],
        out_specs=[row_spec, row_spec, full_spec, full_spec],
        out_shape=[out, out, out, out],
        scratch_shapes=[pltpu.VMEM((length, HD), jnp.float32), pltpu.VMEM((length, HD), jnp.float32)],
        compiler_params=pltpu.CompilerParams(vmem_limit_bytes=48 * 1024 * 1024),
        cost_estimate=pl.CostEstimate(
            flops=flops, transcendentals=length * length, bytes_accessed=8 * length * HD * 2
        ),
    )(q, k, v, g, live_cols)


def gather_kernel(nseq, sx, a_ref, b_ref, a_out, b_out, send_sem, recv_sem, copy_sem):
    me = lax.axis_index("sqy") * sx + lax.axis_index("sqx")
    mesh_id = pl.DeviceIdType.MESH
    barrier = pltpu.get_barrier_semaphore()
    for off in range(1, nseq):
        peer = (me + off) % nseq
        pl.semaphore_signal(barrier, 1, device_id={"sqy": peer // sx, "sqx": peer % sx}, device_id_type=mesh_id)
    pl.semaphore_wait(barrier, nseq - 1)
    copies = []
    for t, (src, dst) in enumerate(((a_ref, a_out), (b_ref, b_out))):
        local = pltpu.make_async_copy(src, dst.at[me], copy_sem.at[t])
        local.start()
        copies.append(local)
        for off in range(1, nseq):
            peer = (me + off) % nseq
            remote = pltpu.make_async_remote_copy(
                src_ref=src,
                dst_ref=dst.at[me],
                send_sem=send_sem.at[t, off - 1],
                recv_sem=recv_sem.at[t, off - 1],
                device_id={"sqy": peer // sx, "sqx": peer % sx},
                device_id_type=mesh_id,
            )
            remote.start()
            copies.append(remote)
    for copy in copies:
        copy.wait()


def seq_gather(a, b, nseq, sx):
    any_spec = pl.BlockSpec(memory_space=pl.ANY)
    out = jax.ShapeDtypeStruct((nseq,) + a.shape, a.dtype)
    return pl.pallas_call(
        functools.partial(gather_kernel, nseq, sx),
        in_specs=[any_spec, any_spec],
        out_specs=[any_spec, any_spec],
        out_shape=[out, out],
        scratch_shapes=[
            pltpu.SemaphoreType.DMA((2, nseq - 1)),
            pltpu.SemaphoreType.DMA((2, nseq - 1)),
            pltpu.SemaphoreType.DMA((2,)),
        ],
        compiler_params=pltpu.CompilerParams(collective_id=0, has_side_effects=True),
    )(a, b)


DP = ("dpy", "dpz", "dpc")
SQ = ("sqy", "sqx")


def local(inputs, d_output, loss_mask, queries, keys, values, out_weight, block_mask):
    sizes = {name: lax.axis_size(name) for name in DP + SQ}
    head = lax.axis_index("sqy") * sizes["sqx"] + lax.axis_index("sqx")
    masked = d_output[0] * loss_mask[0][:, None].astype(jnp.bfloat16)
    own_rows, width = out_weight.shape
    gathered = lax.all_gather(out_weight, "dpc", axis=0)
    gathered = lax.all_gather(gathered, "dpy", axis=0)
    gathered = lax.all_gather(gathered, "dpz", axis=0)
    gathered = jnp.transpose(gathered, (1, 0, 2, 3, 4)).reshape(-1, width)
    head_weight = lax.dynamic_slice_in_dim(gathered, head * HD, HD, 0)
    nseq = sizes["sqy"] * sizes["sqx"]
    masked_all, inputs_all = seq_gather(masked, inputs[0], nseq, sizes["sqx"])
    masked_all = masked_all.reshape(-1, width)
    inputs_all = inputs_all.reshape(-1, width)
    d_attn = lax.dot_general(
        masked_all, head_weight, (((1,), (1,)), ((), ())), preferred_element_type=jnp.float32
    ).astype(jnp.bfloat16)
    blocks = block_mask[0, 0]
    live_cols = jnp.repeat(blocks, BLOCK, axis=1)[:, None, :]
    d_query, attended, d_key, d_value = attention_backward(
        queries[0, :, 0], keys[0, :, 0], values[0, :, 0], d_attn, live_cols
    )
    tn = (((0,), (0,)), ((), ()))
    terms = jnp.stack(
        [
            lax.dot_general(d_query, inputs_all, tn, preferred_element_type=jnp.float32),
            lax.dot_general(d_key, inputs_all, tn, preferred_element_type=jnp.float32),
            lax.dot_general(d_value, inputs_all, tn, preferred_element_type=jnp.float32),
            lax.dot_general(attended, masked_all, tn, preferred_element_type=jnp.float32),
        ],
        axis=1,
    )
    chunk = terms.shape[0] // (sizes["dpy"] * sizes["dpz"] * sizes["dpc"])
    terms = terms.reshape(sizes["dpy"], sizes["dpz"], sizes["dpc"], chunk, 4, width)
    terms = jnp.transpose(terms, (2, 0, 1, 3, 4, 5)).reshape(-1, 4 * width // 128, 128)
    owned = lax.psum_scatter(terms, "dpc", scatter_dimension=0, tiled=True)
    owned = lax.psum_scatter(owned, "dpy", scatter_dimension=0, tiled=True)
    owned = lax.psum_scatter(owned, "dpz", scatter_dimension=0, tiled=True)
    owned = owned.reshape(chunk, 4, width)
    return tuple(owned[:, part][:, None, :] for part in range(4))


def solution(mesh):
    dp, seq = mesh.devices.shape
    devices = mesh.devices.reshape(2, dp // 4, 2, 2, seq // 2)
    fine = jax.sharding.Mesh(devices, DP + SQ)
    in_specs = (
        P(DP, SQ, None),
        P(DP, SQ, None),
        P(DP, SQ),
        P(DP, None, SQ, None),
        P(DP, None, SQ, None),
        P(DP, None, SQ, None),
        P(DP, None),
        P(DP, SQ, None, None),
    )
    out_specs = (
        P(DP, SQ, None),
        P(DP, SQ, None),
        P(DP, SQ, None),
        P(DP, SQ, None),
    )
    return jax.shard_map(local, mesh=fine, in_specs=in_specs, out_specs=out_specs, check_vma=False)
```

```python
import functools

import jax
import jax.numpy as jnp
from jax import lax
from jax.experimental import pallas as pl
from jax.experimental.pallas import tpu as pltpu
from jax.sharding import PartitionSpec as P

HD = 128
BLOCK = 128
ROWS = 256

masked_score = -1e30


def attention_kernel(q_ref, k_ref, v_ref, g_ref, m_ref, dq_ref, att_ref, dk_ref, dv_ref, dk_acc, dv_acc):
    step = pl.program_id(0)
    steps = pl.num_programs(0)
    scale = HD ** (-0.5)
    groups = ROWS // BLOCK

    @pl.when(step == 0)
    def _():
        dk_acc[...] = jnp.zeros_like(dk_acc)
        dv_acc[...] = jnp.zeros_like(dv_acc)

    q = q_ref[...]
    k = k_ref[...]
    v = v_ref[...]
    g = g_ref[...]
    length = k.shape[0]
    nt = (((1,), (1,)), ((), ()))
    tn = (((0,), (0,)), ((), ()))
    scores = lax.dot_general(q, k, nt, preferred_element_type=jnp.float32) * scale
    live = m_ref[...]
    scores = scores.reshape(groups, BLOCK, length)
    scores = jnp.where(live > 0, scores, masked_score).reshape(ROWS, length)
    row_max = jnp.max(scores, axis=1, keepdims=True)
    weights = jnp.exp(scores - row_max)
    row_total = jnp.sum(weights, axis=1, keepdims=True)
    prob = weights / row_total
    prob_low = prob.astype(jnp.bfloat16)
    attended = jnp.dot(prob_low, v, preferred_element_type=jnp.float32).astype(jnp.bfloat16)
    row_delta = jnp.sum(g.astype(jnp.float32) * attended.astype(jnp.float32), axis=1, keepdims=True)
    d_prob = lax.dot_general(g, v, nt, preferred_element_type=jnp.float32)
    d_score = (prob * (d_prob - row_delta)).astype(jnp.bfloat16)
    dq_ref[...] = (jnp.dot(d_score, k, preferred_element_type=jnp.float32) * scale).astype(jnp.bfloat16)
    att_ref[...] = attended
    dk_acc[...] += lax.dot_general(d_score, q, tn, preferred_element_type=jnp.float32)
    dv_acc[...] += lax.dot_general(prob_low, g, tn, preferred_element_type=jnp.float32)

    @pl.when(step == steps - 1)
    def _():
        dk_ref[...] = (dk_acc[...] * scale).astype(jnp.bfloat16)
        dv_ref[...] = dv_acc[...].astype(jnp.bfloat16)


def attention_backward(q, k, v, g, live_cols):
    length = q.shape[0]
    row_spec = pl.BlockSpec((ROWS, HD), lambda i: (i, 0))
    full_spec = pl.BlockSpec((length, HD), lambda i: (0, 0))
    mask_spec = pl.BlockSpec((ROWS // BLOCK, 1, length), lambda i: (i, 0, 0))
    out = jax.ShapeDtypeStruct((length, HD), jnp.bfloat16)
    flops = 12 * length * length * HD
    return pl.pallas_call(
        attention_kernel,
        grid=(length // ROWS,),
        in_specs=[row_spec, full_spec, full_spec, row_spec, mask_spec],
        out_specs=[row_spec, row_spec, full_spec, full_spec],
        out_shape=[out, out, out, out],
        scratch_shapes=[pltpu.VMEM((length, HD), jnp.float32), pltpu.VMEM((length, HD), jnp.float32)],
        compiler_params=pltpu.CompilerParams(vmem_limit_bytes=48 * 1024 * 1024),
        cost_estimate=pl.CostEstimate(
            flops=flops, transcendentals=length * length, bytes_accessed=8 * length * HD * 2
        ),
    )(q, k, v, g, live_cols)


def gather_kernel(nseq, a_ref, b_ref, a_out, b_out, send_sem, recv_sem, copy_sem):
    me = lax.axis_index("sqx")
    mesh_id = pl.DeviceIdType.MESH
    barrier = pltpu.get_barrier_semaphore()
    for off in range(1, nseq):
        peer = (me + off) % nseq
        pl.semaphore_signal(barrier, 1, device_id={"sqx": peer}, device_id_type=mesh_id)
    pl.semaphore_wait(barrier, nseq - 1)
    copies = []
    for t, (src, dst) in enumerate(((a_ref, a_out), (b_ref, b_out))):
        local = pltpu.make_async_copy(src, dst.at[me], copy_sem.at[t])
        local.start()
        copies.append(local)
        for off in range(1, nseq):
            peer = (me + off) % nseq
            remote = pltpu.make_async_remote_copy(
                src_ref=src,
                dst_ref=dst.at[me],
                send_sem=send_sem.at[t, off - 1],
                recv_sem=recv_sem.at[t, off - 1],
                device_id={"sqx": peer},
                device_id_type=mesh_id,
            )
            remote.start()
            copies.append(remote)
    for copy in copies:
        copy.wait()


def seq_gather(a, b, nseq):
    any_spec = pl.BlockSpec(memory_space=pl.ANY)
    out = jax.ShapeDtypeStruct((nseq,) + a.shape, a.dtype)
    return pl.pallas_call(
        functools.partial(gather_kernel, nseq),
        in_specs=[any_spec, any_spec],
        out_specs=[any_spec, any_spec],
        out_shape=[out, out],
        scratch_shapes=[
            pltpu.SemaphoreType.DMA((2, nseq - 1)),
            pltpu.SemaphoreType.DMA((2, nseq - 1)),
            pltpu.SemaphoreType.DMA((2,)),
        ],
        compiler_params=pltpu.CompilerParams(collective_id=0, has_side_effects=True),
    )(a, b)


DP = ("dpy", "dpz", "dpc")
SQ = ("sqy", "sqx")


def local(inputs, d_output, loss_mask, queries, keys, values, out_weight, block_mask):
    sizes = {name: lax.axis_size(name) for name in DP + SQ}
    half = lax.axis_index("sqy")
    other = 1 - half
    col = lax.axis_index("sqx")
    head = half * sizes["sqx"] + col
    partner_head = other * sizes["sqx"] + col
    swap = [(0, 1), (1, 0)]
    masked = d_output[0] * loss_mask[0][:, None].astype(jnp.bfloat16)
    own_rows, width = out_weight.shape
    gathered = lax.all_gather(out_weight, "dpc", axis=0)
    gathered = lax.all_gather(gathered, "dpy", axis=0)
    gathered = lax.all_gather(gathered, "dpz", axis=0)
    gathered = jnp.transpose(gathered, (1, 0, 2, 3, 4)).reshape(-1, width)
    head_weight = lax.dynamic_slice_in_dim(gathered, head * HD, HD, 0)
    partner_weight = lax.dynamic_slice_in_dim(gathered, partner_head * HD, HD, 0)
    masked_half, inputs_half = seq_gather(masked, inputs[0], sizes["sqx"])
    masked_half = masked_half.reshape(-1, width)
    inputs_half = inputs_half.reshape(-1, width)
    half_len = masked_half.shape[0]
    nt = (((1,), (1,)), ((), ()))
    d_own = lax.dot_general(masked_half, head_weight, nt, preferred_element_type=jnp.float32).astype(jnp.bfloat16)
    d_give = lax.dot_general(masked_half, partner_weight, nt, preferred_element_type=jnp.float32).astype(jnp.bfloat16)
    d_got = lax.ppermute(d_give, "sqy", swap)
    d_attn = jnp.zeros((2 * half_len, HD), jnp.bfloat16)
    d_attn = lax.dynamic_update_slice_in_dim(d_attn, d_own, half * half_len, 0)
    d_attn = lax.dynamic_update_slice_in_dim(d_attn, d_got, other * half_len, 0)
    blocks = block_mask[0, 0]
    live_cols = jnp.repeat(blocks, BLOCK, axis=1)[:, None, :]
    d_query, attended, d_key, d_value = attention_backward(
        queries[0, :, 0], keys[0, :, 0], values[0, :, 0], d_attn, live_cols
    )
    grads = jnp.stack([d_query, d_key, d_value, attended])
    grads_own = lax.dynamic_slice_in_dim(grads, half * half_len, half_len, 1)
    grads_give = lax.dynamic_slice_in_dim(grads, other * half_len, half_len, 1)
    grads_got = lax.ppermute(grads_give, "sqy", swap)
    tn = (((0,), (0,)), ((), ()))

    def terms_of(parts):
        return jnp.stack(
            [
                lax.dot_general(parts[0], inputs_half, tn, preferred_element_type=jnp.float32),
                lax.dot_general(parts[1], inputs_half, tn, preferred_element_type=jnp.float32),
                lax.dot_general(parts[2], inputs_half, tn, preferred_element_type=jnp.float32),
                lax.dot_general(parts[3], masked_half, tn, preferred_element_type=jnp.float32),
            ],
            axis=1,
        )

    own_terms = terms_of(grads_own)
    got_terms = terms_of(grads_got)
    terms = jnp.where(half == 0, jnp.stack([own_terms, got_terms], 1), jnp.stack([got_terms, own_terms], 1))
    chunk = terms.shape[0] // (sizes["dpy"] * sizes["dpz"] * sizes["dpc"])
    terms = terms.reshape(sizes["dpy"], sizes["dpz"], sizes["dpc"], chunk, 2 * 4 * width)
    terms = jnp.transpose(terms, (2, 0, 1, 3, 4)).reshape(-1, 2 * 4 * width // 128, 128)
    owned = lax.psum_scatter(terms, "dpc", scatter_dimension=0, tiled=True)
    owned = lax.psum_scatter(owned, "dpy", scatter_dimension=0, tiled=True)
    owned = lax.psum_scatter(owned, "dpz", scatter_dimension=0, tiled=True)
    owned = owned.reshape(chunk, 2, 4 * width)
    kept = lax.dynamic_index_in_dim(owned, half, 1, keepdims=False)
    sent = lax.dynamic_index_in_dim(owned, other, 1, keepdims=False)
    owned = (kept + lax.ppermute(sent, "sqy", swap)).reshape(chunk, 4, width)
    return tuple(owned[:, part][:, None, :] for part in range(4))


def solution(mesh):
    dp, seq = mesh.devices.shape
    devices = mesh.devices.reshape(2, dp // 4, 2, 2, seq // 2)
    fine = jax.sharding.Mesh(devices, DP + SQ)
    in_specs = (
        P(DP, SQ, None),
        P(DP, SQ, None),
        P(DP, SQ),
        P(DP, None, SQ, None),
        P(DP, None, SQ, None),
        P(DP, None, SQ, None),
        P(DP, None),
        P(DP, SQ, None, None),
    )
    out_specs = (
        P(DP, SQ, None),
        P(DP, SQ, None),
        P(DP, SQ, None),
        P(DP, SQ, None),
    )
    return jax.shard_map(local, mesh=fine, in_specs=in_specs, out_specs=out_specs, check_vma=False)
```

```python
import functools

import jax
import jax.numpy as jnp
from jax import lax
from jax.experimental import pallas as pl
from jax.experimental.pallas import tpu as pltpu
from jax.sharding import PartitionSpec as P

HD = 128
BLOCK = 128
ROWS = 256

masked_score = -1e30


def attention_kernel(q_ref, k_ref, v_ref, g_ref, m_ref, dq_ref, att_ref, dk_ref, dv_ref, dk_acc, dv_acc):
    step = pl.program_id(0)
    steps = pl.num_programs(0)
    scale = HD ** (-0.5)
    groups = ROWS // BLOCK

    @pl.when(step == 0)
    def _():
        dk_acc[...] = jnp.zeros_like(dk_acc)
        dv_acc[...] = jnp.zeros_like(dv_acc)

    q = q_ref[...]
    k = k_ref[...]
    v = v_ref[...]
    g = g_ref[...]
    length = k.shape[0]
    nt = (((1,), (1,)), ((), ()))
    tn = (((0,), (0,)), ((), ()))
    scores = lax.dot_general(q, k, nt, preferred_element_type=jnp.float32) * scale
    live = m_ref[...]
    scores = scores.reshape(groups, BLOCK, length)
    scores = jnp.where(live > 0, scores, masked_score).reshape(ROWS, length)
    row_max = jnp.max(scores, axis=1, keepdims=True)
    weights = jnp.exp(scores - row_max)
    row_total = jnp.sum(weights, axis=1, keepdims=True)
    prob = weights / row_total
    prob_low = prob.astype(jnp.bfloat16)
    attended = jnp.dot(prob_low, v, preferred_element_type=jnp.float32).astype(jnp.bfloat16)
    row_delta = jnp.sum(g.astype(jnp.float32) * attended.astype(jnp.float32), axis=1, keepdims=True)
    d_prob = lax.dot_general(g, v, nt, preferred_element_type=jnp.float32)
    d_score = (prob * (d_prob - row_delta)).astype(jnp.bfloat16)
    dq_ref[...] = (jnp.dot(d_score, k, preferred_element_type=jnp.float32) * scale).astype(jnp.bfloat16)
    att_ref[...] = attended
    dk_acc[...] += lax.dot_general(d_score, q, tn, preferred_element_type=jnp.float32)
    dv_acc[...] += lax.dot_general(prob_low, g, tn, preferred_element_type=jnp.float32)

    @pl.when(step == steps - 1)
    def _():
        dk_ref[...] = (dk_acc[...] * scale).astype(jnp.bfloat16)
        dv_ref[...] = dv_acc[...].astype(jnp.bfloat16)


def attention_backward(q, k, v, g, live_cols):
    length = q.shape[0]
    row_spec = pl.BlockSpec((ROWS, HD), lambda i: (i, 0))
    full_spec = pl.BlockSpec((length, HD), lambda i: (0, 0))
    mask_spec = pl.BlockSpec((ROWS // BLOCK, 1, length), lambda i: (i, 0, 0))
    out = jax.ShapeDtypeStruct((length, HD), jnp.bfloat16)
    flops = 12 * length * length * HD
    return pl.pallas_call(
        attention_kernel,
        grid=(length // ROWS,),
        in_specs=[row_spec, full_spec, full_spec, row_spec, mask_spec],
        out_specs=[row_spec, row_spec, full_spec, full_spec],
        out_shape=[out, out, out, out],
        scratch_shapes=[pltpu.VMEM((length, HD), jnp.float32), pltpu.VMEM((length, HD), jnp.float32)],
        compiler_params=pltpu.CompilerParams(vmem_limit_bytes=48 * 1024 * 1024),
        cost_estimate=pl.CostEstimate(
            flops=flops, transcendentals=length * length, bytes_accessed=8 * length * HD * 2
        ),
    )(q, k, v, g, live_cols)


def gather_kernel(nseq, a_ref, b_ref, a_out, b_out, send_sem, recv_sem, copy_sem):
    me = lax.axis_index("sqx")
    mesh_id = pl.DeviceIdType.MESH
    barrier = pltpu.get_barrier_semaphore()
    for off in range(1, nseq):
        peer = (me + off) % nseq
        pl.semaphore_signal(barrier, 1, device_id={"sqx": peer}, device_id_type=mesh_id)
    pl.semaphore_wait(barrier, nseq - 1)
    copies = []
    for t, (src, dst) in enumerate(((a_ref, a_out), (b_ref, b_out))):
        local = pltpu.make_async_copy(src, dst.at[me], copy_sem.at[t])
        local.start()
        copies.append(local)
        for off in range(1, nseq):
            peer = (me + off) % nseq
            remote = pltpu.make_async_remote_copy(
                src_ref=src,
                dst_ref=dst.at[me],
                send_sem=send_sem.at[t, off - 1],
                recv_sem=recv_sem.at[t, off - 1],
                device_id={"sqx": peer},
                device_id_type=mesh_id,
            )
            remote.start()
            copies.append(remote)
    for copy in copies:
        copy.wait()


def seq_gather(a, b, nseq):
    any_spec = pl.BlockSpec(memory_space=pl.ANY)
    out = jax.ShapeDtypeStruct((nseq,) + a.shape, a.dtype)
    return pl.pallas_call(
        functools.partial(gather_kernel, nseq),
        in_specs=[any_spec, any_spec],
        out_specs=[any_spec, any_spec],
        out_shape=[out, out],
        scratch_shapes=[
            pltpu.SemaphoreType.DMA((2, nseq - 1)),
            pltpu.SemaphoreType.DMA((2, nseq - 1)),
            pltpu.SemaphoreType.DMA((2,)),
        ],
        compiler_params=pltpu.CompilerParams(collective_id=0, has_side_effects=True),
    )(a, b)


DP = ("dpy", "dpz", "dpc")
SQ = ("sqy", "sqx")


def local(inputs, d_output, loss_mask, queries, keys, values, out_weight, block_mask):
    sizes = {name: lax.axis_size(name) for name in DP + SQ}
    half = lax.axis_index("sqy")
    other = 1 - half
    col = lax.axis_index("sqx")
    head = half * sizes["sqx"] + col
    partner_head = other * sizes["sqx"] + col
    swap = [(0, 1), (1, 0)]
    masked = d_output[0] * loss_mask[0][:, None].astype(jnp.bfloat16)
    own_rows, width = out_weight.shape
    gathered = lax.all_gather(out_weight, "dpc", axis=0)
    gathered = lax.all_gather(gathered, "dpy", axis=0)
    gathered = lax.all_gather(gathered, "dpz", axis=0)
    gathered = jnp.transpose(gathered, (1, 0, 2, 3, 4)).reshape(-1, width)
    head_weight = lax.dynamic_slice_in_dim(gathered, head * HD, HD, 0)
    partner_weight = lax.dynamic_slice_in_dim(gathered, partner_head * HD, HD, 0)
    masked_half, inputs_half = seq_gather(masked, inputs[0], sizes["sqx"])
    masked_half = masked_half.reshape(-1, width)
    inputs_half = inputs_half.reshape(-1, width)
    half_len = masked_half.shape[0]
    nt = (((1,), (1,)), ((), ()))
    d_own = lax.dot_general(masked_half, head_weight, nt, preferred_element_type=jnp.float32).astype(jnp.bfloat16)
    d_give = lax.dot_general(masked_half, partner_weight, nt, preferred_element_type=jnp.float32).astype(jnp.bfloat16)
    d_got = lax.ppermute(d_give, "sqy", swap)
    d_attn = jnp.zeros((2 * half_len, HD), jnp.bfloat16)
    d_attn = lax.dynamic_update_slice_in_dim(d_attn, d_own, half * half_len, 0)
    d_attn = lax.dynamic_update_slice_in_dim(d_attn, d_got, other * half_len, 0)
    blocks = block_mask[0, 0]
    live_cols = jnp.repeat(blocks, BLOCK, axis=1)[:, None, :]
    d_query, attended, d_key, d_value = attention_backward(
        queries[0, :, 0], keys[0, :, 0], values[0, :, 0], d_attn, live_cols
    )
    grads = jnp.stack([d_query, d_key, d_value, attended])
    grads_own = lax.dynamic_slice_in_dim(grads, half * half_len, half_len, 1)
    grads_give = lax.dynamic_slice_in_dim(grads, other * half_len, half_len, 1)
    grads_got = lax.ppermute(grads_give, "sqy", swap)
    tn = (((0,), (0,)), ((), ()))

    def terms_of(parts):
        return jnp.stack(
            [
                lax.dot_general(parts[0], inputs_half, tn, preferred_element_type=jnp.float32),
                lax.dot_general(parts[1], inputs_half, tn, preferred_element_type=jnp.float32),
                lax.dot_general(parts[2], inputs_half, tn, preferred_element_type=jnp.float32),
                lax.dot_general(parts[3], masked_half, tn, preferred_element_type=jnp.float32),
            ],
            axis=0,
        )

    terms = jnp.stack([terms_of(grads_own), terms_of(grads_got)])
    ny, nz, nc = sizes["dpy"], sizes["dpz"], sizes["dpc"]
    chunk = terms.shape[2] // (ny * nz * nc)
    terms = terms.reshape(2, 4, ny, nz, nc, chunk, width)
    core = lax.axis_index("dpc")
    kept = lax.dynamic_index_in_dim(terms, core, 4, keepdims=False)
    sent = lax.dynamic_index_in_dim(terms, 1 - core, 4, keepdims=False)
    terms = kept + lax.ppermute(sent, "dpc", swap)
    row = lax.axis_index("dpy")
    kept = lax.dynamic_index_in_dim(terms, row, 2, keepdims=False)
    sent = lax.dynamic_index_in_dim(terms, 1 - row, 2, keepdims=False)
    terms = kept + lax.ppermute(sent, "dpy", swap)
    terms = jnp.transpose(terms.reshape(2, 4, nz, chunk * width), (2, 0, 1, 3))
    terms = lax.psum_scatter(terms.reshape(nz, -1, 128), "dpz", scatter_dimension=0, tiled=True)
    terms = terms.reshape(2, 4, chunk, width)
    owned = terms[0] + lax.ppermute(terms[1], "sqy", swap)
    owned = jnp.transpose(owned, (1, 0, 2))
    return tuple(owned[:, part][:, None, :] for part in range(4))


def solution(mesh):
    dp, seq = mesh.devices.shape
    devices = mesh.devices.reshape(2, dp // 4, 2, 2, seq // 2)
    fine = jax.sharding.Mesh(devices, DP + SQ)
    in_specs = (
        P(DP, SQ, None),
        P(DP, SQ, None),
        P(DP, SQ),
        P(DP, None, SQ, None),
        P(DP, None, SQ, None),
        P(DP, None, SQ, None),
        P(DP, None),
        P(DP, SQ, None, None),
    )
    out_specs = (
        P(DP, SQ, None),
        P(DP, SQ, None),
        P(DP, SQ, None),
        P(DP, SQ, None),
    )
    return jax.shard_map(local, mesh=fine, in_specs=in_specs, out_specs=out_specs, check_vma=False)
```

```python
import functools

import jax
import jax.numpy as jnp
from jax import lax
from jax.experimental import pallas as pl
from jax.experimental.pallas import tpu as pltpu
from jax.sharding import PartitionSpec as P

HD = 128
BLOCK = 128
ROWS = 256

masked_score = -1e30


def attention_kernel(
    nseq, q_ref, k_ref, v_ref, g_ref, m_ref, x_ref, dq_ref, att_ref, dk_ref, dv_ref, x_out,
    dk_acc, dv_acc, send_sem, recv_sem, copy_sem,
):
    step = pl.program_id(0)
    steps = pl.num_programs(0)
    scale = HD ** (-0.5)
    groups = ROWS // BLOCK
    copies = start_gather(nseq, x_ref, x_out, send_sem, recv_sem, copy_sem)

    @pl.when(step == 0)
    def _():
        enter_barrier(nseq)
        for copy in copies:
            copy.start()
        dk_acc[...] = jnp.zeros_like(dk_acc)
        dv_acc[...] = jnp.zeros_like(dv_acc)

    q = q_ref[...]
    k = k_ref[...]
    v = v_ref[...]
    g = g_ref[...]
    length = k.shape[0]
    nt = (((1,), (1,)), ((), ()))
    tn = (((0,), (0,)), ((), ()))
    scores = lax.dot_general(q, k, nt, preferred_element_type=jnp.float32) * scale
    live = m_ref[...]
    scores = scores.reshape(groups, BLOCK, length)
    scores = jnp.where(live > 0, scores, masked_score).reshape(ROWS, length)
    row_max = jnp.max(scores, axis=1, keepdims=True)
    weights = jnp.exp(scores - row_max)
    row_total = jnp.sum(weights, axis=1, keepdims=True)
    prob = weights / row_total
    prob_low = prob.astype(jnp.bfloat16)
    attended = jnp.dot(prob_low, v, preferred_element_type=jnp.float32).astype(jnp.bfloat16)
    row_delta = jnp.sum(g.astype(jnp.float32) * attended.astype(jnp.float32), axis=1, keepdims=True)
    d_prob = lax.dot_general(g, v, nt, preferred_element_type=jnp.float32)
    d_score = (prob * (d_prob - row_delta)).astype(jnp.bfloat16)
    dq_ref[...] = (jnp.dot(d_score, k, preferred_element_type=jnp.float32) * scale).astype(jnp.bfloat16)
    att_ref[...] = attended
    dk_acc[...] += lax.dot_general(d_score, q, tn, preferred_element_type=jnp.float32)
    dv_acc[...] += lax.dot_general(prob_low, g, tn, preferred_element_type=jnp.float32)

    @pl.when(step == steps - 1)
    def _():
        dk_ref[...] = (dk_acc[...] * scale).astype(jnp.bfloat16)
        dv_ref[...] = dv_acc[...].astype(jnp.bfloat16)
        for copy in copies:
            copy.wait()


def attention_backward(q, k, v, g, live_cols, x, nseq):
    length = q.shape[0]
    row_spec = pl.BlockSpec((ROWS, HD), lambda i: (i, 0))
    full_spec = pl.BlockSpec((length, HD), lambda i: (0, 0))
    mask_spec = pl.BlockSpec((ROWS // BLOCK, 1, length), lambda i: (i, 0, 0))
    out = jax.ShapeDtypeStruct((length, HD), jnp.bfloat16)
    flops = 12 * length * length * HD
    any_spec = pl.BlockSpec(memory_space=pl.ANY)
    return pl.pallas_call(
        functools.partial(attention_kernel, nseq),
        grid=(length // ROWS,),
        in_specs=[row_spec, full_spec, full_spec, row_spec, mask_spec, any_spec],
        out_specs=[row_spec, row_spec, full_spec, full_spec, any_spec],
        out_shape=[out, out, out, out, jax.ShapeDtypeStruct((nseq,) + x.shape, x.dtype)],
        scratch_shapes=[
            pltpu.VMEM((length, HD), jnp.float32),
            pltpu.VMEM((length, HD), jnp.float32),
            pltpu.SemaphoreType.DMA((nseq - 1,)),
            pltpu.SemaphoreType.DMA((nseq - 1,)),
            pltpu.SemaphoreType.DMA(()),
        ],
        compiler_params=pltpu.CompilerParams(
            vmem_limit_bytes=48 * 1024 * 1024, collective_id=1, has_side_effects=True
        ),
        cost_estimate=pl.CostEstimate(
            flops=flops, transcendentals=length * length, bytes_accessed=8 * length * HD * 2
        ),
    )(q, k, v, g, live_cols, x)


def start_gather(nseq, src, dst, send_sem, recv_sem, copy_sem):
    me = lax.axis_index("sqx")
    copies = [pltpu.make_async_copy(src, dst.at[me], copy_sem)]
    for off in range(1, nseq):
        peer = (me + off) % nseq
        copies.append(
            pltpu.make_async_remote_copy(
                src_ref=src,
                dst_ref=dst.at[me],
                send_sem=send_sem.at[off - 1],
                recv_sem=recv_sem.at[off - 1],
                device_id={"sqx": peer},
                device_id_type=pl.DeviceIdType.MESH,
            )
        )
    return copies


def enter_barrier(nseq):
    me = lax.axis_index("sqx")
    barrier = pltpu.get_barrier_semaphore()
    for off in range(1, nseq):
        peer = (me + off) % nseq
        pl.semaphore_signal(barrier, 1, device_id={"sqx": peer}, device_id_type=pl.DeviceIdType.MESH)
    pl.semaphore_wait(barrier, nseq - 1)


def gather_kernel(nseq, a_ref, a_out, send_sem, recv_sem, copy_sem):
    enter_barrier(nseq)
    copies = start_gather(nseq, a_ref, a_out, send_sem, recv_sem, copy_sem)
    for copy in copies:
        copy.start()
    for copy in copies:
        copy.wait()


def seq_gather(a, nseq):
    any_spec = pl.BlockSpec(memory_space=pl.ANY)
    return pl.pallas_call(
        functools.partial(gather_kernel, nseq),
        in_specs=[any_spec],
        out_specs=any_spec,
        out_shape=jax.ShapeDtypeStruct((nseq,) + a.shape, a.dtype),
        scratch_shapes=[
            pltpu.SemaphoreType.DMA((nseq - 1,)),
            pltpu.SemaphoreType.DMA((nseq - 1,)),
            pltpu.SemaphoreType.DMA(()),
        ],
        compiler_params=pltpu.CompilerParams(collective_id=0, has_side_effects=True),
    )(a)


DP = ("dpy", "dpz", "dpc")
SQ = ("sqy", "sqx")


def local(inputs, d_output, loss_mask, queries, keys, values, out_weight, block_mask):
    sizes = {name: lax.axis_size(name) for name in DP + SQ}
    half = lax.axis_index("sqy")
    other = 1 - half
    col = lax.axis_index("sqx")
    head = half * sizes["sqx"] + col
    partner_head = other * sizes["sqx"] + col
    swap = [(0, 1), (1, 0)]
    masked = d_output[0] * loss_mask[0][:, None].astype(jnp.bfloat16)
    own_rows, width = out_weight.shape
    gathered = lax.all_gather(out_weight, "dpc", axis=0)
    gathered = lax.all_gather(gathered, "dpy", axis=0)
    gathered = lax.all_gather(gathered, "dpz", axis=0)
    gathered = jnp.transpose(gathered, (1, 0, 2, 3, 4)).reshape(-1, width)
    head_weight = lax.dynamic_slice_in_dim(gathered, head * HD, HD, 0)
    partner_weight = lax.dynamic_slice_in_dim(gathered, partner_head * HD, HD, 0)
    masked_half = seq_gather(masked, sizes["sqx"]).reshape(-1, width)
    half_len = masked_half.shape[0]
    nt = (((1,), (1,)), ((), ()))
    d_own = lax.dot_general(masked_half, head_weight, nt, preferred_element_type=jnp.float32).astype(jnp.bfloat16)
    d_give = lax.dot_general(masked_half, partner_weight, nt, preferred_element_type=jnp.float32).astype(jnp.bfloat16)
    d_got = lax.ppermute(d_give, "sqy", swap)
    d_attn = jnp.zeros((2 * half_len, HD), jnp.bfloat16)
    d_attn = lax.dynamic_update_slice_in_dim(d_attn, d_own, half * half_len, 0)
    d_attn = lax.dynamic_update_slice_in_dim(d_attn, d_got, other * half_len, 0)
    blocks = block_mask[0, 0]
    live_cols = jnp.repeat(blocks, BLOCK, axis=1)[:, None, :]
    d_query, attended, d_key, d_value, inputs_half = attention_backward(
        queries[0, :, 0], keys[0, :, 0], values[0, :, 0], d_attn, live_cols, inputs[0], sizes["sqx"]
    )
    inputs_half = inputs_half.reshape(-1, width)
    grads = jnp.stack([d_query, d_key, d_value, attended])
    grads_own = lax.dynamic_slice_in_dim(grads, half * half_len, half_len, 1)
    grads_give = lax.dynamic_slice_in_dim(grads, other * half_len, half_len, 1)
    grads_got = lax.ppermute(grads_give, "sqy", swap)
    tn = (((0,), (0,)), ((), ()))

    def terms_of(parts):
        return jnp.stack(
            [
                lax.dot_general(parts[0], inputs_half, tn, preferred_element_type=jnp.float32),
                lax.dot_general(parts[1], inputs_half, tn, preferred_element_type=jnp.float32),
                lax.dot_general(parts[2], inputs_half, tn, preferred_element_type=jnp.float32),
                lax.dot_general(parts[3], masked_half, tn, preferred_element_type=jnp.float32),
            ],
            axis=0,
        )

    terms = jnp.stack([terms_of(grads_own), terms_of(grads_got)])
    ny, nz, nc = sizes["dpy"], sizes["dpz"], sizes["dpc"]
    chunk = terms.shape[2] // (ny * nz * nc)
    terms = terms.reshape(2, 4, ny, nz, nc, chunk, width)
    core = lax.axis_index("dpc")
    kept = lax.dynamic_index_in_dim(terms, core, 4, keepdims=False)
    sent = lax.dynamic_index_in_dim(terms, 1 - core, 4, keepdims=False)
    terms = kept + lax.ppermute(sent, "dpc", swap)
    row = lax.axis_index("dpy")
    kept = lax.dynamic_index_in_dim(terms, row, 2, keepdims=False)
    sent = lax.dynamic_index_in_dim(terms, 1 - row, 2, keepdims=False)
    terms = kept + lax.ppermute(sent, "dpy", swap)
    terms = jnp.transpose(terms.reshape(2, 4, nz, chunk * width), (2, 0, 1, 3))
    terms = lax.psum_scatter(terms.reshape(nz, -1, 128), "dpz", scatter_dimension=0, tiled=True)
    terms = terms.reshape(2, 4, chunk, width)
    owned = terms[0] + lax.ppermute(terms[1], "sqy", swap)
    owned = jnp.transpose(owned, (1, 0, 2))
    return tuple(owned[:, part][:, None, :] for part in range(4))


def solution(mesh):
    dp, seq = mesh.devices.shape
    devices = mesh.devices.reshape(2, dp // 4, 2, 2, seq // 2)
    fine = jax.sharding.Mesh(devices, DP + SQ)
    in_specs = (
        P(DP, SQ, None),
        P(DP, SQ, None),
        P(DP, SQ),
        P(DP, None, SQ, None),
        P(DP, None, SQ, None),
        P(DP, None, SQ, None),
        P(DP, None),
        P(DP, SQ, None, None),
    )
    out_specs = (
        P(DP, SQ, None),
        P(DP, SQ, None),
        P(DP, SQ, None),
        P(DP, SQ, None),
    )
    return jax.shard_map(local, mesh=fine, in_specs=in_specs, out_specs=out_specs, check_vma=False)
```

```python
import functools

import jax
import jax.numpy as jnp
from jax import lax
from jax.experimental import pallas as pl
from jax.experimental.pallas import tpu as pltpu
from jax.sharding import PartitionSpec as P

HD = 128
BLOCK = 128
ROWS = 256

masked_score = -1e30


def attention_kernel(
    nseq, q_ref, k_ref, v_ref, g_ref, m_ref, x_ref, dq_ref, att_ref, dk_ref, dv_ref, x_out,
    dk_acc, dv_acc, send_sem, recv_sem, copy_sem,
):
    step = pl.program_id(0)
    steps = pl.num_programs(0)
    scale = HD ** (-0.5)
    groups = ROWS // BLOCK
    copies = start_gather(nseq, x_ref, x_out, send_sem, recv_sem, copy_sem)

    @pl.when(step == 0)
    def _():
        enter_barrier(nseq)
        for copy in copies:
            copy.start()
        dk_acc[...] = jnp.zeros_like(dk_acc)
        dv_acc[...] = jnp.zeros_like(dv_acc)

    q = q_ref[...]
    k = k_ref[...]
    v = v_ref[...]
    g = g_ref[...]
    length = k.shape[0]
    nt = (((1,), (1,)), ((), ()))
    tn = (((0,), (0,)), ((), ()))
    scores = lax.dot_general(q, k, nt, preferred_element_type=jnp.float32) * scale
    live = m_ref[...]
    scores = scores.reshape(groups, BLOCK, length)
    scores = jnp.where(live > 0, scores, masked_score).reshape(ROWS, length)
    row_max = jnp.max(scores, axis=1, keepdims=True)
    weights = jnp.exp(scores - row_max)
    row_total = jnp.sum(weights, axis=1, keepdims=True)
    prob = weights / row_total
    prob_low = prob.astype(jnp.bfloat16)
    attended = jnp.dot(prob_low, v, preferred_element_type=jnp.float32).astype(jnp.bfloat16)
    row_delta = jnp.sum(g.astype(jnp.float32) * attended.astype(jnp.float32), axis=1, keepdims=True)
    d_prob = lax.dot_general(g, v, nt, preferred_element_type=jnp.float32)
    d_score = (prob * (d_prob - row_delta)).astype(jnp.bfloat16)
    dq_ref[...] = (jnp.dot(d_score, k, preferred_element_type=jnp.float32) * scale).astype(jnp.bfloat16)
    att_ref[...] = attended
    dk_acc[...] += lax.dot_general(d_score, q, tn, preferred_element_type=jnp.float32)
    dv_acc[...] += lax.dot_general(prob_low, g, tn, preferred_element_type=jnp.float32)

    @pl.when(step == steps - 1)
    def _():
        dk_ref[...] = (dk_acc[...] * scale).astype(jnp.bfloat16)
        dv_ref[...] = dv_acc[...].astype(jnp.bfloat16)
        for copy in copies:
            copy.wait()


def attention_backward(q, k, v, g, live_cols, x, nseq):
    length = q.shape[0]
    row_spec = pl.BlockSpec((ROWS, HD), lambda i: (i, 0))
    full_spec = pl.BlockSpec((length, HD), lambda i: (0, 0))
    mask_spec = pl.BlockSpec((ROWS // BLOCK, 1, length), lambda i: (i, 0, 0))
    out = jax.ShapeDtypeStruct((length, HD), jnp.bfloat16)
    flops = 12 * length * length * HD
    any_spec = pl.BlockSpec(memory_space=pl.ANY)
    return pl.pallas_call(
        functools.partial(attention_kernel, nseq),
        grid=(length // ROWS,),
        in_specs=[row_spec, full_spec, full_spec, row_spec, mask_spec, any_spec],
        out_specs=[row_spec, row_spec, full_spec, full_spec, any_spec],
        out_shape=[out, out, out, out, jax.ShapeDtypeStruct((nseq,) + x.shape, x.dtype)],
        scratch_shapes=[
            pltpu.VMEM((length, HD), jnp.float32),
            pltpu.VMEM((length, HD), jnp.float32),
            pltpu.SemaphoreType.DMA((nseq - 1,)),
            pltpu.SemaphoreType.DMA((nseq - 1,)),
            pltpu.SemaphoreType.DMA(()),
        ],
        compiler_params=pltpu.CompilerParams(
            vmem_limit_bytes=48 * 1024 * 1024, collective_id=1, has_side_effects=True
        ),
        cost_estimate=pl.CostEstimate(
            flops=flops, transcendentals=length * length, bytes_accessed=8 * length * HD * 2
        ),
    )(q, k, v, g, live_cols, x)


def start_gather(nseq, src, dst, send_sem, recv_sem, copy_sem):
    me = lax.axis_index("sqx")
    copies = [pltpu.make_async_copy(src, dst.at[me], copy_sem)]
    for off in range(1, nseq):
        peer = (me + off) % nseq
        copies.append(
            pltpu.make_async_remote_copy(
                src_ref=src,
                dst_ref=dst.at[me],
                send_sem=send_sem.at[off - 1],
                recv_sem=recv_sem.at[off - 1],
                device_id={"sqx": peer},
                device_id_type=pl.DeviceIdType.MESH,
            )
        )
    return copies


def enter_barrier(nseq, nz=1):
    me = lax.axis_index("sqx")
    zme = lax.axis_index("dpz")
    barrier = pltpu.get_barrier_semaphore()
    for off in range(1, nseq):
        peer = (me + off) % nseq
        pl.semaphore_signal(barrier, 1, device_id={"sqx": peer}, device_id_type=pl.DeviceIdType.MESH)
    for off in range(1, nz):
        peer = (zme + off) % nz
        pl.semaphore_signal(barrier, 1, device_id={"dpz": peer}, device_id_type=pl.DeviceIdType.MESH)
    pl.semaphore_wait(barrier, nseq - 1 + nz - 1)


def gather_kernel(nseq, nz, a_ref, w_ref, a_out, w_out, send_sem, recv_sem, copy_sem, w_send, w_recv, w_copy):
    enter_barrier(nseq, nz)
    copies = start_gather(nseq, a_ref, a_out, send_sem, recv_sem, copy_sem)
    for copy in copies:
        copy.start()
    zme = lax.axis_index("dpz")
    col = lax.axis_index("sqx")
    slot = zme % 2
    w_local = pltpu.make_async_copy(w_ref, w_out.at[slot], w_copy)
    w_sends = [
        pltpu.make_async_remote_copy(
            src_ref=w_ref,
            dst_ref=w_out.at[slot],
            send_sem=w_send.at[off - 1],
            recv_sem=w_recv.at[slot],
            device_id={"dpz": (zme + off) % nz},
            device_id_type=pl.DeviceIdType.MESH,
        )
        for off in range(1, nz)
    ]

    @pl.when(zme // 2 == col)
    def _():
        w_local.start()
        for copy in w_sends:
            copy.start()

    for copy in copies:
        copy.wait()

    @pl.when(zme // 2 == col)
    def _():
        w_local.wait()
        for copy in w_sends:
            copy.wait_send()

    for part in range(2):
        incoming = pltpu.make_async_remote_copy(
            src_ref=w_ref,
            dst_ref=w_out.at[part],
            send_sem=w_send.at[0],
            recv_sem=w_recv.at[part],
            device_id={"dpz": 2 * col + part},
            device_id_type=pl.DeviceIdType.MESH,
        )

        @pl.when(2 * col + part != zme)
        def _():
            incoming.wait_recv()


def seq_gather(a, w, nseq, nz):
    any_spec = pl.BlockSpec(memory_space=pl.ANY)
    return pl.pallas_call(
        functools.partial(gather_kernel, nseq, nz),
        in_specs=[any_spec, any_spec],
        out_specs=[any_spec, any_spec],
        out_shape=[
            jax.ShapeDtypeStruct((nseq,) + a.shape, a.dtype),
            jax.ShapeDtypeStruct((2,) + w.shape, w.dtype),
        ],
        scratch_shapes=[
            pltpu.SemaphoreType.DMA((nseq - 1,)),
            pltpu.SemaphoreType.DMA((nseq - 1,)),
            pltpu.SemaphoreType.DMA(()),
            pltpu.SemaphoreType.DMA((nz - 1,)),
            pltpu.SemaphoreType.DMA((2,)),
            pltpu.SemaphoreType.DMA(()),
        ],
        compiler_params=pltpu.CompilerParams(collective_id=0, has_side_effects=True),
    )(a, w)


DP = ("dpy", "dpz", "dpc")
SQ = ("sqy", "sqx")


def local(inputs, d_output, loss_mask, queries, keys, values, out_weight, block_mask):
    sizes = {name: lax.axis_size(name) for name in DP + SQ}
    half = lax.axis_index("sqy")
    other = 1 - half
    col = lax.axis_index("sqx")
    head = half * sizes["sqx"] + col
    partner_head = other * sizes["sqx"] + col
    swap = [(0, 1), (1, 0)]
    masked = d_output[0] * loss_mask[0][:, None].astype(jnp.bfloat16)
    own_rows, width = out_weight.shape
    gathered = lax.all_gather(out_weight, "dpc", axis=0)
    gathered = lax.all_gather(gathered, "dpy", axis=0)
    masked_half, pair_weight = seq_gather(masked, gathered, sizes["sqx"], sizes["dpz"])
    masked_half = masked_half.reshape(-1, width)
    head_weight = lax.dynamic_index_in_dim(pair_weight, half, 1, keepdims=False).reshape(HD, width)
    partner_weight = lax.dynamic_index_in_dim(pair_weight, other, 1, keepdims=False).reshape(HD, width)
    half_len = masked_half.shape[0]
    nt = (((1,), (1,)), ((), ()))
    d_own = lax.dot_general(masked_half, head_weight, nt, preferred_element_type=jnp.float32).astype(jnp.bfloat16)
    d_give = lax.dot_general(masked_half, partner_weight, nt, preferred_element_type=jnp.float32).astype(jnp.bfloat16)
    d_got = lax.ppermute(d_give, "sqy", swap)
    d_attn = jnp.zeros((2 * half_len, HD), jnp.bfloat16)
    d_attn = lax.dynamic_update_slice_in_dim(d_attn, d_own, half * half_len, 0)
    d_attn = lax.dynamic_update_slice_in_dim(d_attn, d_got, other * half_len, 0)
    blocks = block_mask[0, 0]
    live_cols = jnp.repeat(blocks, BLOCK, axis=1)[:, None, :]
    d_query, attended, d_key, d_value, inputs_half = attention_backward(
        queries[0, :, 0], keys[0, :, 0], values[0, :, 0], d_attn, live_cols, inputs[0], sizes["sqx"]
    )
    inputs_half = inputs_half.reshape(-1, width)
    grads = jnp.stack([d_query, d_key, d_value, attended])
    grads_own = lax.dynamic_slice_in_dim(grads, half * half_len, half_len, 1)
    grads_give = lax.dynamic_slice_in_dim(grads, other * half_len, half_len, 1)
    grads_got = lax.ppermute(grads_give, "sqy", swap)
    tn = (((0,), (0,)), ((), ()))

    def terms_of(parts):
        return jnp.stack(
            [
                lax.dot_general(parts[0], inputs_half, tn, preferred_element_type=jnp.float32),
                lax.dot_general(parts[1], inputs_half, tn, preferred_element_type=jnp.float32),
                lax.dot_general(parts[2], inputs_half, tn, preferred_element_type=jnp.float32),
                lax.dot_general(parts[3], masked_half, tn, preferred_element_type=jnp.float32),
            ],
            axis=0,
        )

    terms = jnp.stack([terms_of(grads_own), terms_of(grads_got)])
    ny, nz, nc = sizes["dpy"], sizes["dpz"], sizes["dpc"]
    chunk = terms.shape[2] // (ny * nz * nc)
    terms = terms.reshape(2, 4, ny, nz, nc, chunk, width)
    core = lax.axis_index("dpc")
    kept = lax.dynamic_index_in_dim(terms, core, 4, keepdims=False)
    sent = lax.dynamic_index_in_dim(terms, 1 - core, 4, keepdims=False)
    terms = kept + lax.ppermute(sent, "dpc", swap)
    row = lax.axis_index("dpy")
    kept = lax.dynamic_index_in_dim(terms, row, 2, keepdims=False)
    sent = lax.dynamic_index_in_dim(terms, 1 - row, 2, keepdims=False)
    terms = kept + lax.ppermute(sent, "dpy", swap)
    terms = jnp.transpose(terms.reshape(2, 4, nz, chunk * width), (2, 0, 1, 3))
    terms = lax.psum_scatter(terms.reshape(nz, -1, 128), "dpz", scatter_dimension=0, tiled=True)
    terms = terms.reshape(2, 4, chunk, width)
    owned = terms[0] + lax.ppermute(terms[1], "sqy", swap)
    owned = jnp.transpose(owned, (1, 0, 2))
    return tuple(owned[:, part][:, None, :] for part in range(4))


def solution(mesh):
    dp, seq = mesh.devices.shape
    devices = mesh.devices.reshape(2, dp // 4, 2, 2, seq // 2)
    fine = jax.sharding.Mesh(devices, DP + SQ)
    in_specs = (
        P(DP, SQ, None),
        P(DP, SQ, None),
        P(DP, SQ),
        P(DP, None, SQ, None),
        P(DP, None, SQ, None),
        P(DP, None, SQ, None),
        P(DP, None),
        P(DP, SQ, None, None),
    )
    out_specs = (
        P(DP, SQ, None),
        P(DP, SQ, None),
        P(DP, SQ, None),
        P(DP, SQ, None),
    )
    return jax.shard_map(local, mesh=fine, in_specs=in_specs, out_specs=out_specs, check_vma=False)
```

```python
import functools

import jax
import jax.numpy as jnp
from jax import lax
from jax.experimental import pallas as pl
from jax.experimental.pallas import tpu as pltpu
from jax.sharding import PartitionSpec as P

HD = 128
BLOCK = 128
ROWS = 256

masked_score = -1e30


def attention_kernel(
    nseq, q_ref, k_ref, v_ref, g_ref, m_ref, x_ref, dq_ref, att_ref, dk_ref, dv_ref, x_out,
    dk_acc, dv_acc, send_sem, recv_sem, copy_sem,
):
    step = pl.program_id(0)
    steps = pl.num_programs(0)
    scale = HD ** (-0.5)
    groups = ROWS // BLOCK
    copies = start_gather(nseq, x_ref, x_out, send_sem, recv_sem, copy_sem)

    @pl.when(step == 0)
    def _():
        enter_barrier(nseq)
        for copy in copies:
            copy.start()
        dk_acc[...] = jnp.zeros_like(dk_acc)
        dv_acc[...] = jnp.zeros_like(dv_acc)

    q = q_ref[...]
    k = k_ref[...]
    v = v_ref[...]
    g = g_ref[...]
    length = k.shape[0]
    nt = (((1,), (1,)), ((), ()))
    tn = (((0,), (0,)), ((), ()))
    scores = lax.dot_general(q, k, nt, preferred_element_type=jnp.float32) * scale
    live = m_ref[...]
    scores = scores.reshape(groups, BLOCK, length)
    scores = jnp.where(live > 0, scores, masked_score).reshape(ROWS, length)
    row_max = jnp.max(scores, axis=1, keepdims=True)
    weights = jnp.exp(scores - row_max)
    row_total = jnp.sum(weights, axis=1, keepdims=True)
    prob = weights / row_total
    prob_low = prob.astype(jnp.bfloat16)
    attended = jnp.dot(prob_low, v, preferred_element_type=jnp.float32).astype(jnp.bfloat16)
    row_delta = jnp.sum(g.astype(jnp.float32) * attended.astype(jnp.float32), axis=1, keepdims=True)
    d_prob = lax.dot_general(g, v, nt, preferred_element_type=jnp.float32)
    d_score = (prob * (d_prob - row_delta)).astype(jnp.bfloat16)
    dq_ref[...] = (jnp.dot(d_score, k, preferred_element_type=jnp.float32) * scale).astype(jnp.bfloat16)
    att_ref[...] = attended
    dk_acc[...] += lax.dot_general(d_score, q, tn, preferred_element_type=jnp.float32)
    dv_acc[...] += lax.dot_general(prob_low, g, tn, preferred_element_type=jnp.float32)

    @pl.when(step == steps - 1)
    def _():
        dk_ref[...] = (dk_acc[...] * scale).astype(jnp.bfloat16)
        dv_ref[...] = dv_acc[...].astype(jnp.bfloat16)
        for copy in copies:
            copy.wait()


def attention_backward(q, k, v, g, live_cols, x, nseq):
    length = q.shape[0]
    row_spec = pl.BlockSpec((ROWS, HD), lambda i: (i, 0))
    full_spec = pl.BlockSpec((length, HD), lambda i: (0, 0))
    mask_spec = pl.BlockSpec((ROWS // BLOCK, 1, length), lambda i: (i, 0, 0))
    out = jax.ShapeDtypeStruct((length, HD), jnp.bfloat16)
    flops = 12 * length * length * HD
    any_spec = pl.BlockSpec(memory_space=pl.ANY)
    return pl.pallas_call(
        functools.partial(attention_kernel, nseq),
        grid=(length // ROWS,),
        in_specs=[row_spec, full_spec, full_spec, row_spec, mask_spec, any_spec],
        out_specs=[row_spec, row_spec, full_spec, full_spec, any_spec],
        out_shape=[out, out, out, out, jax.ShapeDtypeStruct((nseq,) + x.shape, x.dtype)],
        scratch_shapes=[
            pltpu.VMEM((length, HD), jnp.float32),
            pltpu.VMEM((length, HD), jnp.float32),
            pltpu.SemaphoreType.DMA((nseq - 1,)),
            pltpu.SemaphoreType.DMA((nseq - 1,)),
            pltpu.SemaphoreType.DMA(()),
        ],
        compiler_params=pltpu.CompilerParams(
            vmem_limit_bytes=48 * 1024 * 1024, collective_id=1, has_side_effects=True
        ),
        cost_estimate=pl.CostEstimate(
            flops=flops, transcendentals=length * length, bytes_accessed=8 * length * HD * 2
        ),
    )(q, k, v, g, live_cols, x)


def start_gather(nseq, src, dst, send_sem, recv_sem, copy_sem):
    me = lax.axis_index("sqx")
    copies = [pltpu.make_async_copy(src, dst.at[me], copy_sem)]
    for off in range(1, nseq):
        peer = (me + off) % nseq
        copies.append(
            pltpu.make_async_remote_copy(
                src_ref=src,
                dst_ref=dst.at[me],
                send_sem=send_sem.at[off - 1],
                recv_sem=recv_sem.at[off - 1],
                device_id={"sqx": peer},
                device_id_type=pl.DeviceIdType.MESH,
            )
        )
    return copies


def enter_barrier(nseq):
    me = lax.axis_index("sqx")
    barrier = pltpu.get_barrier_semaphore()
    for off in range(1, nseq):
        peer = (me + off) % nseq
        pl.semaphore_signal(barrier, 1, device_id={"sqx": peer}, device_id_type=pl.DeviceIdType.MESH)
    pl.semaphore_wait(barrier, nseq - 1)


def gather_kernel(nseq, a_ref, a_out, send_sem, recv_sem, copy_sem):
    enter_barrier(nseq)
    copies = start_gather(nseq, a_ref, a_out, send_sem, recv_sem, copy_sem)
    for copy in copies:
        copy.start()
    for copy in copies:
        copy.wait()


def seq_gather(a, nseq):
    any_spec = pl.BlockSpec(memory_space=pl.ANY)
    return pl.pallas_call(
        functools.partial(gather_kernel, nseq),
        in_specs=[any_spec],
        out_specs=any_spec,
        out_shape=jax.ShapeDtypeStruct((nseq,) + a.shape, a.dtype),
        scratch_shapes=[
            pltpu.SemaphoreType.DMA((nseq - 1,)),
            pltpu.SemaphoreType.DMA((nseq - 1,)),
            pltpu.SemaphoreType.DMA(()),
        ],
        compiler_params=pltpu.CompilerParams(collective_id=0, has_side_effects=True),
    )(a)


DP = ("dpy", "dpz", "dpc")
SQ = ("sqy", "sqx")


def local(inputs, d_output, loss_mask, queries, keys, values, out_weight, block_mask):
    sizes = {name: lax.axis_size(name) for name in DP + SQ}
    half = lax.axis_index("sqy")
    other = 1 - half
    col = lax.axis_index("sqx")
    head = half * sizes["sqx"] + col
    partner_head = other * sizes["sqx"] + col
    swap = [(0, 1), (1, 0)]
    masked = d_output[0] * loss_mask[0][:, None].astype(jnp.bfloat16)
    own_rows, width = out_weight.shape
    gathered = lax.all_gather(out_weight, "dpz", axis=0)
    gathered = lax.all_gather(gathered, "dpc", axis=0)
    gathered = lax.all_gather(gathered, "dpy", axis=0)
    gathered = jnp.transpose(gathered, (0, 2, 1, 3, 4)).reshape(-1, width)
    head_weight = lax.dynamic_slice_in_dim(gathered, head * HD, HD, 0)
    partner_weight = lax.dynamic_slice_in_dim(gathered, partner_head * HD, HD, 0)
    masked_half = seq_gather(masked, sizes["sqx"]).reshape(-1, width)
    half_len = masked_half.shape[0]
    nt = (((1,), (1,)), ((), ()))
    d_own = lax.dot_general(masked_half, head_weight, nt, preferred_element_type=jnp.float32).astype(jnp.bfloat16)
    d_give = lax.dot_general(masked_half, partner_weight, nt, preferred_element_type=jnp.float32).astype(jnp.bfloat16)
    d_got = lax.ppermute(d_give, "sqy", swap)
    d_attn = jnp.zeros((2 * half_len, HD), jnp.bfloat16)
    d_attn = lax.dynamic_update_slice_in_dim(d_attn, d_own, half * half_len, 0)
    d_attn = lax.dynamic_update_slice_in_dim(d_attn, d_got, other * half_len, 0)
    blocks = block_mask[0, 0]
    live_cols = jnp.repeat(blocks, BLOCK, axis=1)[:, None, :]
    d_query, attended, d_key, d_value, inputs_half = attention_backward(
        queries[0, :, 0], keys[0, :, 0], values[0, :, 0], d_attn, live_cols, inputs[0], sizes["sqx"]
    )
    inputs_half = inputs_half.reshape(-1, width)
    grads = jnp.stack([d_query, d_key, d_value, attended])
    grads_own = lax.dynamic_slice_in_dim(grads, half * half_len, half_len, 1)
    grads_give = lax.dynamic_slice_in_dim(grads, other * half_len, half_len, 1)
    grads_got = lax.ppermute(grads_give, "sqy", swap)
    tn = (((0,), (0,)), ((), ()))

    def terms_of(parts):
        return jnp.stack(
            [
                lax.dot_general(parts[0], inputs_half, tn, preferred_element_type=jnp.float32),
                lax.dot_general(parts[1], inputs_half, tn, preferred_element_type=jnp.float32),
                lax.dot_general(parts[2], inputs_half, tn, preferred_element_type=jnp.float32),
                lax.dot_general(parts[3], masked_half, tn, preferred_element_type=jnp.float32),
            ],
            axis=0,
        )

    terms = jnp.stack([terms_of(grads_own), terms_of(grads_got)])
    ny, nz, nc = sizes["dpy"], sizes["dpz"], sizes["dpc"]
    chunk = terms.shape[2] // (ny * nz * nc)
    terms = terms.reshape(2, 4, ny, nz, nc, chunk, width)
    core = lax.axis_index("dpc")
    kept = lax.dynamic_index_in_dim(terms, core, 4, keepdims=False)
    sent = lax.dynamic_index_in_dim(terms, 1 - core, 4, keepdims=False)
    terms = kept + lax.ppermute(sent, "dpc", swap)
    row = lax.axis_index("dpy")
    kept = lax.dynamic_index_in_dim(terms, row, 2, keepdims=False)
    sent = lax.dynamic_index_in_dim(terms, 1 - row, 2, keepdims=False)
    terms = kept + lax.ppermute(sent, "dpy", swap)
    terms = jnp.transpose(terms.reshape(2, 4, nz, chunk * width), (2, 0, 1, 3))
    terms = lax.psum_scatter(terms.reshape(nz, -1, 128), "dpz", scatter_dimension=0, tiled=True)
    terms = terms.reshape(2, 4, chunk, width)
    owned = terms[0] + lax.ppermute(terms[1], "sqy", swap)
    owned = jnp.transpose(owned, (1, 0, 2))
    return tuple(owned[:, part][:, None, :] for part in range(4))


def solution(mesh):
    dp, seq = mesh.devices.shape
    devices = mesh.devices.reshape(2, dp // 4, 2, 2, seq // 2)
    fine = jax.sharding.Mesh(devices, DP + SQ)
    in_specs = (
        P(DP, SQ, None),
        P(DP, SQ, None),
        P(DP, SQ),
        P(DP, None, SQ, None),
        P(DP, None, SQ, None),
        P(DP, None, SQ, None),
        P(DP, None),
        P(DP, SQ, None, None),
    )
    out_specs = (
        P(DP, SQ, None),
        P(DP, SQ, None),
        P(DP, SQ, None),
        P(DP, SQ, None),
    )
    return jax.shard_map(local, mesh=fine, in_specs=in_specs, out_specs=out_specs, check_vma=False)
```

```python
import functools

import jax
import jax.numpy as jnp
from jax import lax
from jax.experimental import pallas as pl
from jax.experimental.pallas import tpu as pltpu
from jax.sharding import PartitionSpec as P

HD = 128
BLOCK = 128
ROWS = 256

masked_score = -1e30


def attention_kernel(
    nseq, q_ref, k_ref, v_ref, g_ref, m_ref, x_ref, dq_ref, att_ref, dk_ref, dv_ref, x_out,
    dk_acc, dv_acc, send_sem, recv_sem, copy_sem,
):
    step = pl.program_id(0)
    steps = pl.num_programs(0)
    scale = HD ** (-0.5)
    groups = ROWS // BLOCK
    copies = start_gather(nseq, x_ref, x_out, send_sem, recv_sem, copy_sem)

    @pl.when(step == 0)
    def _():
        enter_barrier(nseq)
        for copy in copies:
            copy.start()
        dk_acc[...] = jnp.zeros_like(dk_acc)
        dv_acc[...] = jnp.zeros_like(dv_acc)

    q = q_ref[...]
    k = k_ref[...]
    v = v_ref[...]
    g = g_ref[...]
    length = k.shape[0]
    nt = (((1,), (1,)), ((), ()))
    tn = (((0,), (0,)), ((), ()))
    scores = lax.dot_general(q, k, nt, preferred_element_type=jnp.float32) * scale
    live = m_ref[...]
    scores = scores.reshape(groups, BLOCK, length)
    scores = jnp.where(live > 0, scores, masked_score).reshape(ROWS, length)
    row_max = jnp.max(scores, axis=1, keepdims=True)
    weights = jnp.exp(scores - row_max)
    row_total = jnp.sum(weights, axis=1, keepdims=True)
    prob = weights / row_total
    prob_low = prob.astype(jnp.bfloat16)
    attended = jnp.dot(prob_low, v, preferred_element_type=jnp.float32).astype(jnp.bfloat16)
    row_delta = jnp.sum(g.astype(jnp.float32) * attended.astype(jnp.float32), axis=1, keepdims=True)
    d_prob = lax.dot_general(g, v, nt, preferred_element_type=jnp.float32)
    d_score = (prob * (d_prob - row_delta)).astype(jnp.bfloat16)
    dq_ref[...] = (jnp.dot(d_score, k, preferred_element_type=jnp.float32) * scale).astype(jnp.bfloat16)
    att_ref[...] = attended
    dk_acc[...] += lax.dot_general(d_score, q, tn, preferred_element_type=jnp.float32)
    dv_acc[...] += lax.dot_general(prob_low, g, tn, preferred_element_type=jnp.float32)

    @pl.when(step == steps - 1)
    def _():
        dk_ref[...] = (dk_acc[...] * scale).astype(jnp.bfloat16)
        dv_ref[...] = dv_acc[...].astype(jnp.bfloat16)
        for copy in copies:
            copy.wait()


def attention_backward(q, k, v, g, live_cols, x, nseq):
    length = q.shape[0]
    row_spec = pl.BlockSpec((ROWS, HD), lambda i: (i, 0))
    full_spec = pl.BlockSpec((length, HD), lambda i: (0, 0))
    mask_spec = pl.BlockSpec((ROWS // BLOCK, 1, length), lambda i: (i, 0, 0))
    out = jax.ShapeDtypeStruct((length, HD), jnp.bfloat16)
    flops = 12 * length * length * HD
    any_spec = pl.BlockSpec(memory_space=pl.ANY)
    return pl.pallas_call(
        functools.partial(attention_kernel, nseq),
        grid=(length // ROWS,),
        in_specs=[row_spec, full_spec, full_spec, row_spec, mask_spec, any_spec],
        out_specs=[row_spec, row_spec, full_spec, full_spec, any_spec],
        out_shape=[out, out, out, out, jax.ShapeDtypeStruct((nseq,) + x.shape, x.dtype)],
        scratch_shapes=[
            pltpu.VMEM((length, HD), jnp.float32),
            pltpu.VMEM((length, HD), jnp.float32),
            pltpu.SemaphoreType.DMA((nseq - 1,)),
            pltpu.SemaphoreType.DMA((nseq - 1,)),
            pltpu.SemaphoreType.DMA(()),
        ],
        compiler_params=pltpu.CompilerParams(
            vmem_limit_bytes=48 * 1024 * 1024, collective_id=1, has_side_effects=True
        ),
        cost_estimate=pl.CostEstimate(
            flops=flops, transcendentals=length * length, bytes_accessed=8 * length * HD * 2
        ),
    )(q, k, v, g, live_cols, x)


def start_gather(nseq, src, dst, send_sem, recv_sem, copy_sem):
    me = lax.axis_index("sqx")
    copies = [pltpu.make_async_copy(src, dst.at[me], copy_sem)]
    for off in range(1, nseq):
        peer = (me + off) % nseq
        copies.append(
            pltpu.make_async_remote_copy(
                src_ref=src,
                dst_ref=dst.at[me],
                send_sem=send_sem.at[off - 1],
                recv_sem=recv_sem.at[off - 1],
                device_id={"sqx": peer},
                device_id_type=pl.DeviceIdType.MESH,
            )
        )
    return copies


def enter_barrier(nseq):
    me = lax.axis_index("sqx")
    barrier = pltpu.get_barrier_semaphore()
    for off in range(1, nseq):
        peer = (me + off) % nseq
        pl.semaphore_signal(barrier, 1, device_id={"sqx": peer}, device_id_type=pl.DeviceIdType.MESH)
    pl.semaphore_wait(barrier, nseq - 1)


def gather_kernel(nseq, a_ref, a_out, send_sem, recv_sem, copy_sem):
    enter_barrier(nseq)
    copies = start_gather(nseq, a_ref, a_out, send_sem, recv_sem, copy_sem)
    for copy in copies:
        copy.start()
    for copy in copies:
        copy.wait()


def seq_gather(a, nseq):
    any_spec = pl.BlockSpec(memory_space=pl.ANY)
    return pl.pallas_call(
        functools.partial(gather_kernel, nseq),
        in_specs=[any_spec],
        out_specs=any_spec,
        out_shape=jax.ShapeDtypeStruct((nseq,) + a.shape, a.dtype),
        scratch_shapes=[
            pltpu.SemaphoreType.DMA((nseq - 1,)),
            pltpu.SemaphoreType.DMA((nseq - 1,)),
            pltpu.SemaphoreType.DMA(()),
        ],
        compiler_params=pltpu.CompilerParams(collective_id=0, has_side_effects=True),
    )(a)


DP = ("dpy", "dpz", "dpc")
SQ = ("sqy", "sqx")


def local(inputs, d_output, loss_mask, queries, keys, values, out_weight, block_mask):
    sizes = {name: lax.axis_size(name) for name in DP + SQ}
    half = lax.axis_index("sqy")
    other = 1 - half
    col = lax.axis_index("sqx")
    head = half * sizes["sqx"] + col
    partner_head = other * sizes["sqx"] + col
    swap = [(0, 1), (1, 0)]
    masked = d_output[0] * loss_mask[0][:, None].astype(jnp.bfloat16)
    own_rows, width = out_weight.shape
    gathered = lax.all_gather(out_weight, "dpc", axis=0)
    gathered = lax.all_gather(gathered, "dpy", axis=0)
    gathered = lax.all_gather(gathered, "dpz", axis=0)
    gathered = jnp.transpose(gathered, (1, 0, 2, 3, 4)).reshape(-1, width)
    head_weight = lax.dynamic_slice_in_dim(gathered, head * HD, HD, 0)
    partner_weight = lax.dynamic_slice_in_dim(gathered, partner_head * HD, HD, 0)
    masked_half = seq_gather(masked, sizes["sqx"]).reshape(-1, width)
    half_len = masked_half.shape[0]
    nt = (((1,), (1,)), ((), ()))
    d_own = lax.dot_general(masked_half, head_weight, nt, preferred_element_type=jnp.float32).astype(jnp.bfloat16)
    d_give = lax.dot_general(masked_half, partner_weight, nt, preferred_element_type=jnp.float32).astype(jnp.bfloat16)
    d_got = lax.ppermute(d_give, "sqy", swap)
    d_attn = jnp.zeros((2 * half_len, HD), jnp.bfloat16)
    d_attn = lax.dynamic_update_slice_in_dim(d_attn, d_own, half * half_len, 0)
    d_attn = lax.dynamic_update_slice_in_dim(d_attn, d_got, other * half_len, 0)
    blocks = block_mask[0, 0]
    live_cols = jnp.repeat(blocks, BLOCK, axis=1)[:, None, :]
    d_query, attended, d_key, d_value, inputs_half = attention_backward(
        queries[0, :, 0], keys[0, :, 0], values[0, :, 0], d_attn, live_cols, inputs[0], sizes["sqx"]
    )
    inputs_half = inputs_half.reshape(-1, width)
    grads = jnp.stack([d_query, d_key, d_value, attended])
    grads_own = lax.dynamic_slice_in_dim(grads, half * half_len, half_len, 1)
    grads_give = lax.dynamic_slice_in_dim(grads, other * half_len, half_len, 1)
    grads_got = lax.ppermute(grads_give, "sqy", swap)
    tn = (((0,), (0,)), ((), ()))

    def terms_of(parts):
        return jnp.stack(
            [
                lax.dot_general(parts[0], inputs_half, tn, preferred_element_type=jnp.float32),
                lax.dot_general(parts[1], inputs_half, tn, preferred_element_type=jnp.float32),
                lax.dot_general(parts[2], inputs_half, tn, preferred_element_type=jnp.float32),
                lax.dot_general(parts[3], masked_half, tn, preferred_element_type=jnp.float32),
            ],
            axis=0,
        )

    terms = jnp.stack([terms_of(grads_own), terms_of(grads_got)])
    ny, nz, nc = sizes["dpy"], sizes["dpz"], sizes["dpc"]
    chunk = terms.shape[2] // (ny * nz * nc)
    terms = terms.reshape(2, 4, ny, nz, nc, chunk, width)
    core = lax.axis_index("dpc")
    kept = lax.dynamic_index_in_dim(terms, core, 4, keepdims=False)
    sent = lax.dynamic_index_in_dim(terms, 1 - core, 4, keepdims=False)
    terms = kept + lax.ppermute(sent, "dpc", swap)
    terms = jnp.transpose(terms, (3, 0, 1, 2, 4, 5))
    terms = lax.psum_scatter(terms.reshape(nz, -1, 128), "dpz", scatter_dimension=0, tiled=True)
    terms = terms.reshape(2, 4, ny, chunk, width)
    row = lax.axis_index("dpy")
    kept = lax.dynamic_index_in_dim(terms, row, 2, keepdims=False)
    sent = lax.dynamic_index_in_dim(terms, 1 - row, 2, keepdims=False)
    terms = kept + lax.ppermute(sent, "dpy", swap)
    owned = terms[0] + lax.ppermute(terms[1], "sqy", swap)
    owned = jnp.transpose(owned, (1, 0, 2))
    return tuple(owned[:, part][:, None, :] for part in range(4))


def solution(mesh):
    dp, seq = mesh.devices.shape
    devices = mesh.devices.reshape(2, dp // 4, 2, 2, seq // 2)
    fine = jax.sharding.Mesh(devices, DP + SQ)
    in_specs = (
        P(DP, SQ, None),
        P(DP, SQ, None),
        P(DP, SQ),
        P(DP, None, SQ, None),
        P(DP, None, SQ, None),
        P(DP, None, SQ, None),
        P(DP, None),
        P(DP, SQ, None, None),
    )
    out_specs = (
        P(DP, SQ, None),
        P(DP, SQ, None),
        P(DP, SQ, None),
        P(DP, SQ, None),
    )
    return jax.shard_map(local, mesh=fine, in_specs=in_specs, out_specs=out_specs, check_vma=False)
```

```python
import functools

import jax
import jax.numpy as jnp
from jax import lax
from jax.experimental import pallas as pl
from jax.experimental.pallas import tpu as pltpu
from jax.sharding import PartitionSpec as P

HD = 128
BLOCK = 128
ROWS = 256

masked_score = -1e30


def attention_kernel(
    nseq, q_ref, k_ref, v_ref, g_ref, m_ref, x_ref, dq_ref, att_ref, dk_ref, dv_ref, x_out,
    dk_acc, dv_acc, send_sem, recv_sem, copy_sem,
):
    step = pl.program_id(0)
    steps = pl.num_programs(0)
    scale = HD ** (-0.5)
    groups = ROWS // BLOCK
    copies = start_gather(nseq, x_ref, x_out, send_sem, recv_sem, copy_sem)

    @pl.when(step == 0)
    def _():
        enter_barrier(nseq)
        for copy in copies:
            copy.start()
        dk_acc[...] = jnp.zeros_like(dk_acc)
        dv_acc[...] = jnp.zeros_like(dv_acc)

    q = q_ref[...]
    k = k_ref[...]
    v = v_ref[...]
    g = g_ref[...]
    length = k.shape[0]
    nt = (((1,), (1,)), ((), ()))
    tn = (((0,), (0,)), ((), ()))
    scores = lax.dot_general(q, k, nt, preferred_element_type=jnp.float32) * scale
    live = m_ref[...]
    scores = scores.reshape(groups, BLOCK, length)
    scores = jnp.where(live > 0, scores, masked_score).reshape(ROWS, length)
    row_max = jnp.max(scores, axis=1, keepdims=True)
    weights = jnp.exp(scores - row_max)
    row_total = jnp.sum(weights, axis=1, keepdims=True)
    prob = weights / row_total
    prob_low = prob.astype(jnp.bfloat16)
    attended = jnp.dot(prob_low, v, preferred_element_type=jnp.float32).astype(jnp.bfloat16)
    row_delta = jnp.sum(g.astype(jnp.float32) * attended.astype(jnp.float32), axis=1, keepdims=True)
    d_prob = lax.dot_general(g, v, nt, preferred_element_type=jnp.float32)
    d_score = (prob * (d_prob - row_delta)).astype(jnp.bfloat16)
    dq_ref[...] = (jnp.dot(d_score, k, preferred_element_type=jnp.float32) * scale).astype(jnp.bfloat16)
    att_ref[...] = attended
    dk_acc[...] += lax.dot_general(d_score, q, tn, preferred_element_type=jnp.float32)
    dv_acc[...] += lax.dot_general(prob_low, g, tn, preferred_element_type=jnp.float32)

    @pl.when(step == steps - 1)
    def _():
        dk_ref[...] = (dk_acc[...] * scale).astype(jnp.bfloat16)
        dv_ref[...] = dv_acc[...].astype(jnp.bfloat16)
        for copy in copies:
            copy.wait()


def attention_backward(q, k, v, g, live_cols, x, nseq):
    length = q.shape[0]
    row_spec = pl.BlockSpec((ROWS, HD), lambda i: (i, 0))
    full_spec = pl.BlockSpec((length, HD), lambda i: (0, 0))
    mask_spec = pl.BlockSpec((ROWS // BLOCK, 1, length), lambda i: (i, 0, 0))
    out = jax.ShapeDtypeStruct((length, HD), jnp.bfloat16)
    flops = 12 * length * length * HD
    any_spec = pl.BlockSpec(memory_space=pl.ANY)
    return pl.pallas_call(
        functools.partial(attention_kernel, nseq),
        grid=(length // ROWS,),
        in_specs=[row_spec, full_spec, full_spec, row_spec, mask_spec, any_spec],
        out_specs=[row_spec, row_spec, full_spec, full_spec, any_spec],
        out_shape=[out, out, out, out, jax.ShapeDtypeStruct((nseq,) + x.shape, x.dtype)],
        scratch_shapes=[
            pltpu.VMEM((length, HD), jnp.float32),
            pltpu.VMEM((length, HD), jnp.float32),
            pltpu.SemaphoreType.DMA((nseq - 1,)),
            pltpu.SemaphoreType.DMA((nseq - 1,)),
            pltpu.SemaphoreType.DMA(()),
        ],
        compiler_params=pltpu.CompilerParams(
            vmem_limit_bytes=48 * 1024 * 1024, collective_id=1, has_side_effects=True
        ),
        cost_estimate=pl.CostEstimate(
            flops=flops, transcendentals=length * length, bytes_accessed=8 * length * HD * 2
        ),
    )(q, k, v, g, live_cols, x)


def start_gather(nseq, src, dst, send_sem, recv_sem, copy_sem):
    me = lax.axis_index("sqx")
    copies = [pltpu.make_async_copy(src, dst.at[me], copy_sem)]
    for off in range(1, nseq):
        peer = (me + off) % nseq
        copies.append(
            pltpu.make_async_remote_copy(
                src_ref=src,
                dst_ref=dst.at[me],
                send_sem=send_sem.at[off - 1],
                recv_sem=recv_sem.at[off - 1],
                device_id={"sqx": peer},
                device_id_type=pl.DeviceIdType.MESH,
            )
        )
    return copies


def enter_barrier(nseq):
    me = lax.axis_index("sqx")
    barrier = pltpu.get_barrier_semaphore()
    for off in range(1, nseq):
        peer = (me + off) % nseq
        pl.semaphore_signal(barrier, 1, device_id={"sqx": peer}, device_id_type=pl.DeviceIdType.MESH)
    pl.semaphore_wait(barrier, nseq - 1)


def gather_kernel(nseq, a_ref, a_out, send_sem, recv_sem, copy_sem):
    enter_barrier(nseq)
    copies = start_gather(nseq, a_ref, a_out, send_sem, recv_sem, copy_sem)
    for copy in copies:
        copy.start()
    for copy in copies:
        copy.wait()


def seq_gather(a, nseq):
    any_spec = pl.BlockSpec(memory_space=pl.ANY)
    return pl.pallas_call(
        functools.partial(gather_kernel, nseq),
        in_specs=[any_spec],
        out_specs=any_spec,
        out_shape=jax.ShapeDtypeStruct((nseq,) + a.shape, a.dtype),
        scratch_shapes=[
            pltpu.SemaphoreType.DMA((nseq - 1,)),
            pltpu.SemaphoreType.DMA((nseq - 1,)),
            pltpu.SemaphoreType.DMA(()),
        ],
        compiler_params=pltpu.CompilerParams(collective_id=0, has_side_effects=True),
    )(a)


DP = ("dpy", "dpz", "dpc")
SQ = ("sqy", "sqx")


def local(inputs, d_output, loss_mask, queries, keys, values, out_weight, block_mask):
    sizes = {name: lax.axis_size(name) for name in DP + SQ}
    half = lax.axis_index("sqy")
    other = 1 - half
    col = lax.axis_index("sqx")
    head = half * sizes["sqx"] + col
    partner_head = other * sizes["sqx"] + col
    swap = [(0, 1), (1, 0)]
    masked = d_output[0] * loss_mask[0][:, None].astype(jnp.bfloat16)
    own_rows, width = out_weight.shape
    gathered = lax.all_gather(out_weight, ("dpy", "dpc"), axis=0).reshape((2, 2) + out_weight.shape)
    gathered = lax.all_gather(gathered, "dpz", axis=0)
    gathered = jnp.transpose(gathered, (1, 0, 2, 3, 4)).reshape(-1, width)
    head_weight = lax.dynamic_slice_in_dim(gathered, head * HD, HD, 0)
    partner_weight = lax.dynamic_slice_in_dim(gathered, partner_head * HD, HD, 0)
    masked_half = seq_gather(masked, sizes["sqx"]).reshape(-1, width)
    half_len = masked_half.shape[0]
    nt = (((1,), (1,)), ((), ()))
    d_own = lax.dot_general(masked_half, head_weight, nt, preferred_element_type=jnp.float32).astype(jnp.bfloat16)
    d_give = lax.dot_general(masked_half, partner_weight, nt, preferred_element_type=jnp.float32).astype(jnp.bfloat16)
    d_got = lax.ppermute(d_give, "sqy", swap)
    d_attn = jnp.zeros((2 * half_len, HD), jnp.bfloat16)
    d_attn = lax.dynamic_update_slice_in_dim(d_attn, d_own, half * half_len, 0)
    d_attn = lax.dynamic_update_slice_in_dim(d_attn, d_got, other * half_len, 0)
    blocks = block_mask[0, 0]
    live_cols = jnp.repeat(blocks, BLOCK, axis=1)[:, None, :]
    d_query, attended, d_key, d_value, inputs_half = attention_backward(
        queries[0, :, 0], keys[0, :, 0], values[0, :, 0], d_attn, live_cols, inputs[0], sizes["sqx"]
    )
    inputs_half = inputs_half.reshape(-1, width)
    grads = jnp.stack([d_query, d_key, d_value, attended])
    grads_own = lax.dynamic_slice_in_dim(grads, half * half_len, half_len, 1)
    grads_give = lax.dynamic_slice_in_dim(grads, other * half_len, half_len, 1)
    grads_got = lax.ppermute(grads_give, "sqy", swap)
    tn = (((0,), (0,)), ((), ()))

    def terms_of(parts):
        return jnp.stack(
            [
                lax.dot_general(parts[0], inputs_half, tn, preferred_element_type=jnp.float32),
                lax.dot_general(parts[1], inputs_half, tn, preferred_element_type=jnp.float32),
                lax.dot_general(parts[2], inputs_half, tn, preferred_element_type=jnp.float32),
                lax.dot_general(parts[3], masked_half, tn, preferred_element_type=jnp.float32),
            ],
            axis=0,
        )

    terms = jnp.stack([terms_of(grads_own), terms_of(grads_got)])
    ny, nz, nc = sizes["dpy"], sizes["dpz"], sizes["dpc"]
    chunk = terms.shape[2] // (ny * nz * nc)
    terms = terms.reshape(2, 4, ny, nz, nc, chunk, width)
    core = lax.axis_index("dpc")
    kept = lax.dynamic_index_in_dim(terms, core, 4, keepdims=False)
    sent = lax.dynamic_index_in_dim(terms, 1 - core, 4, keepdims=False)
    terms = kept + lax.ppermute(sent, "dpc", swap)
    terms = jnp.transpose(terms, (3, 0, 1, 2, 4, 5))
    terms = lax.psum_scatter(terms.reshape(nz, -1, 128), "dpz", scatter_dimension=0, tiled=True)
    terms = terms.reshape(2, 4, ny, chunk, width)
    row = lax.axis_index("dpy")
    kept = lax.dynamic_index_in_dim(terms, row, 2, keepdims=False)
    sent = lax.dynamic_index_in_dim(terms, 1 - row, 2, keepdims=False)
    terms = kept + lax.ppermute(sent, "dpy", swap)
    owned = terms[0] + lax.ppermute(terms[1], "sqy", swap)
    owned = jnp.transpose(owned, (1, 0, 2))
    return tuple(owned[:, part][:, None, :] for part in range(4))


def solution(mesh):
    dp, seq = mesh.devices.shape
    devices = mesh.devices.reshape(2, dp // 4, 2, 2, seq // 2)
    fine = jax.sharding.Mesh(devices, DP + SQ)
    in_specs = (
        P(DP, SQ, None),
        P(DP, SQ, None),
        P(DP, SQ),
        P(DP, None, SQ, None),
        P(DP, None, SQ, None),
        P(DP, None, SQ, None),
        P(DP, None),
        P(DP, SQ, None, None),
    )
    out_specs = (
        P(DP, SQ, None),
        P(DP, SQ, None),
        P(DP, SQ, None),
        P(DP, SQ, None),
    )
    return jax.shard_map(local, mesh=fine, in_specs=in_specs, out_specs=out_specs, check_vma=False)
```

```python
import functools

import jax
import jax.numpy as jnp
from jax import lax
from jax.experimental import pallas as pl
from jax.experimental.pallas import tpu as pltpu
from jax.sharding import PartitionSpec as P

HD = 128
BLOCK = 128
ROWS = 256

masked_score = -1e30


def attention_kernel(
    nseq, q_ref, k_ref, v_ref, g_ref, m_ref, x_ref, dq_ref, att_ref, dk_ref, dv_ref, x_out,
    dk_acc, dv_acc, send_sem, recv_sem, copy_sem,
):
    step = pl.program_id(0)
    steps = pl.num_programs(0)
    scale = HD ** (-0.5)
    groups = ROWS // BLOCK
    copies = start_gather(nseq, x_ref, x_out, send_sem, recv_sem, copy_sem)

    @pl.when(step == 0)
    def _():
        enter_barrier(nseq)
        for copy in copies:
            copy.start()
        dk_acc[...] = jnp.zeros_like(dk_acc)
        dv_acc[...] = jnp.zeros_like(dv_acc)

    q = q_ref[...]
    k = k_ref[...]
    v = v_ref[...]
    g = g_ref[...]
    length = k.shape[0]
    nt = (((1,), (1,)), ((), ()))
    tn = (((0,), (0,)), ((), ()))
    scores = lax.dot_general(q, k, nt, preferred_element_type=jnp.float32) * scale
    live = m_ref[...]
    scores = scores.reshape(groups, BLOCK, length)
    scores = jnp.where(live > 0, scores, masked_score).reshape(ROWS, length)
    row_max = jnp.max(scores, axis=1, keepdims=True)
    weights = jnp.exp(scores - row_max)
    row_total = jnp.sum(weights, axis=1, keepdims=True)
    prob = weights / row_total
    prob_low = prob.astype(jnp.bfloat16)
    attended = jnp.dot(prob_low, v, preferred_element_type=jnp.float32).astype(jnp.bfloat16)
    row_delta = jnp.sum(g.astype(jnp.float32) * attended.astype(jnp.float32), axis=1, keepdims=True)
    d_prob = lax.dot_general(g, v, nt, preferred_element_type=jnp.float32)
    d_score = (prob * (d_prob - row_delta)).astype(jnp.bfloat16)
    dq_ref[...] = (jnp.dot(d_score, k, preferred_element_type=jnp.float32) * scale).astype(jnp.bfloat16)
    att_ref[...] = attended
    dk_acc[...] += lax.dot_general(d_score, q, tn, preferred_element_type=jnp.float32)
    dv_acc[...] += lax.dot_general(prob_low, g, tn, preferred_element_type=jnp.float32)

    @pl.when(step == steps - 1)
    def _():
        dk_ref[...] = (dk_acc[...] * scale).astype(jnp.bfloat16)
        dv_ref[...] = dv_acc[...].astype(jnp.bfloat16)
        for copy in copies:
            copy.wait()


def attention_backward(q, k, v, g, live_cols, x, nseq):
    length = q.shape[0]
    row_spec = pl.BlockSpec((ROWS, HD), lambda i: (i, 0))
    full_spec = pl.BlockSpec((length, HD), lambda i: (0, 0))
    mask_spec = pl.BlockSpec((ROWS // BLOCK, 1, length), lambda i: (i, 0, 0))
    out = jax.ShapeDtypeStruct((length, HD), jnp.bfloat16)
    flops = 12 * length * length * HD
    any_spec = pl.BlockSpec(memory_space=pl.ANY)
    return pl.pallas_call(
        functools.partial(attention_kernel, nseq),
        grid=(length // ROWS,),
        in_specs=[row_spec, full_spec, full_spec, row_spec, mask_spec, any_spec],
        out_specs=[row_spec, row_spec, full_spec, full_spec, any_spec],
        out_shape=[out, out, out, out, jax.ShapeDtypeStruct((nseq,) + x.shape, x.dtype)],
        scratch_shapes=[
            pltpu.VMEM((length, HD), jnp.float32),
            pltpu.VMEM((length, HD), jnp.float32),
            pltpu.SemaphoreType.DMA((nseq - 1,)),
            pltpu.SemaphoreType.DMA((nseq - 1,)),
            pltpu.SemaphoreType.DMA(()),
        ],
        compiler_params=pltpu.CompilerParams(
            vmem_limit_bytes=48 * 1024 * 1024, collective_id=1, has_side_effects=True
        ),
        cost_estimate=pl.CostEstimate(
            flops=flops, transcendentals=length * length, bytes_accessed=8 * length * HD * 2
        ),
    )(q, k, v, g, live_cols, x)


def start_gather(nseq, src, dst, send_sem, recv_sem, copy_sem):
    me = lax.axis_index("sqx")
    copies = [pltpu.make_async_copy(src, dst.at[me], copy_sem)]
    for off in range(1, nseq):
        peer = (me + off) % nseq
        copies.append(
            pltpu.make_async_remote_copy(
                src_ref=src,
                dst_ref=dst.at[me],
                send_sem=send_sem.at[off - 1],
                recv_sem=recv_sem.at[off - 1],
                device_id={"sqx": peer},
                device_id_type=pl.DeviceIdType.MESH,
            )
        )
    return copies


def enter_barrier(nseq):
    me = lax.axis_index("sqx")
    barrier = pltpu.get_barrier_semaphore()
    for off in range(1, nseq):
        peer = (me + off) % nseq
        pl.semaphore_signal(barrier, 1, device_id={"sqx": peer}, device_id_type=pl.DeviceIdType.MESH)
    pl.semaphore_wait(barrier, nseq - 1)


def gather_kernel(nseq, a_ref, b_ref, a_out, b_out, send_sem, recv_sem, copy_sem):
    enter_barrier(nseq)
    copies = start_gather(nseq, a_ref, a_out, send_sem.at[0], recv_sem.at[0], copy_sem.at[0])
    copies += start_gather(nseq, b_ref, b_out, send_sem.at[1], recv_sem.at[1], copy_sem.at[1])
    for copy in copies:
        copy.start()
    for copy in copies:
        copy.wait()


def seq_gather(a, b, nseq):
    any_spec = pl.BlockSpec(memory_space=pl.ANY)
    return pl.pallas_call(
        functools.partial(gather_kernel, nseq),
        in_specs=[any_spec, any_spec],
        out_specs=[any_spec, any_spec],
        out_shape=[
            jax.ShapeDtypeStruct((nseq,) + a.shape, a.dtype),
            jax.ShapeDtypeStruct((nseq,) + b.shape, b.dtype),
        ],
        scratch_shapes=[
            pltpu.SemaphoreType.DMA((2, nseq - 1)),
            pltpu.SemaphoreType.DMA((2, nseq - 1)),
            pltpu.SemaphoreType.DMA((2,)),
        ],
        compiler_params=pltpu.CompilerParams(collective_id=0, has_side_effects=True),
    )(a, b)


DP = ("dpy", "dpz", "dpc")
SQ = ("sqy", "sqx")


def local(inputs, d_output, loss_mask, queries, keys, values, out_weight, block_mask):
    sizes = {name: lax.axis_size(name) for name in DP + SQ}
    half = lax.axis_index("sqy")
    other = 1 - half
    col = lax.axis_index("sqx")
    head = half * sizes["sqx"] + col
    partner_head = other * sizes["sqx"] + col
    swap = [(0, 1), (1, 0)]
    masked = d_output[0] * loss_mask[0][:, None].astype(jnp.bfloat16)
    own_rows, width = out_weight.shape
    gathered = lax.all_gather(out_weight, ("dpy", "dpc"), axis=0).reshape((2, 2) + out_weight.shape)
    gathered = lax.all_gather(gathered, "dpz", axis=0)
    gathered = jnp.transpose(gathered, (1, 0, 2, 3, 4)).reshape(-1, width)
    head_weight = lax.dynamic_slice_in_dim(gathered, head * HD, HD, 0)
    partner_weight = lax.dynamic_slice_in_dim(gathered, partner_head * HD, HD, 0)
    slab = inputs.shape[1]
    lead = slab // 2
    masked_half, inputs_lead = seq_gather(masked, inputs[0, :lead], sizes["sqx"])
    masked_half = masked_half.reshape(-1, width)
    inputs_lead = inputs_lead.reshape(-1, width)
    half_len = masked_half.shape[0]
    nt = (((1,), (1,)), ((), ()))
    d_own = lax.dot_general(masked_half, head_weight, nt, preferred_element_type=jnp.float32).astype(jnp.bfloat16)
    d_give = lax.dot_general(masked_half, partner_weight, nt, preferred_element_type=jnp.float32).astype(jnp.bfloat16)
    d_got = lax.ppermute(d_give, "sqy", swap)
    d_attn = jnp.zeros((2 * half_len, HD), jnp.bfloat16)
    d_attn = lax.dynamic_update_slice_in_dim(d_attn, d_own, half * half_len, 0)
    d_attn = lax.dynamic_update_slice_in_dim(d_attn, d_got, other * half_len, 0)
    blocks = block_mask[0, 0]
    live_cols = jnp.repeat(blocks, BLOCK, axis=1)[:, None, :]
    d_query, attended, d_key, d_value, inputs_half = attention_backward(
        queries[0, :, 0], keys[0, :, 0], values[0, :, 0], d_attn, live_cols, inputs[0, lead:], sizes["sqx"]
    )
    inputs_tail = inputs_half.reshape(-1, width)
    grads = jnp.stack([d_query, d_key, d_value, attended])
    grads_own = lax.dynamic_slice_in_dim(grads, half * half_len, half_len, 1)
    grads_give = lax.dynamic_slice_in_dim(grads, other * half_len, half_len, 1)
    grads_got = lax.ppermute(grads_give, "sqy", swap)
    tn = (((0,), (0,)), ((), ()))

    def by_inputs(part):
        rows = part.reshape(sizes["sqx"], slab, HD)
        lead_rows = rows[:, :lead].reshape(-1, HD)
        tail_rows = rows[:, lead:].reshape(-1, HD)
        return lax.dot_general(lead_rows, inputs_lead, tn, preferred_element_type=jnp.float32) + lax.dot_general(
            tail_rows, inputs_tail, tn, preferred_element_type=jnp.float32
        )

    def terms_of(parts):
        return jnp.stack(
            [
                by_inputs(parts[0]),
                by_inputs(parts[1]),
                by_inputs(parts[2]),
                lax.dot_general(parts[3], masked_half, tn, preferred_element_type=jnp.float32),
            ],
            axis=0,
        )

    terms = jnp.stack([terms_of(grads_own), terms_of(grads_got)])
    ny, nz, nc = sizes["dpy"], sizes["dpz"], sizes["dpc"]
    chunk = terms.shape[2] // (ny * nz * nc)
    terms = terms.reshape(2, 4, ny, nz, nc, chunk, width)
    core = lax.axis_index("dpc")
    kept = lax.dynamic_index_in_dim(terms, core, 4, keepdims=False)
    sent = lax.dynamic_index_in_dim(terms, 1 - core, 4, keepdims=False)
    terms = kept + lax.ppermute(sent, "dpc", swap)
    terms = jnp.transpose(terms, (3, 0, 1, 2, 4, 5))
    terms = lax.psum_scatter(terms.reshape(nz, -1, 128), "dpz", scatter_dimension=0, tiled=True)
    terms = terms.reshape(2, 4, ny, chunk, width)
    row = lax.axis_index("dpy")
    kept = lax.dynamic_index_in_dim(terms, row, 2, keepdims=False)
    sent = lax.dynamic_index_in_dim(terms, 1 - row, 2, keepdims=False)
    terms = kept + lax.ppermute(sent, "dpy", swap)
    owned = terms[0] + lax.ppermute(terms[1], "sqy", swap)
    owned = jnp.transpose(owned, (1, 0, 2))
    return tuple(owned[:, part][:, None, :] for part in range(4))


def solution(mesh):
    dp, seq = mesh.devices.shape
    devices = mesh.devices.reshape(2, dp // 4, 2, 2, seq // 2)
    fine = jax.sharding.Mesh(devices, DP + SQ)
    in_specs = (
        P(DP, SQ, None),
        P(DP, SQ, None),
        P(DP, SQ),
        P(DP, None, SQ, None),
        P(DP, None, SQ, None),
        P(DP, None, SQ, None),
        P(DP, None),
        P(DP, SQ, None, None),
    )
    out_specs = (
        P(DP, SQ, None),
        P(DP, SQ, None),
        P(DP, SQ, None),
        P(DP, SQ, None),
    )
    return jax.shard_map(local, mesh=fine, in_specs=in_specs, out_specs=out_specs, check_vma=False)
```

```python
import functools

import jax
import jax.numpy as jnp
from jax import lax
from jax.experimental import pallas as pl
from jax.experimental.pallas import tpu as pltpu
from jax.sharding import PartitionSpec as P

HD = 128
BLOCK = 128
ROWS = 256

masked_score = -1e30


def attention_kernel(
    nseq, q_ref, k_ref, v_ref, g_ref, m_ref, x_ref, dq_ref, att_ref, dk_ref, dv_ref, x_out,
    dk_acc, dv_acc, send_sem, recv_sem, copy_sem,
):
    step = pl.program_id(0)
    steps = pl.num_programs(0)
    scale = HD ** (-0.5)
    groups = ROWS // BLOCK
    copies = start_gather(nseq, x_ref, x_out, send_sem, recv_sem, copy_sem)

    @pl.when(step == 0)
    def _():
        enter_barrier(nseq)
        for copy in copies:
            copy.start()
        dk_acc[...] = jnp.zeros_like(dk_acc)
        dv_acc[...] = jnp.zeros_like(dv_acc)

    q = q_ref[...]
    k = k_ref[...]
    v = v_ref[...]
    g = g_ref[...]
    length = k.shape[0]
    nt = (((1,), (1,)), ((), ()))
    tn = (((0,), (0,)), ((), ()))
    scores = lax.dot_general(q, k, nt, preferred_element_type=jnp.float32) * scale
    live = m_ref[...]
    scores = scores.reshape(groups, BLOCK, length)
    scores = jnp.where(live > 0, scores, masked_score).reshape(ROWS, length)
    row_max = jnp.max(scores, axis=1, keepdims=True)
    weights = jnp.exp(scores - row_max)
    row_total = jnp.sum(weights, axis=1, keepdims=True)
    prob = weights / row_total
    prob_low = prob.astype(jnp.bfloat16)
    attended = jnp.dot(prob_low, v, preferred_element_type=jnp.float32).astype(jnp.bfloat16)
    row_delta = jnp.sum(g.astype(jnp.float32) * attended.astype(jnp.float32), axis=1, keepdims=True)
    d_prob = lax.dot_general(g, v, nt, preferred_element_type=jnp.float32)
    d_score = (prob * (d_prob - row_delta)).astype(jnp.bfloat16)
    dq_ref[...] = (jnp.dot(d_score, k, preferred_element_type=jnp.float32) * scale).astype(jnp.bfloat16)
    att_ref[...] = attended
    dk_acc[...] += lax.dot_general(d_score, q, tn, preferred_element_type=jnp.float32)
    dv_acc[...] += lax.dot_general(prob_low, g, tn, preferred_element_type=jnp.float32)

    @pl.when(step == steps - 1)
    def _():
        dk_ref[...] = (dk_acc[...] * scale).astype(jnp.bfloat16)
        dv_ref[...] = dv_acc[...].astype(jnp.bfloat16)
        for copy in copies:
            copy.wait()


def attention_backward(q, k, v, g, live_cols, x, nseq):
    length = q.shape[0]
    row_spec = pl.BlockSpec((ROWS, HD), lambda i: (i, 0))
    full_spec = pl.BlockSpec((length, HD), lambda i: (0, 0))
    mask_spec = pl.BlockSpec((ROWS // BLOCK, 1, length), lambda i: (i, 0, 0))
    out = jax.ShapeDtypeStruct((length, HD), jnp.bfloat16)
    flops = 12 * length * length * HD
    any_spec = pl.BlockSpec(memory_space=pl.ANY)
    return pl.pallas_call(
        functools.partial(attention_kernel, nseq),
        grid=(length // ROWS,),
        in_specs=[row_spec, full_spec, full_spec, row_spec, mask_spec, any_spec],
        out_specs=[row_spec, row_spec, full_spec, full_spec, any_spec],
        out_shape=[out, out, out, out, jax.ShapeDtypeStruct((nseq,) + x.shape, x.dtype)],
        scratch_shapes=[
            pltpu.VMEM((length, HD), jnp.float32),
            pltpu.VMEM((length, HD), jnp.float32),
            pltpu.SemaphoreType.DMA((nseq - 1,)),
            pltpu.SemaphoreType.DMA((nseq - 1,)),
            pltpu.SemaphoreType.DMA(()),
        ],
        compiler_params=pltpu.CompilerParams(
            vmem_limit_bytes=48 * 1024 * 1024, collective_id=1, has_side_effects=True
        ),
        cost_estimate=pl.CostEstimate(
            flops=flops, transcendentals=length * length, bytes_accessed=8 * length * HD * 2
        ),
    )(q, k, v, g, live_cols, x)


def start_gather(nseq, src, dst, send_sem, recv_sem, copy_sem):
    me = lax.axis_index("sqx")
    copies = [pltpu.make_async_copy(src, dst.at[me], copy_sem)]
    for off in range(1, nseq):
        peer = (me + off) % nseq
        copies.append(
            pltpu.make_async_remote_copy(
                src_ref=src,
                dst_ref=dst.at[me],
                send_sem=send_sem.at[off - 1],
                recv_sem=recv_sem.at[off - 1],
                device_id={"sqx": peer},
                device_id_type=pl.DeviceIdType.MESH,
            )
        )
    return copies


def enter_barrier(nseq):
    me = lax.axis_index("sqx")
    barrier = pltpu.get_barrier_semaphore()
    for off in range(1, nseq):
        peer = (me + off) % nseq
        pl.semaphore_signal(barrier, 1, device_id={"sqx": peer}, device_id_type=pl.DeviceIdType.MESH)
    pl.semaphore_wait(barrier, nseq - 1)


def gather_kernel(nseq, a_ref, a_out, send_sem, recv_sem, copy_sem):
    enter_barrier(nseq)
    copies = start_gather(nseq, a_ref, a_out, send_sem, recv_sem, copy_sem)
    for copy in copies:
        copy.start()
    for copy in copies:
        copy.wait()


def seq_gather(a, nseq):
    any_spec = pl.BlockSpec(memory_space=pl.ANY)
    return pl.pallas_call(
        functools.partial(gather_kernel, nseq),
        in_specs=[any_spec],
        out_specs=any_spec,
        out_shape=jax.ShapeDtypeStruct((nseq,) + a.shape, a.dtype),
        scratch_shapes=[
            pltpu.SemaphoreType.DMA((nseq - 1,)),
            pltpu.SemaphoreType.DMA((nseq - 1,)),
            pltpu.SemaphoreType.DMA(()),
        ],
        compiler_params=pltpu.CompilerParams(collective_id=0, has_side_effects=True),
    )(a)


DP = ("dpy", "dpz", "dpc")
SQ = ("sqy", "sqx")


def local(inputs, d_output, loss_mask, queries, keys, values, out_weight, block_mask):
    sizes = {name: lax.axis_size(name) for name in DP + SQ}
    half = lax.axis_index("sqy")
    other = 1 - half
    col = lax.axis_index("sqx")
    head = half * sizes["sqx"] + col
    partner_head = other * sizes["sqx"] + col
    swap = [(0, 1), (1, 0)]
    masked = d_output[0] * loss_mask[0][:, None].astype(jnp.bfloat16)
    own_rows, width = out_weight.shape
    gathered = lax.all_gather(out_weight, ("dpy", "dpc"), axis=0).reshape((2, 2) + out_weight.shape)
    gathered = lax.all_gather(gathered, "dpz", axis=0)
    gathered = jnp.transpose(gathered, (1, 0, 2, 3, 4)).reshape(-1, width)
    head_weight = lax.dynamic_slice_in_dim(gathered, head * HD, HD, 0)
    partner_weight = lax.dynamic_slice_in_dim(gathered, partner_head * HD, HD, 0)
    masked_half = seq_gather(masked, sizes["sqx"]).reshape(-1, width)
    half_len = masked_half.shape[0]
    nt = (((1,), (1,)), ((), ()))
    d_own = lax.dot_general(masked_half, head_weight, nt, preferred_element_type=jnp.float32).astype(jnp.bfloat16)
    d_give = lax.dot_general(masked_half, partner_weight, nt, preferred_element_type=jnp.float32).astype(jnp.bfloat16)
    d_got = lax.ppermute(d_give, "sqy", swap)
    d_attn = jnp.zeros((2 * half_len, HD), jnp.bfloat16)
    d_attn = lax.dynamic_update_slice_in_dim(d_attn, d_own, half * half_len, 0)
    d_attn = lax.dynamic_update_slice_in_dim(d_attn, d_got, other * half_len, 0)
    blocks = block_mask[0, 0]
    live_cols = jnp.repeat(blocks, BLOCK, axis=1)[:, None, :]
    d_query, attended, d_key, d_value, inputs_half = attention_backward(
        queries[0, :, 0], keys[0, :, 0], values[0, :, 0], d_attn, live_cols, inputs[0], sizes["sqx"]
    )
    inputs_half = inputs_half.reshape(-1, width)
    grads = jnp.stack([d_query, d_key, d_value, attended])
    grads_own = lax.dynamic_slice_in_dim(grads, half * half_len, half_len, 1)
    grads_give = lax.dynamic_slice_in_dim(grads, other * half_len, half_len, 1)
    grads_got = lax.ppermute(grads_give, "sqy", swap)
    tn = (((0,), (0,)), ((), ()))

    def terms_of(parts):
        return jnp.stack(
            [
                lax.dot_general(parts[0], inputs_half, tn, preferred_element_type=jnp.float32),
                lax.dot_general(parts[1], inputs_half, tn, preferred_element_type=jnp.float32),
                lax.dot_general(parts[2], inputs_half, tn, preferred_element_type=jnp.float32),
                lax.dot_general(parts[3], masked_half, tn, preferred_element_type=jnp.float32),
            ],
            axis=0,
        )

    terms = jnp.stack([terms_of(grads_own), terms_of(grads_got)])
    ny, nz, nc = sizes["dpy"], sizes["dpz"], sizes["dpc"]
    chunk = terms.shape[2] // (ny * nz * nc)
    terms = terms.reshape(2, 4, ny, nz, nc, chunk, width)
    core = lax.axis_index("dpc")
    kept = lax.dynamic_index_in_dim(terms, core, 4, keepdims=False)
    sent = lax.dynamic_index_in_dim(terms, 1 - core, 4, keepdims=False)
    terms = kept + lax.ppermute(sent, "dpc", swap)
    terms = jnp.transpose(terms, (3, 0, 1, 2, 4, 5))
    terms = lax.psum_scatter(terms.reshape(nz, -1, 128), "dpz", scatter_dimension=0, tiled=True)
    terms = terms.reshape(2, 4, ny, chunk, width)
    row = lax.axis_index("dpy")
    mine = lax.dynamic_index_in_dim(terms, row, 2, keepdims=False)
    theirs = lax.dynamic_index_in_dim(terms, 1 - row, 2, keepdims=False)
    cross = [(0, 3), (3, 0), (1, 2), (2, 1)]
    owned = (
        mine[0]
        + lax.ppermute(theirs[0], "dpy", swap)
        + lax.ppermute(mine[1], "sqy", swap)
        + lax.ppermute(theirs[1], ("dpy", "sqy"), cross)
    )
    owned = jnp.transpose(owned, (1, 0, 2))
    return tuple(owned[:, part][:, None, :] for part in range(4))


def solution(mesh):
    dp, seq = mesh.devices.shape
    devices = mesh.devices.reshape(2, dp // 4, 2, 2, seq // 2)
    fine = jax.sharding.Mesh(devices, DP + SQ)
    in_specs = (
        P(DP, SQ, None),
        P(DP, SQ, None),
        P(DP, SQ),
        P(DP, None, SQ, None),
        P(DP, None, SQ, None),
        P(DP, None, SQ, None),
        P(DP, None),
        P(DP, SQ, None, None),
    )
    out_specs = (
        P(DP, SQ, None),
        P(DP, SQ, None),
        P(DP, SQ, None),
        P(DP, SQ, None),
    )
    return jax.shard_map(local, mesh=fine, in_specs=in_specs, out_specs=out_specs, check_vma=False)
```

```python
import functools

import jax
import jax.numpy as jnp
from jax import lax
from jax.experimental import pallas as pl
from jax.experimental.pallas import tpu as pltpu
from jax.sharding import PartitionSpec as P

HD = 128
BLOCK = 128
ROWS = 256

masked_score = -1e30


def attention_kernel(
    nseq, q_ref, k_ref, v_ref, g_ref, m_ref, x_ref, dq_ref, att_ref, dk_ref, dv_ref, x_out,
    dk_acc, dv_acc, send_sem, recv_sem, copy_sem,
):
    step = pl.program_id(0)
    steps = pl.num_programs(0)
    scale = HD ** (-0.5)
    groups = ROWS // BLOCK
    copies = start_gather(nseq, x_ref, x_out, send_sem, recv_sem, copy_sem)

    @pl.when(step == 0)
    def _():
        enter_barrier(nseq)
        for copy in copies:
            copy.start()
        dk_acc[...] = jnp.zeros_like(dk_acc)
        dv_acc[...] = jnp.zeros_like(dv_acc)

    q = q_ref[...]
    k = k_ref[...]
    v = v_ref[...]
    g = g_ref[...]
    length = k.shape[0]
    nt = (((1,), (1,)), ((), ()))
    tn = (((0,), (0,)), ((), ()))
    scores = lax.dot_general(q, k, nt, preferred_element_type=jnp.float32) * scale
    live = m_ref[...]
    scores = scores.reshape(groups, BLOCK, length)
    scores = jnp.where(live > 0, scores, masked_score).reshape(ROWS, length)
    row_max = jnp.max(scores, axis=1, keepdims=True)
    weights = jnp.exp(scores - row_max)
    row_total = jnp.sum(weights, axis=1, keepdims=True)
    prob = weights * (1.0 / row_total)
    prob_low = prob.astype(jnp.bfloat16)
    attended = jnp.dot(prob_low, v, preferred_element_type=jnp.float32).astype(jnp.bfloat16)
    row_delta = jnp.sum(g.astype(jnp.float32) * attended.astype(jnp.float32), axis=1, keepdims=True)
    d_prob = lax.dot_general(g, v, nt, preferred_element_type=jnp.float32)
    d_score = (prob * (d_prob - row_delta)).astype(jnp.bfloat16)
    dq_ref[...] = (jnp.dot(d_score, k, preferred_element_type=jnp.float32) * scale).astype(jnp.bfloat16)
    att_ref[...] = attended
    dk_acc[...] += lax.dot_general(d_score, q, tn, preferred_element_type=jnp.float32)
    dv_acc[...] += lax.dot_general(prob_low, g, tn, preferred_element_type=jnp.float32)

    @pl.when(step == steps - 1)
    def _():
        dk_ref[...] = (dk_acc[...] * scale).astype(jnp.bfloat16)
        dv_ref[...] = dv_acc[...].astype(jnp.bfloat16)
        for copy in copies:
            copy.wait()


def attention_backward(q, k, v, g, live_cols, x, nseq):
    length = q.shape[0]
    row_spec = pl.BlockSpec((ROWS, HD), lambda i: (i, 0))
    full_spec = pl.BlockSpec((length, HD), lambda i: (0, 0))
    mask_spec = pl.BlockSpec((ROWS // BLOCK, 1, length), lambda i: (i, 0, 0))
    out = jax.ShapeDtypeStruct((length, HD), jnp.bfloat16)
    flops = 12 * length * length * HD
    any_spec = pl.BlockSpec(memory_space=pl.ANY)
    return pl.pallas_call(
        functools.partial(attention_kernel, nseq),
        grid=(length // ROWS,),
        in_specs=[row_spec, full_spec, full_spec, row_spec, mask_spec, any_spec],
        out_specs=[row_spec, row_spec, full_spec, full_spec, any_spec],
        out_shape=[out, out, out, out, jax.ShapeDtypeStruct((nseq,) + x.shape, x.dtype)],
        scratch_shapes=[
            pltpu.VMEM((length, HD), jnp.float32),
            pltpu.VMEM((length, HD), jnp.float32),
            pltpu.SemaphoreType.DMA((nseq - 1,)),
            pltpu.SemaphoreType.DMA((nseq - 1,)),
            pltpu.SemaphoreType.DMA(()),
        ],
        compiler_params=pltpu.CompilerParams(
            vmem_limit_bytes=48 * 1024 * 1024, collective_id=1, has_side_effects=True
        ),
        cost_estimate=pl.CostEstimate(
            flops=flops, transcendentals=length * length, bytes_accessed=8 * length * HD * 2
        ),
    )(q, k, v, g, live_cols, x)


def start_gather(nseq, src, dst, send_sem, recv_sem, copy_sem):
    me = lax.axis_index("sqx")
    copies = [pltpu.make_async_copy(src, dst.at[me], copy_sem)]
    for off in range(1, nseq):
        peer = (me + off) % nseq
        copies.append(
            pltpu.make_async_remote_copy(
                src_ref=src,
                dst_ref=dst.at[me],
                send_sem=send_sem.at[off - 1],
                recv_sem=recv_sem.at[off - 1],
                device_id={"sqx": peer},
                device_id_type=pl.DeviceIdType.MESH,
            )
        )
    return copies


def enter_barrier(nseq):
    me = lax.axis_index("sqx")
    barrier = pltpu.get_barrier_semaphore()
    for off in range(1, nseq):
        peer = (me + off) % nseq
        pl.semaphore_signal(barrier, 1, device_id={"sqx": peer}, device_id_type=pl.DeviceIdType.MESH)
    pl.semaphore_wait(barrier, nseq - 1)


def gather_kernel(nseq, a_ref, b_ref, a_out, b_out, send_sem, recv_sem, copy_sem):
    enter_barrier(nseq)
    copies = start_gather(nseq, a_ref, a_out, send_sem.at[0], recv_sem.at[0], copy_sem.at[0])
    copies += start_gather(nseq, b_ref, b_out, send_sem.at[1], recv_sem.at[1], copy_sem.at[1])
    for copy in copies:
        copy.start()
    for copy in copies:
        copy.wait()


def seq_gather(a, b, nseq):
    any_spec = pl.BlockSpec(memory_space=pl.ANY)
    return pl.pallas_call(
        functools.partial(gather_kernel, nseq),
        in_specs=[any_spec, any_spec],
        out_specs=[any_spec, any_spec],
        out_shape=[
            jax.ShapeDtypeStruct((nseq,) + a.shape, a.dtype),
            jax.ShapeDtypeStruct((nseq,) + b.shape, b.dtype),
        ],
        scratch_shapes=[
            pltpu.SemaphoreType.DMA((2, nseq - 1)),
            pltpu.SemaphoreType.DMA((2, nseq - 1)),
            pltpu.SemaphoreType.DMA((2,)),
        ],
        compiler_params=pltpu.CompilerParams(collective_id=0, has_side_effects=True),
    )(a, b)


DP = ("dpy", "dpz", "dpc")
SQ = ("sqy", "sqx")


def local(inputs, d_output, loss_mask, queries, keys, values, out_weight, block_mask):
    sizes = {name: lax.axis_size(name) for name in DP + SQ}
    half = lax.axis_index("sqy")
    other = 1 - half
    col = lax.axis_index("sqx")
    head = half * sizes["sqx"] + col
    partner_head = other * sizes["sqx"] + col
    swap = [(0, 1), (1, 0)]
    masked = d_output[0] * loss_mask[0][:, None].astype(jnp.bfloat16)
    own_rows, width = out_weight.shape
    gathered = lax.all_gather(out_weight, ("dpy", "dpc"), axis=0).reshape((2, 2) + out_weight.shape)
    gathered = lax.all_gather(gathered, "dpz", axis=0)
    gathered = jnp.transpose(gathered, (1, 0, 2, 3, 4)).reshape(-1, width)
    head_weight = lax.dynamic_slice_in_dim(gathered, head * HD, HD, 0)
    partner_weight = lax.dynamic_slice_in_dim(gathered, partner_head * HD, HD, 0)
    split = width // 2
    masked_half, inputs_lead = seq_gather(masked, inputs[0, :, :split], sizes["sqx"])
    masked_half = masked_half.reshape(-1, width)
    inputs_lead = inputs_lead.reshape(-1, split)
    half_len = masked_half.shape[0]
    nt = (((1,), (1,)), ((), ()))
    d_own = lax.dot_general(masked_half, head_weight, nt, preferred_element_type=jnp.float32).astype(jnp.bfloat16)
    d_give = lax.dot_general(masked_half, partner_weight, nt, preferred_element_type=jnp.float32).astype(jnp.bfloat16)
    d_got = lax.ppermute(d_give, "sqy", swap)
    d_attn = jnp.zeros((2 * half_len, HD), jnp.bfloat16)
    d_attn = lax.dynamic_update_slice_in_dim(d_attn, d_own, half * half_len, 0)
    d_attn = lax.dynamic_update_slice_in_dim(d_attn, d_got, other * half_len, 0)
    blocks = block_mask[0, 0]
    live_cols = jnp.repeat(blocks, BLOCK, axis=1)[:, None, :]
    d_query, attended, d_key, d_value, inputs_half = attention_backward(
        queries[0, :, 0], keys[0, :, 0], values[0, :, 0], d_attn, live_cols, inputs[0, :, split:], sizes["sqx"]
    )
    inputs_tail = inputs_half.reshape(-1, split)
    masked_lead = masked_half[:, :split]
    masked_tail = masked_half[:, split:]
    grads = jnp.stack([d_query, d_key, d_value, attended])
    grads_own = lax.dynamic_slice_in_dim(grads, half * half_len, half_len, 1)
    grads_give = lax.dynamic_slice_in_dim(grads, other * half_len, half_len, 1)
    grads_got = lax.ppermute(grads_give, "sqy", swap)
    tn = (((0,), (0,)), ((), ()))

    def terms_of(parts):
        sources = ((inputs_lead, inputs_tail),) * 3 + ((masked_lead, masked_tail),)
        return jnp.stack(
            [
                jnp.stack([lax.dot_general(part, src, tn, preferred_element_type=jnp.float32) for src in pair])
                for part, pair in zip(parts, sources)
            ]
        )

    terms = jnp.stack([terms_of(grads_own), terms_of(grads_got)])
    ny, nz, nc = sizes["dpy"], sizes["dpz"], sizes["dpc"]
    chunk = terms.shape[3] // (ny * nz * nc)
    terms = terms.reshape(2, 4, 2, ny, nz, nc, chunk, split)
    core = lax.axis_index("dpc")
    kept = lax.dynamic_index_in_dim(terms, core, 5, keepdims=False)
    sent = lax.dynamic_index_in_dim(terms, 1 - core, 5, keepdims=False)
    terms = kept + lax.ppermute(sent, "dpc", swap)
    terms = jnp.transpose(terms, (4, 0, 1, 2, 3, 5, 6))
    terms = lax.psum_scatter(terms.reshape(nz, -1, 128), "dpz", scatter_dimension=0, tiled=True)
    terms = terms.reshape(2, 4, 2, ny, chunk, split)
    row = lax.axis_index("dpy")
    mine = lax.dynamic_index_in_dim(terms, row, 3, keepdims=False)
    theirs = lax.dynamic_index_in_dim(terms, 1 - row, 3, keepdims=False)
    cross = [(0, 3), (3, 0), (1, 2), (2, 1)]
    owned = (
        mine[0]
        + lax.ppermute(theirs[0], "dpy", swap)
        + lax.ppermute(mine[1], "sqy", swap)
        + lax.ppermute(theirs[1], ("dpy", "sqy"), cross)
    )
    owned = jnp.transpose(owned, (2, 0, 1, 3)).reshape(chunk, 4, width)
    return tuple(owned[:, part][:, None, :] for part in range(4))


def solution(mesh):
    dp, seq = mesh.devices.shape
    devices = mesh.devices.reshape(2, dp // 4, 2, 2, seq // 2)
    fine = jax.sharding.Mesh(devices, DP + SQ)
    in_specs = (
        P(DP, SQ, None),
        P(DP, SQ, None),
        P(DP, SQ),
        P(DP, None, SQ, None),
        P(DP, None, SQ, None),
        P(DP, None, SQ, None),
        P(DP, None),
        P(DP, SQ, None, None),
    )
    out_specs = (
        P(DP, SQ, None),
        P(DP, SQ, None),
        P(DP, SQ, None),
        P(DP, SQ, None),
    )
    return jax.shard_map(local, mesh=fine, in_specs=in_specs, out_specs=out_specs, check_vma=False)
```

```python
import functools

import jax
import jax.numpy as jnp
from jax import lax
from jax.experimental import pallas as pl
from jax.experimental.pallas import tpu as pltpu
from jax.sharding import PartitionSpec as P

HD = 128
BLOCK = 128
ROWS = 256

masked_score = -1e30


def attention_kernel(
    nseq, q_ref, k_ref, v_ref, g_ref, m_ref, x_ref, dq_ref, att_ref, dk_ref, dv_ref, x_out,
    dk_acc, dv_acc, send_sem, recv_sem, copy_sem,
):
    step = pl.program_id(0)
    steps = pl.num_programs(0)
    scale = HD ** (-0.5)
    groups = ROWS // BLOCK
    copies = start_gather(nseq, x_ref, x_out, send_sem, recv_sem, copy_sem)

    @pl.when(step == 0)
    def _():
        enter_barrier(nseq)
        for copy in copies:
            copy.start()
        dk_acc[...] = jnp.zeros_like(dk_acc)
        dv_acc[...] = jnp.zeros_like(dv_acc)

    q = q_ref[...]
    k = k_ref[...]
    v = v_ref[...]
    g = g_ref[...]
    length = k.shape[0]
    nt = (((1,), (1,)), ((), ()))
    tn = (((0,), (0,)), ((), ()))
    scores = lax.dot_general(q, k, nt, preferred_element_type=jnp.float32) * scale
    live = m_ref[...]
    scores = scores.reshape(groups, BLOCK, length)
    scores = jnp.where(live > 0, scores, masked_score).reshape(ROWS, length)
    row_max = jnp.max(scores, axis=1, keepdims=True)
    weights = jnp.exp(scores - row_max)
    row_total = jnp.sum(weights, axis=1, keepdims=True)
    prob = weights / row_total
    prob_low = prob.astype(jnp.bfloat16)
    attended = jnp.dot(prob_low, v, preferred_element_type=jnp.float32).astype(jnp.bfloat16)
    row_delta = jnp.sum(g.astype(jnp.float32) * attended.astype(jnp.float32), axis=1, keepdims=True)
    d_prob = lax.dot_general(g, v, nt, preferred_element_type=jnp.float32)
    d_score = (prob * (d_prob - row_delta)).astype(jnp.bfloat16)
    dq_ref[...] = (jnp.dot(d_score, k, preferred_element_type=jnp.float32) * scale).astype(jnp.bfloat16)
    att_ref[...] = attended
    dk_acc[...] += lax.dot_general(q, d_score, tn, preferred_element_type=jnp.float32)
    dv_acc[...] += lax.dot_general(g, prob_low, tn, preferred_element_type=jnp.float32)

    @pl.when(step == steps - 1)
    def _():
        dk_ref[...] = (dk_acc[...].T * scale).astype(jnp.bfloat16)
        dv_ref[...] = dv_acc[...].T.astype(jnp.bfloat16)
        for copy in copies:
            copy.wait()


def attention_backward(q, k, v, g, live_cols, x, nseq):
    length = q.shape[0]
    row_spec = pl.BlockSpec((ROWS, HD), lambda i: (i, 0))
    full_spec = pl.BlockSpec((length, HD), lambda i: (0, 0))
    mask_spec = pl.BlockSpec((ROWS // BLOCK, 1, length), lambda i: (i, 0, 0))
    out = jax.ShapeDtypeStruct((length, HD), jnp.bfloat16)
    flops = 12 * length * length * HD
    any_spec = pl.BlockSpec(memory_space=pl.ANY)
    return pl.pallas_call(
        functools.partial(attention_kernel, nseq),
        grid=(length // ROWS,),
        in_specs=[row_spec, full_spec, full_spec, row_spec, mask_spec, any_spec],
        out_specs=[row_spec, row_spec, full_spec, full_spec, any_spec],
        out_shape=[out, out, out, out, jax.ShapeDtypeStruct((nseq,) + x.shape, x.dtype)],
        scratch_shapes=[
            pltpu.VMEM((HD, length), jnp.float32),
            pltpu.VMEM((HD, length), jnp.float32),
            pltpu.SemaphoreType.DMA((nseq - 1,)),
            pltpu.SemaphoreType.DMA((nseq - 1,)),
            pltpu.SemaphoreType.DMA(()),
        ],
        compiler_params=pltpu.CompilerParams(
            vmem_limit_bytes=48 * 1024 * 1024, collective_id=1, has_side_effects=True
        ),
        cost_estimate=pl.CostEstimate(
            flops=flops, transcendentals=length * length, bytes_accessed=8 * length * HD * 2
        ),
    )(q, k, v, g, live_cols, x)


def start_gather(nseq, src, dst, send_sem, recv_sem, copy_sem):
    me = lax.axis_index("sqx")
    copies = [pltpu.make_async_copy(src, dst.at[me], copy_sem)]
    for off in range(1, nseq):
        peer = (me + off) % nseq
        copies.append(
            pltpu.make_async_remote_copy(
                src_ref=src,
                dst_ref=dst.at[me],
                send_sem=send_sem.at[off - 1],
                recv_sem=recv_sem.at[off - 1],
                device_id={"sqx": peer},
                device_id_type=pl.DeviceIdType.MESH,
            )
        )
    return copies


def enter_barrier(nseq):
    me = lax.axis_index("sqx")
    barrier = pltpu.get_barrier_semaphore()
    for off in range(1, nseq):
        peer = (me + off) % nseq
        pl.semaphore_signal(barrier, 1, device_id={"sqx": peer}, device_id_type=pl.DeviceIdType.MESH)
    pl.semaphore_wait(barrier, nseq - 1)


def gather_kernel(nseq, a_ref, a_out, send_sem, recv_sem, copy_sem):
    enter_barrier(nseq)
    copies = start_gather(nseq, a_ref, a_out, send_sem, recv_sem, copy_sem)
    for copy in copies:
        copy.start()
    for copy in copies:
        copy.wait()


def seq_gather(a, nseq):
    any_spec = pl.BlockSpec(memory_space=pl.ANY)
    return pl.pallas_call(
        functools.partial(gather_kernel, nseq),
        in_specs=[any_spec],
        out_specs=any_spec,
        out_shape=jax.ShapeDtypeStruct((nseq,) + a.shape, a.dtype),
        scratch_shapes=[
            pltpu.SemaphoreType.DMA((nseq - 1,)),
            pltpu.SemaphoreType.DMA((nseq - 1,)),
            pltpu.SemaphoreType.DMA(()),
        ],
        compiler_params=pltpu.CompilerParams(collective_id=0, has_side_effects=True),
    )(a)


DP = ("dpy", "dpz", "dpc")
SQ = ("sqy", "sqx")


def local(inputs, d_output, loss_mask, queries, keys, values, out_weight, block_mask):
    sizes = {name: lax.axis_size(name) for name in DP + SQ}
    half = lax.axis_index("sqy")
    other = 1 - half
    col = lax.axis_index("sqx")
    head = half * sizes["sqx"] + col
    partner_head = other * sizes["sqx"] + col
    swap = [(0, 1), (1, 0)]
    masked = d_output[0] * loss_mask[0][:, None].astype(jnp.bfloat16)
    own_rows, width = out_weight.shape
    gathered = lax.all_gather(out_weight, ("dpy", "dpc"), axis=0).reshape((2, 2) + out_weight.shape)
    gathered = lax.all_gather(gathered, "dpz", axis=0)
    gathered = jnp.transpose(gathered, (1, 0, 2, 3, 4)).reshape(-1, width)
    head_weight = lax.dynamic_slice_in_dim(gathered, head * HD, HD, 0)
    partner_weight = lax.dynamic_slice_in_dim(gathered, partner_head * HD, HD, 0)
    masked_half = seq_gather(masked, sizes["sqx"]).reshape(-1, width)
    half_len = masked_half.shape[0]
    nt = (((1,), (1,)), ((), ()))
    d_own = lax.dot_general(masked_half, head_weight, nt, preferred_element_type=jnp.float32).astype(jnp.bfloat16)
    d_give = lax.dot_general(masked_half, partner_weight, nt, preferred_element_type=jnp.float32).astype(jnp.bfloat16)
    d_got = lax.ppermute(d_give, "sqy", swap)
    d_attn = jnp.zeros((2 * half_len, HD), jnp.bfloat16)
    d_attn = lax.dynamic_update_slice_in_dim(d_attn, d_own, half * half_len, 0)
    d_attn = lax.dynamic_update_slice_in_dim(d_attn, d_got, other * half_len, 0)
    blocks = block_mask[0, 0]
    live_cols = jnp.repeat(blocks, BLOCK, axis=1)[:, None, :]
    d_query, attended, d_key, d_value, inputs_half = attention_backward(
        queries[0, :, 0], keys[0, :, 0], values[0, :, 0], d_attn, live_cols, inputs[0], sizes["sqx"]
    )
    inputs_half = inputs_half.reshape(-1, width)
    grads = jnp.stack([d_query, d_key, d_value, attended])
    grads_own = lax.dynamic_slice_in_dim(grads, half * half_len, half_len, 1)
    grads_give = lax.dynamic_slice_in_dim(grads, other * half_len, half_len, 1)
    grads_got = lax.ppermute(grads_give, "sqy", swap)
    tn = (((0,), (0,)), ((), ()))

    def terms_of(parts):
        return jnp.stack(
            [
                lax.dot_general(parts[0], inputs_half, tn, preferred_element_type=jnp.float32),
                lax.dot_general(parts[1], inputs_half, tn, preferred_element_type=jnp.float32),
                lax.dot_general(parts[2], inputs_half, tn, preferred_element_type=jnp.float32),
                lax.dot_general(parts[3], masked_half, tn, preferred_element_type=jnp.float32),
            ],
            axis=0,
        )

    terms = jnp.stack([terms_of(grads_own), terms_of(grads_got)])
    ny, nz, nc = sizes["dpy"], sizes["dpz"], sizes["dpc"]
    chunk = terms.shape[2] // (ny * nz * nc)
    terms = terms.reshape(2, 4, ny, nz, nc, chunk, width)
    core = lax.axis_index("dpc")
    kept = lax.dynamic_index_in_dim(terms, core, 4, keepdims=False)
    sent = lax.dynamic_index_in_dim(terms, 1 - core, 4, keepdims=False)
    terms = kept + lax.ppermute(sent, "dpc", swap)
    terms = jnp.transpose(terms, (3, 0, 1, 2, 4, 5))
    terms = lax.psum_scatter(terms.reshape(nz, -1, 128), "dpz", scatter_dimension=0, tiled=True)
    terms = terms.reshape(2, 4, ny, chunk, width)
    row = lax.axis_index("dpy")
    mine = lax.dynamic_index_in_dim(terms, row, 2, keepdims=False)
    theirs = lax.dynamic_index_in_dim(terms, 1 - row, 2, keepdims=False)
    cross = [(0, 3), (3, 0), (1, 2), (2, 1)]
    owned = (
        mine[0]
        + lax.ppermute(theirs[0], "dpy", swap)
        + lax.ppermute(mine[1], "sqy", swap)
        + lax.ppermute(theirs[1], ("dpy", "sqy"), cross)
    )
    owned = jnp.transpose(owned, (1, 0, 2))
    return tuple(owned[:, part][:, None, :] for part in range(4))


def solution(mesh):
    dp, seq = mesh.devices.shape
    devices = mesh.devices.reshape(2, dp // 4, 2, 2, seq // 2)
    fine = jax.sharding.Mesh(devices, DP + SQ)
    in_specs = (
        P(DP, SQ, None),
        P(DP, SQ, None),
        P(DP, SQ),
        P(DP, None, SQ, None),
        P(DP, None, SQ, None),
        P(DP, None, SQ, None),
        P(DP, None),
        P(DP, SQ, None, None),
    )
    out_specs = (
        P(DP, SQ, None),
        P(DP, SQ, None),
        P(DP, SQ, None),
        P(DP, SQ, None),
    )
    return jax.shard_map(local, mesh=fine, in_specs=in_specs, out_specs=out_specs, check_vma=False)
```

```python
import functools

import jax
import jax.numpy as jnp
from jax import lax
from jax.experimental import pallas as pl
from jax.experimental.pallas import tpu as pltpu
from jax.sharding import PartitionSpec as P

HD = 128
BLOCK = 128
ROWS = 256

masked_score = -1e30


def attention_kernel(
    nseq, q_ref, k_ref, v_ref, g_ref, m_ref, x_ref, x_buf, dq_ref, att_ref, dk_ref, dv_ref, x_out,
    dk_acc, dv_acc, send_sem, recv_sem, copy_sem,
):
    step = pl.program_id(0)
    steps = pl.num_programs(0)
    scale = HD ** (-0.5)
    groups = ROWS // BLOCK
    far = [off for off in range(1, nseq) if min(off, nseq - off) > 1]
    copies = start_gather(nseq, x_ref, x_out, send_sem, recv_sem, copy_sem, far, local=False)

    @pl.when(step == 0)
    def _():
        enter_barrier(nseq)
        for copy in copies:
            copy.start()
        dk_acc[...] = jnp.zeros_like(dk_acc)
        dv_acc[...] = jnp.zeros_like(dv_acc)

    q = q_ref[...]
    k = k_ref[...]
    v = v_ref[...]
    g = g_ref[...]
    length = k.shape[0]
    nt = (((1,), (1,)), ((), ()))
    tn = (((0,), (0,)), ((), ()))
    scores = lax.dot_general(q, k, nt, preferred_element_type=jnp.float32) * scale
    live = m_ref[...]
    scores = scores.reshape(groups, BLOCK, length)
    scores = jnp.where(live > 0, scores, masked_score).reshape(ROWS, length)
    row_max = jnp.max(scores, axis=1, keepdims=True)
    weights = jnp.exp(scores - row_max)
    row_total = jnp.sum(weights, axis=1, keepdims=True)
    prob = weights / row_total
    prob_low = prob.astype(jnp.bfloat16)
    attended = jnp.dot(prob_low, v, preferred_element_type=jnp.float32).astype(jnp.bfloat16)
    row_delta = jnp.sum(g.astype(jnp.float32) * attended.astype(jnp.float32), axis=1, keepdims=True)
    d_prob = lax.dot_general(g, v, nt, preferred_element_type=jnp.float32)
    d_score = (prob * (d_prob - row_delta)).astype(jnp.bfloat16)
    dq_ref[...] = (jnp.dot(d_score, k, preferred_element_type=jnp.float32) * scale).astype(jnp.bfloat16)
    att_ref[...] = attended
    dk_acc[...] += lax.dot_general(q, d_score, tn, preferred_element_type=jnp.float32)
    dv_acc[...] += lax.dot_general(g, prob_low, tn, preferred_element_type=jnp.float32)

    @pl.when(step == steps - 1)
    def _():
        dk_ref[...] = (dk_acc[...].T * scale).astype(jnp.bfloat16)
        dv_ref[...] = dv_acc[...].T.astype(jnp.bfloat16)
        for copy in copies:
            copy.wait()


def attention_backward(q, k, v, g, live_cols, x, x_buf, nseq):
    length = q.shape[0]
    row_spec = pl.BlockSpec((ROWS, HD), lambda i: (i, 0))
    full_spec = pl.BlockSpec((length, HD), lambda i: (0, 0))
    mask_spec = pl.BlockSpec((ROWS // BLOCK, 1, length), lambda i: (i, 0, 0))
    out = jax.ShapeDtypeStruct((length, HD), jnp.bfloat16)
    flops = 12 * length * length * HD
    any_spec = pl.BlockSpec(memory_space=pl.ANY)
    return pl.pallas_call(
        functools.partial(attention_kernel, nseq),
        grid=(length // ROWS,),
        in_specs=[row_spec, full_spec, full_spec, row_spec, mask_spec, any_spec, any_spec],
        out_specs=[row_spec, row_spec, full_spec, full_spec, any_spec],
        out_shape=[out, out, out, out, jax.ShapeDtypeStruct(x_buf.shape, x_buf.dtype)],
        input_output_aliases={6: 4},
        scratch_shapes=[
            pltpu.VMEM((HD, length), jnp.float32),
            pltpu.VMEM((HD, length), jnp.float32),
            pltpu.SemaphoreType.DMA((nseq - 1,)),
            pltpu.SemaphoreType.DMA((nseq - 1,)),
            pltpu.SemaphoreType.DMA(()),
        ],
        compiler_params=pltpu.CompilerParams(
            vmem_limit_bytes=48 * 1024 * 1024, collective_id=1, has_side_effects=True
        ),
        cost_estimate=pl.CostEstimate(
            flops=flops, transcendentals=length * length, bytes_accessed=8 * length * HD * 2
        ),
    )(q, k, v, g, live_cols, x, x_buf)


def start_gather(nseq, src, dst, send_sem, recv_sem, copy_sem, offsets=None, local=True):
    me = lax.axis_index("sqx")
    copies = [pltpu.make_async_copy(src, dst.at[me], copy_sem)] if local else []
    for off in offsets or range(1, nseq):
        peer = (me + off) % nseq
        copies.append(
            pltpu.make_async_remote_copy(
                src_ref=src,
                dst_ref=dst.at[me],
                send_sem=send_sem.at[off - 1],
                recv_sem=recv_sem.at[off - 1],
                device_id={"sqx": peer},
                device_id_type=pl.DeviceIdType.MESH,
            )
        )
    return copies


def enter_barrier(nseq):
    me = lax.axis_index("sqx")
    barrier = pltpu.get_barrier_semaphore()
    for off in range(1, nseq):
        peer = (me + off) % nseq
        pl.semaphore_signal(barrier, 1, device_id={"sqx": peer}, device_id_type=pl.DeviceIdType.MESH)
    pl.semaphore_wait(barrier, nseq - 1)


def gather_kernel(nseq, a_ref, b_ref, a_out, b_out, send_sem, recv_sem, copy_sem):
    enter_barrier(nseq)
    copies = start_gather(nseq, a_ref, a_out, send_sem.at[0], recv_sem.at[0], copy_sem.at[0])
    near = [off for off in range(1, nseq) if min(off, nseq - off) == 1]
    copies += start_gather(nseq, b_ref, b_out, send_sem.at[1], recv_sem.at[1], copy_sem.at[1], near)
    for copy in copies:
        copy.start()
    for copy in copies:
        copy.wait()


def seq_gather(a, b, nseq):
    any_spec = pl.BlockSpec(memory_space=pl.ANY)
    return pl.pallas_call(
        functools.partial(gather_kernel, nseq),
        in_specs=[any_spec, any_spec],
        out_specs=[any_spec, any_spec],
        out_shape=[
            jax.ShapeDtypeStruct((nseq,) + a.shape, a.dtype),
            jax.ShapeDtypeStruct((nseq,) + b.shape, b.dtype),
        ],
        scratch_shapes=[
            pltpu.SemaphoreType.DMA((2, nseq - 1)),
            pltpu.SemaphoreType.DMA((2, nseq - 1)),
            pltpu.SemaphoreType.DMA((2,)),
        ],
        compiler_params=pltpu.CompilerParams(collective_id=0, has_side_effects=True),
    )(a, b)


DP = ("dpy", "dpz", "dpc")
SQ = ("sqy", "sqx")


def local(inputs, d_output, loss_mask, queries, keys, values, out_weight, block_mask):
    sizes = {name: lax.axis_size(name) for name in DP + SQ}
    half = lax.axis_index("sqy")
    other = 1 - half
    col = lax.axis_index("sqx")
    head = half * sizes["sqx"] + col
    partner_head = other * sizes["sqx"] + col
    swap = [(0, 1), (1, 0)]
    masked = d_output[0] * loss_mask[0][:, None].astype(jnp.bfloat16)
    own_rows, width = out_weight.shape
    gathered = lax.all_gather(out_weight, ("dpy", "dpc"), axis=0).reshape((2, 2) + out_weight.shape)
    gathered = lax.all_gather(gathered, "dpz", axis=0)
    gathered = jnp.transpose(gathered, (1, 0, 2, 3, 4)).reshape(-1, width)
    head_weight = lax.dynamic_slice_in_dim(gathered, head * HD, HD, 0)
    partner_weight = lax.dynamic_slice_in_dim(gathered, partner_head * HD, HD, 0)
    masked_half, inputs_near = seq_gather(masked, inputs[0], sizes["sqx"])
    masked_half = masked_half.reshape(-1, width)
    half_len = masked_half.shape[0]
    nt = (((1,), (1,)), ((), ()))
    d_own = lax.dot_general(masked_half, head_weight, nt, preferred_element_type=jnp.float32).astype(jnp.bfloat16)
    d_give = lax.dot_general(masked_half, partner_weight, nt, preferred_element_type=jnp.float32).astype(jnp.bfloat16)
    d_got = lax.ppermute(d_give, "sqy", swap)
    d_attn = jnp.zeros((2 * half_len, HD), jnp.bfloat16)
    d_attn = lax.dynamic_update_slice_in_dim(d_attn, d_own, half * half_len, 0)
    d_attn = lax.dynamic_update_slice_in_dim(d_attn, d_got, other * half_len, 0)
    blocks = block_mask[0, 0]
    live_cols = jnp.repeat(blocks, BLOCK, axis=1)[:, None, :]
    d_query, attended, d_key, d_value, inputs_half = attention_backward(
        queries[0, :, 0], keys[0, :, 0], values[0, :, 0], d_attn, live_cols, inputs[0], inputs_near, sizes["sqx"]
    )
    inputs_half = inputs_half.reshape(-1, width)
    grads = jnp.stack([d_query, d_key, d_value, attended])
    grads_own = lax.dynamic_slice_in_dim(grads, half * half_len, half_len, 1)
    grads_give = lax.dynamic_slice_in_dim(grads, other * half_len, half_len, 1)
    grads_got = lax.ppermute(grads_give, "sqy", swap)
    tn = (((0,), (0,)), ((), ()))

    def terms_of(parts):
        return jnp.stack(
            [
                lax.dot_general(parts[0], inputs_half, tn, preferred_element_type=jnp.float32),
                lax.dot_general(parts[1], inputs_half, tn, preferred_element_type=jnp.float32),
                lax.dot_general(parts[2], inputs_half, tn, preferred_element_type=jnp.float32),
                lax.dot_general(parts[3], masked_half, tn, preferred_element_type=jnp.float32),
            ],
            axis=0,
        )

    terms = jnp.stack([terms_of(grads_own), terms_of(grads_got)])
    ny, nz, nc = sizes["dpy"], sizes["dpz"], sizes["dpc"]
    chunk = terms.shape[2] // (ny * nz * nc)
    terms = terms.reshape(2, 4, ny, nz, nc, chunk, width)
    core = lax.axis_index("dpc")
    kept = lax.dynamic_index_in_dim(terms, core, 4, keepdims=False)
    sent = lax.dynamic_index_in_dim(terms, 1 - core, 4, keepdims=False)
    terms = kept + lax.ppermute(sent, "dpc", swap)
    terms = jnp.transpose(terms, (3, 0, 1, 2, 4, 5))
    terms = lax.psum_scatter(terms.reshape(nz, -1, 128), "dpz", scatter_dimension=0, tiled=True)
    terms = terms.reshape(2, 4, ny, chunk, width)
    row = lax.axis_index("dpy")
    mine = lax.dynamic_index_in_dim(terms, row, 2, keepdims=False)
    theirs = lax.dynamic_index_in_dim(terms, 1 - row, 2, keepdims=False)
    cross = [(0, 3), (3, 0), (1, 2), (2, 1)]
    owned = (
        mine[0]
        + lax.ppermute(theirs[0], "dpy", swap)
        + lax.ppermute(mine[1], "sqy", swap)
        + lax.ppermute(theirs[1], ("dpy", "sqy"), cross)
    )
    owned = jnp.transpose(owned, (1, 0, 2))
    return tuple(owned[:, part][:, None, :] for part in range(4))


def solution(mesh):
    dp, seq = mesh.devices.shape
    devices = mesh.devices.reshape(2, dp // 4, 2, 2, seq // 2)
    fine = jax.sharding.Mesh(devices, DP + SQ)
    in_specs = (
        P(DP, SQ, None),
        P(DP, SQ, None),
        P(DP, SQ),
        P(DP, None, SQ, None),
        P(DP, None, SQ, None),
        P(DP, None, SQ, None),
        P(DP, None),
        P(DP, SQ, None, None),
    )
    out_specs = (
        P(DP, SQ, None),
        P(DP, SQ, None),
        P(DP, SQ, None),
        P(DP, SQ, None),
    )
    return jax.shard_map(local, mesh=fine, in_specs=in_specs, out_specs=out_specs, check_vma=False)
```

```python
import functools

import jax
import jax.numpy as jnp
from jax import lax
from jax.experimental import pallas as pl
from jax.experimental.pallas import tpu as pltpu
from jax.sharding import PartitionSpec as P

HD = 128
BLOCK = 128
ROWS = 256

masked_score = -1e30


def attention_kernel(
    nseq, q_ref, k_ref, v_ref, g_ref, m_ref, x_ref, dq_ref, att_ref, dk_ref, dv_ref, x_out,
    dk_acc, dv_acc, send_sem, recv_sem, copy_sem,
):
    step = pl.program_id(0)
    steps = pl.num_programs(0)
    scale = HD ** (-0.5)
    groups = ROWS // BLOCK
    copies = start_gather(nseq, x_ref, x_out, send_sem, recv_sem, copy_sem, local=False)

    @pl.when(step == 0)
    def _():
        enter_barrier(nseq)
        for copy in copies:
            copy.start()
        dk_acc[...] = jnp.zeros_like(dk_acc)
        dv_acc[...] = jnp.zeros_like(dv_acc)

    q = q_ref[...]
    k = k_ref[...]
    v = v_ref[...]
    g = g_ref[...]
    length = k.shape[0]
    nt = (((1,), (1,)), ((), ()))
    tn = (((0,), (0,)), ((), ()))
    scores = lax.dot_general(q, k, nt, preferred_element_type=jnp.float32) * scale
    live = m_ref[...]
    scores = scores.reshape(groups, BLOCK, length)
    scores = jnp.where(live > 0, scores, masked_score).reshape(ROWS, length)
    row_max = jnp.max(scores, axis=1, keepdims=True)
    weights = jnp.exp(scores - row_max)
    row_total = jnp.sum(weights, axis=1, keepdims=True)
    prob = weights / row_total
    prob_low = prob.astype(jnp.bfloat16)
    attended = jnp.dot(prob_low, v, preferred_element_type=jnp.float32).astype(jnp.bfloat16)
    row_delta = jnp.sum(g.astype(jnp.float32) * attended.astype(jnp.float32), axis=1, keepdims=True)
    d_prob = lax.dot_general(g, v, nt, preferred_element_type=jnp.float32)
    d_score = (prob * (d_prob - row_delta)).astype(jnp.bfloat16)
    dq_ref[...] = (jnp.dot(d_score, k, preferred_element_type=jnp.float32) * scale).astype(jnp.bfloat16)
    att_ref[...] = attended
    dk_acc[...] += lax.dot_general(q, d_score, tn, preferred_element_type=jnp.float32)
    dv_acc[...] += lax.dot_general(g, prob_low, tn, preferred_element_type=jnp.float32)

    @pl.when(step == steps - 1)
    def _():
        dk_ref[...] = (dk_acc[...].T * scale).astype(jnp.bfloat16)
        dv_ref[...] = dv_acc[...].T.astype(jnp.bfloat16)
        for copy in copies:
            copy.wait()


def attention_backward(q, k, v, g, live_cols, x, nseq):
    length = q.shape[0]
    row_spec = pl.BlockSpec((ROWS, HD), lambda i: (i, 0))
    full_spec = pl.BlockSpec((length, HD), lambda i: (0, 0))
    mask_spec = pl.BlockSpec((ROWS // BLOCK, 1, length), lambda i: (i, 0, 0))
    out = jax.ShapeDtypeStruct((length, HD), jnp.bfloat16)
    flops = 12 * length * length * HD
    any_spec = pl.BlockSpec(memory_space=pl.ANY)
    return pl.pallas_call(
        functools.partial(attention_kernel, nseq),
        grid=(length // ROWS,),
        in_specs=[row_spec, full_spec, full_spec, row_spec, mask_spec, any_spec],
        out_specs=[row_spec, row_spec, full_spec, full_spec, any_spec],
        out_shape=[out, out, out, out, jax.ShapeDtypeStruct((nseq,) + x.shape, x.dtype)],
        scratch_shapes=[
            pltpu.VMEM((HD, length), jnp.float32),
            pltpu.VMEM((HD, length), jnp.float32),
            pltpu.SemaphoreType.DMA((nseq - 1,)),
            pltpu.SemaphoreType.DMA((nseq - 1,)),
            pltpu.SemaphoreType.DMA(()),
        ],
        compiler_params=pltpu.CompilerParams(
            vmem_limit_bytes=48 * 1024 * 1024, collective_id=1, has_side_effects=True
        ),
        cost_estimate=pl.CostEstimate(
            flops=flops, transcendentals=length * length, bytes_accessed=8 * length * HD * 2
        ),
    )(q, k, v, g, live_cols, x)


def start_gather(nseq, src, dst, send_sem, recv_sem, copy_sem, local=True):
    me = lax.axis_index("sqx")
    copies = [pltpu.make_async_copy(src, dst.at[me], copy_sem)] if local else []
    for off in range(1, nseq):
        peer = (me + off) % nseq
        copies.append(
            pltpu.make_async_remote_copy(
                src_ref=src,
                dst_ref=dst.at[me],
                send_sem=send_sem.at[off - 1],
                recv_sem=recv_sem.at[off - 1],
                device_id={"sqx": peer},
                device_id_type=pl.DeviceIdType.MESH,
            )
        )
    return copies


def enter_barrier(nseq):
    me = lax.axis_index("sqx")
    barrier = pltpu.get_barrier_semaphore()
    for off in range(1, nseq):
        peer = (me + off) % nseq
        pl.semaphore_signal(barrier, 1, device_id={"sqx": peer}, device_id_type=pl.DeviceIdType.MESH)
    pl.semaphore_wait(barrier, nseq - 1)


def gather_kernel(nseq, a_ref, a_out, send_sem, recv_sem, copy_sem):
    enter_barrier(nseq)
    copies = start_gather(nseq, a_ref, a_out, send_sem, recv_sem, copy_sem)
    for copy in copies:
        copy.start()
    for copy in copies:
        copy.wait()


def seq_gather(a, nseq):
    any_spec = pl.BlockSpec(memory_space=pl.ANY)
    return pl.pallas_call(
        functools.partial(gather_kernel, nseq),
        in_specs=[any_spec],
        out_specs=any_spec,
        out_shape=jax.ShapeDtypeStruct((nseq,) + a.shape, a.dtype),
        scratch_shapes=[
            pltpu.SemaphoreType.DMA((nseq - 1,)),
            pltpu.SemaphoreType.DMA((nseq - 1,)),
            pltpu.SemaphoreType.DMA(()),
        ],
        compiler_params=pltpu.CompilerParams(collective_id=0, has_side_effects=True),
    )(a)


DP = ("dpy", "dpz", "dpc")
SQ = ("sqy", "sqx")


def local(inputs, d_output, loss_mask, queries, keys, values, out_weight, block_mask):
    sizes = {name: lax.axis_size(name) for name in DP + SQ}
    half = lax.axis_index("sqy")
    other = 1 - half
    col = lax.axis_index("sqx")
    head = half * sizes["sqx"] + col
    partner_head = other * sizes["sqx"] + col
    swap = [(0, 1), (1, 0)]
    masked = d_output[0] * loss_mask[0][:, None].astype(jnp.bfloat16)
    own_rows, width = out_weight.shape
    gathered = lax.all_gather(out_weight, ("dpy", "dpc"), axis=0).reshape((2, 2) + out_weight.shape)
    gathered = lax.all_gather(gathered, "dpz", axis=0)
    gathered = jnp.transpose(gathered, (1, 0, 2, 3, 4)).reshape(-1, width)
    head_weight = lax.dynamic_slice_in_dim(gathered, head * HD, HD, 0)
    partner_weight = lax.dynamic_slice_in_dim(gathered, partner_head * HD, HD, 0)
    masked_half = seq_gather(masked, sizes["sqx"]).reshape(-1, width)
    half_len = masked_half.shape[0]
    nt = (((1,), (1,)), ((), ()))
    d_own = lax.dot_general(masked_half, head_weight, nt, preferred_element_type=jnp.float32).astype(jnp.bfloat16)
    d_give = lax.dot_general(masked_half, partner_weight, nt, preferred_element_type=jnp.float32).astype(jnp.bfloat16)
    d_got = lax.ppermute(d_give, "sqy", swap)
    d_attn = jnp.zeros((2 * half_len, HD), jnp.bfloat16)
    d_attn = lax.dynamic_update_slice_in_dim(d_attn, d_own, half * half_len, 0)
    d_attn = lax.dynamic_update_slice_in_dim(d_attn, d_got, other * half_len, 0)
    blocks = block_mask[0, 0]
    live_cols = jnp.repeat(blocks, BLOCK, axis=1)[:, None, :]
    d_query, attended, d_key, d_value, inputs_half = attention_backward(
        queries[0, :, 0], keys[0, :, 0], values[0, :, 0], d_attn, live_cols, inputs[0], sizes["sqx"]
    )
    inputs_half = lax.dynamic_update_index_in_dim(inputs_half, inputs[0], col, 0).reshape(-1, width)
    grads = jnp.stack([d_query, d_key, d_value, attended])
    grads_own = lax.dynamic_slice_in_dim(grads, half * half_len, half_len, 1)
    grads_give = lax.dynamic_slice_in_dim(grads, other * half_len, half_len, 1)
    grads_got = lax.ppermute(grads_give, "sqy", swap)
    tn = (((0,), (0,)), ((), ()))

    def terms_of(parts):
        return jnp.stack(
            [
                lax.dot_general(parts[0], inputs_half, tn, preferred_element_type=jnp.float32),
                lax.dot_general(parts[1], inputs_half, tn, preferred_element_type=jnp.float32),
                lax.dot_general(parts[2], inputs_half, tn, preferred_element_type=jnp.float32),
                lax.dot_general(parts[3], masked_half, tn, preferred_element_type=jnp.float32),
            ],
            axis=0,
        )

    terms = jnp.stack([terms_of(grads_own), terms_of(grads_got)])
    ny, nz, nc = sizes["dpy"], sizes["dpz"], sizes["dpc"]
    chunk = terms.shape[2] // (ny * nz * nc)
    terms = terms.reshape(2, 4, ny, nz, nc, chunk, width)
    core = lax.axis_index("dpc")
    kept = lax.dynamic_index_in_dim(terms, core, 4, keepdims=False)
    sent = lax.dynamic_index_in_dim(terms, 1 - core, 4, keepdims=False)
    terms = kept + lax.ppermute(sent, "dpc", swap)
    terms = jnp.transpose(terms, (3, 0, 1, 2, 4, 5))
    terms = lax.psum_scatter(terms.reshape(nz, -1, 128), "dpz", scatter_dimension=0, tiled=True)
    terms = terms.reshape(2, 4, ny, chunk, width)
    row = lax.axis_index("dpy")
    mine = lax.dynamic_index_in_dim(terms, row, 2, keepdims=False)
    theirs = lax.dynamic_index_in_dim(terms, 1 - row, 2, keepdims=False)
    cross = [(0, 3), (3, 0), (1, 2), (2, 1)]
    owned = (
        mine[0]
        + lax.ppermute(theirs[0], "dpy", swap)
        + lax.ppermute(mine[1], "sqy", swap)
        + lax.ppermute(theirs[1], ("dpy", "sqy"), cross)
    )
    owned = jnp.transpose(owned, (1, 0, 2))
    return tuple(owned[:, part][:, None, :] for part in range(4))


def solution(mesh):
    dp, seq = mesh.devices.shape
    devices = mesh.devices.reshape(2, dp // 4, 2, 2, seq // 2)
    fine = jax.sharding.Mesh(devices, DP + SQ)
    in_specs = (
        P(DP, SQ, None),
        P(DP, SQ, None),
        P(DP, SQ),
        P(DP, None, SQ, None),
        P(DP, None, SQ, None),
        P(DP, None, SQ, None),
        P(DP, None),
        P(DP, SQ, None, None),
    )
    out_specs = (
        P(DP, SQ, None),
        P(DP, SQ, None),
        P(DP, SQ, None),
        P(DP, SQ, None),
    )
    return jax.shard_map(local, mesh=fine, in_specs=in_specs, out_specs=out_specs, check_vma=False)
```

```python
import functools

import jax
import jax.numpy as jnp
from jax import lax
from jax.experimental import pallas as pl
from jax.experimental.pallas import tpu as pltpu
from jax.sharding import PartitionSpec as P

HD = 128
BLOCK = 128
ROWS = 256

masked_score = -1e30


def attention_kernel(
    nseq, q_ref, k_ref, v_ref, g_ref, m_ref, x_ref, dq_ref, att_ref, dk_ref, dv_ref, x_out,
    dk_acc, dv_acc, send_sem, recv_sem, copy_sem,
):
    step = pl.program_id(0)
    steps = pl.num_programs(0)
    scale = HD ** (-0.5)
    groups = ROWS // BLOCK
    copies = start_gather(nseq, x_ref, x_out, send_sem, recv_sem, copy_sem)

    @pl.when(step == 0)
    def _():
        enter_barrier(nseq)
        for copy in copies:
            copy.start()
        dk_acc[...] = jnp.zeros_like(dk_acc)
        dv_acc[...] = jnp.zeros_like(dv_acc)

    q = q_ref[...]
    k = k_ref[...]
    v = v_ref[...]
    g = g_ref[...]
    length = k.shape[0]
    nt = (((1,), (1,)), ((), ()))
    tn = (((0,), (0,)), ((), ()))
    scores = lax.dot_general(q, k, nt, preferred_element_type=jnp.float32) * scale
    live = m_ref[...]
    scores = scores.reshape(groups, BLOCK, length)
    scores = jnp.where(live > 0, scores, masked_score).reshape(ROWS, length)
    row_max = jnp.max(scores, axis=1, keepdims=True)
    weights = jnp.exp(scores - row_max)
    row_total = jnp.sum(weights, axis=1, keepdims=True)
    prob = weights / row_total
    prob_low = prob.astype(jnp.bfloat16)
    attended = jnp.dot(prob_low, v, preferred_element_type=jnp.float32).astype(jnp.bfloat16)
    row_delta = jnp.sum(g.astype(jnp.float32) * attended.astype(jnp.float32), axis=1, keepdims=True)
    d_prob = lax.dot_general(g, v, nt, preferred_element_type=jnp.float32)
    d_score = (prob * (d_prob - row_delta)).astype(jnp.bfloat16)
    dq_ref[...] = (jnp.dot(d_score, k, preferred_element_type=jnp.float32) * scale).astype(jnp.bfloat16)
    att_ref[...] = attended
    dk_acc[...] += lax.dot_general(q, d_score, tn, preferred_element_type=jnp.float32)
    dv_acc[...] += lax.dot_general(g, prob_low, tn, preferred_element_type=jnp.float32)

    @pl.when(step == steps - 1)
    def _():
        dk_ref[...] = (dk_acc[...].T * scale).astype(jnp.bfloat16)
        dv_ref[...] = dv_acc[...].T.astype(jnp.bfloat16)
        for copy in copies:
            copy.wait()


def attention_backward(q, k, v, g, live_cols, x, nseq):
    length = q.shape[0]
    row_spec = pl.BlockSpec((ROWS, HD), lambda i: (i, 0))
    full_spec = pl.BlockSpec((length, HD), lambda i: (0, 0))
    mask_spec = pl.BlockSpec((ROWS // BLOCK, 1, length), lambda i: (i, 0, 0))
    out = jax.ShapeDtypeStruct((length, HD), jnp.bfloat16)
    flops = 12 * length * length * HD
    any_spec = pl.BlockSpec(memory_space=pl.ANY)
    return pl.pallas_call(
        functools.partial(attention_kernel, nseq),
        grid=(length // ROWS,),
        in_specs=[row_spec, full_spec, full_spec, row_spec, mask_spec, any_spec],
        out_specs=[row_spec, row_spec, full_spec, full_spec, any_spec],
        out_shape=[out, out, out, out, jax.ShapeDtypeStruct((nseq,) + x.shape, x.dtype)],
        scratch_shapes=[
            pltpu.VMEM((HD, length), jnp.float32),
            pltpu.VMEM((HD, length), jnp.float32),
            pltpu.SemaphoreType.DMA((nseq - 1,)),
            pltpu.SemaphoreType.DMA((nseq - 1,)),
            pltpu.SemaphoreType.DMA(()),
        ],
        compiler_params=pltpu.CompilerParams(
            vmem_limit_bytes=48 * 1024 * 1024, collective_id=1, has_side_effects=True
        ),
        cost_estimate=pl.CostEstimate(
            flops=flops, transcendentals=length * length, bytes_accessed=8 * length * HD * 2
        ),
    )(q, k, v, g, live_cols, x)


def start_gather(nseq, src, dst, send_sem, recv_sem, copy_sem):
    me = lax.axis_index("sqx")
    copies = [pltpu.make_async_copy(src, dst.at[me], copy_sem)]
    for off in range(1, nseq):
        peer = (me + off) % nseq
        copies.append(
            pltpu.make_async_remote_copy(
                src_ref=src,
                dst_ref=dst.at[me],
                send_sem=send_sem.at[off - 1],
                recv_sem=recv_sem.at[off - 1],
                device_id={"sqx": peer},
                device_id_type=pl.DeviceIdType.MESH,
            )
        )
    return copies


def enter_barrier(nseq):
    me = lax.axis_index("sqx")
    barrier = pltpu.get_barrier_semaphore()
    for off in range(1, nseq):
        peer = (me + off) % nseq
        pl.semaphore_signal(barrier, 1, device_id={"sqx": peer}, device_id_type=pl.DeviceIdType.MESH)
    pl.semaphore_wait(barrier, nseq - 1)


def gather_kernel(nseq, a_ref, a_out, send_sem, recv_sem, copy_sem):
    enter_barrier(nseq)
    copies = start_gather(nseq, a_ref, a_out, send_sem, recv_sem, copy_sem)
    for copy in copies:
        copy.start()
    for copy in copies:
        copy.wait()


def seq_gather(a, nseq):
    any_spec = pl.BlockSpec(memory_space=pl.ANY)
    return pl.pallas_call(
        functools.partial(gather_kernel, nseq),
        in_specs=[any_spec],
        out_specs=any_spec,
        out_shape=jax.ShapeDtypeStruct((nseq,) + a.shape, a.dtype),
        scratch_shapes=[
            pltpu.SemaphoreType.DMA((nseq - 1,)),
            pltpu.SemaphoreType.DMA((nseq - 1,)),
            pltpu.SemaphoreType.DMA(()),
        ],
        compiler_params=pltpu.CompilerParams(collective_id=0, has_side_effects=True),
    )(a)


DP = ("dpy", "dpz", "dpc")
SQ = ("sqy", "sqx")


def local(inputs, d_output, loss_mask, queries, keys, values, out_weight, block_mask):
    sizes = {name: lax.axis_size(name) for name in DP + SQ}
    half = lax.axis_index("sqy")
    other = 1 - half
    col = lax.axis_index("sqx")
    head = half * sizes["sqx"] + col
    partner_head = other * sizes["sqx"] + col
    swap = [(0, 1), (1, 0)]
    masked = d_output[0] * loss_mask[0][:, None].astype(jnp.bfloat16)
    own_rows, width = out_weight.shape
    gathered = lax.all_gather(out_weight, ("dpy", "dpc"), axis=0).reshape((2, 2) + out_weight.shape)
    gathered = lax.all_gather(gathered, "dpz", axis=0)
    gathered = jnp.transpose(gathered, (1, 0, 2, 3, 4)).reshape(-1, width)
    head_weight = lax.dynamic_slice_in_dim(gathered, head * HD, HD, 0)
    partner_weight = lax.dynamic_slice_in_dim(gathered, partner_head * HD, HD, 0)
    masked_half = seq_gather(masked, sizes["sqx"]).reshape(-1, width)
    half_len = masked_half.shape[0]
    nt = (((1,), (1,)), ((), ()))
    d_give = lax.dot_general(masked_half, partner_weight, nt, preferred_element_type=jnp.float32).astype(jnp.bfloat16)
    d_got = lax.ppermute(d_give, "sqy", swap)
    d_give, masked_half, head_weight = lax.optimization_barrier((d_give, masked_half, head_weight))
    d_own = lax.dot_general(masked_half, head_weight, nt, preferred_element_type=jnp.float32).astype(jnp.bfloat16)
    d_attn = jnp.zeros((2 * half_len, HD), jnp.bfloat16)
    d_attn = lax.dynamic_update_slice_in_dim(d_attn, d_own, half * half_len, 0)
    d_attn = lax.dynamic_update_slice_in_dim(d_attn, d_got, other * half_len, 0)
    blocks = block_mask[0, 0]
    live_cols = jnp.repeat(blocks, BLOCK, axis=1)[:, None, :]
    d_query, attended, d_key, d_value, inputs_half = attention_backward(
        queries[0, :, 0], keys[0, :, 0], values[0, :, 0], d_attn, live_cols, inputs[0], sizes["sqx"]
    )
    inputs_half = inputs_half.reshape(-1, width)
    grads = jnp.stack([d_query, d_key, d_value, attended])
    grads_own = lax.dynamic_slice_in_dim(grads, half * half_len, half_len, 1)
    grads_give = lax.dynamic_slice_in_dim(grads, other * half_len, half_len, 1)
    grads_got = lax.ppermute(grads_give, "sqy", swap)
    tn = (((0,), (0,)), ((), ()))

    def terms_of(parts):
        return jnp.stack(
            [
                lax.dot_general(parts[0], inputs_half, tn, preferred_element_type=jnp.float32),
                lax.dot_general(parts[1], inputs_half, tn, preferred_element_type=jnp.float32),
                lax.dot_general(parts[2], inputs_half, tn, preferred_element_type=jnp.float32),
                lax.dot_general(parts[3], masked_half, tn, preferred_element_type=jnp.float32),
            ],
            axis=0,
        )

    terms = jnp.stack([terms_of(grads_own), terms_of(grads_got)])
    ny, nz, nc = sizes["dpy"], sizes["dpz"], sizes["dpc"]
    chunk = terms.shape[2] // (ny * nz * nc)
    terms = terms.reshape(2, 4, ny, nz, nc, chunk, width)
    core = lax.axis_index("dpc")
    kept = lax.dynamic_index_in_dim(terms, core, 4, keepdims=False)
    sent = lax.dynamic_index_in_dim(terms, 1 - core, 4, keepdims=False)
    terms = kept + lax.ppermute(sent, "dpc", swap)
    terms = jnp.transpose(terms, (3, 0, 1, 2, 4, 5))
    terms = lax.psum_scatter(terms.reshape(nz, -1, 128), "dpz", scatter_dimension=0, tiled=True)
    terms = terms.reshape(2, 4, ny, chunk, width)
    row = lax.axis_index("dpy")
    mine = lax.dynamic_index_in_dim(terms, row, 2, keepdims=False)
    theirs = lax.dynamic_index_in_dim(terms, 1 - row, 2, keepdims=False)
    cross = [(0, 3), (3, 0), (1, 2), (2, 1)]
    owned = (
        mine[0]
        + lax.ppermute(theirs[0], "dpy", swap)
        + lax.ppermute(mine[1], "sqy", swap)
        + lax.ppermute(theirs[1], ("dpy", "sqy"), cross)
    )
    owned = jnp.transpose(owned, (1, 0, 2))
    return tuple(owned[:, part][:, None, :] for part in range(4))


def solution(mesh):
    dp, seq = mesh.devices.shape
    devices = mesh.devices.reshape(2, dp // 4, 2, 2, seq // 2)
    fine = jax.sharding.Mesh(devices, DP + SQ)
    in_specs = (
        P(DP, SQ, None),
        P(DP, SQ, None),
        P(DP, SQ),
        P(DP, None, SQ, None),
        P(DP, None, SQ, None),
        P(DP, None, SQ, None),
        P(DP, None),
        P(DP, SQ, None, None),
    )
    out_specs = (
        P(DP, SQ, None),
        P(DP, SQ, None),
        P(DP, SQ, None),
        P(DP, SQ, None),
    )
    return jax.shard_map(local, mesh=fine, in_specs=in_specs, out_specs=out_specs, check_vma=False)
```

```python
import functools

import jax
import jax.numpy as jnp
from jax import lax
from jax.experimental import pallas as pl
from jax.experimental.pallas import tpu as pltpu
from jax.sharding import PartitionSpec as P

HD = 128
BLOCK = 128
ROWS = 512

masked_score = -1e30


def attention_kernel(
    nseq, q_ref, k_ref, v_ref, g_ref, m_ref, x_ref, dq_ref, att_ref, dk_ref, dv_ref, x_out,
    dk_acc, dv_acc, send_sem, recv_sem, copy_sem,
):
    step = pl.program_id(0)
    steps = pl.num_programs(0)
    scale = HD ** (-0.5)
    groups = ROWS // BLOCK
    copies = start_gather(nseq, x_ref, x_out, send_sem, recv_sem, copy_sem)

    @pl.when(step == 0)
    def _():
        enter_barrier(nseq)
        for copy in copies:
            copy.start()
        dk_acc[...] = jnp.zeros_like(dk_acc)
        dv_acc[...] = jnp.zeros_like(dv_acc)

    q = q_ref[...]
    k = k_ref[...]
    v = v_ref[...]
    g = g_ref[...]
    length = k.shape[0]
    nt = (((1,), (1,)), ((), ()))
    tn = (((0,), (0,)), ((), ()))
    scores = lax.dot_general(q, k, nt, preferred_element_type=jnp.float32) * scale
    live = m_ref[...]
    scores = scores.reshape(groups, BLOCK, length)
    scores = jnp.where(live > 0, scores, masked_score).reshape(ROWS, length)
    row_max = jnp.max(scores, axis=1, keepdims=True)
    weights = jnp.exp(scores - row_max)
    row_total = jnp.sum(weights, axis=1, keepdims=True)
    prob = weights / row_total
    prob_low = prob.astype(jnp.bfloat16)
    attended = jnp.dot(prob_low, v, preferred_element_type=jnp.float32).astype(jnp.bfloat16)
    row_delta = jnp.sum(g.astype(jnp.float32) * attended.astype(jnp.float32), axis=1, keepdims=True)
    d_prob = lax.dot_general(g, v, nt, preferred_element_type=jnp.float32)
    d_score = (prob * (d_prob - row_delta)).astype(jnp.bfloat16)
    dq_ref[...] = (jnp.dot(d_score, k, preferred_element_type=jnp.float32) * scale).astype(jnp.bfloat16)
    att_ref[...] = attended
    dk_acc[...] += lax.dot_general(q, d_score, tn, preferred_element_type=jnp.float32)
    dv_acc[...] += lax.dot_general(g, prob_low, tn, preferred_element_type=jnp.float32)

    @pl.when(step == steps - 1)
    def _():
        dk_ref[...] = (dk_acc[...].T * scale).astype(jnp.bfloat16)
        dv_ref[...] = dv_acc[...].T.astype(jnp.bfloat16)
        for copy in copies:
            copy.wait()


def attention_backward(q, k, v, g, live_cols, x, nseq):
    length = q.shape[0]
    row_spec = pl.BlockSpec((ROWS, HD), lambda i: (i, 0))
    full_spec = pl.BlockSpec((length, HD), lambda i: (0, 0))
    mask_spec = pl.BlockSpec((ROWS // BLOCK, 1, length), lambda i: (i, 0, 0))
    out = jax.ShapeDtypeStruct((length, HD), jnp.bfloat16)
    flops = 12 * length * length * HD
    any_spec = pl.BlockSpec(memory_space=pl.ANY)
    return pl.pallas_call(
        functools.partial(attention_kernel, nseq),
        grid=(length // ROWS,),
        in_specs=[row_spec, full_spec, full_spec, row_spec, mask_spec, any_spec],
        out_specs=[row_spec, row_spec, full_spec, full_spec, any_spec],
        out_shape=[out, out, out, out, jax.ShapeDtypeStruct((nseq,) + x.shape, x.dtype)],
        scratch_shapes=[
            pltpu.VMEM((HD, length), jnp.float32),
            pltpu.VMEM((HD, length), jnp.float32),
            pltpu.SemaphoreType.DMA((nseq - 1,)),
            pltpu.SemaphoreType.DMA((nseq - 1,)),
            pltpu.SemaphoreType.DMA(()),
        ],
        compiler_params=pltpu.CompilerParams(
            vmem_limit_bytes=48 * 1024 * 1024, collective_id=1, has_side_effects=True
        ),
        cost_estimate=pl.CostEstimate(
            flops=flops, transcendentals=length * length, bytes_accessed=8 * length * HD * 2
        ),
    )(q, k, v, g, live_cols, x)


def start_gather(nseq, src, dst, send_sem, recv_sem, copy_sem):
    me = lax.axis_index("sqx")
    copies = [pltpu.make_async_copy(src, dst.at[me], copy_sem)]
    for off in range(1, nseq):
        peer = (me + off) % nseq
        copies.append(
            pltpu.make_async_remote_copy(
                src_ref=src,
                dst_ref=dst.at[me],
                send_sem=send_sem.at[off - 1],
                recv_sem=recv_sem.at[off - 1],
                device_id={"sqx": peer},
                device_id_type=pl.DeviceIdType.MESH,
            )
        )
    return copies


def enter_barrier(nseq):
    me = lax.axis_index("sqx")
    barrier = pltpu.get_barrier_semaphore()
    for off in range(1, nseq):
        peer = (me + off) % nseq
        pl.semaphore_signal(barrier, 1, device_id={"sqx": peer}, device_id_type=pl.DeviceIdType.MESH)
    pl.semaphore_wait(barrier, nseq - 1)


def gather_kernel(nseq, a_ref, a_out, send_sem, recv_sem, copy_sem):
    enter_barrier(nseq)
    copies = start_gather(nseq, a_ref, a_out, send_sem, recv_sem, copy_sem)
    for copy in copies:
        copy.start()
    for copy in copies:
        copy.wait()


def seq_gather(a, nseq):
    any_spec = pl.BlockSpec(memory_space=pl.ANY)
    return pl.pallas_call(
        functools.partial(gather_kernel, nseq),
        in_specs=[any_spec],
        out_specs=any_spec,
        out_shape=jax.ShapeDtypeStruct((nseq,) + a.shape, a.dtype),
        scratch_shapes=[
            pltpu.SemaphoreType.DMA((nseq - 1,)),
            pltpu.SemaphoreType.DMA((nseq - 1,)),
            pltpu.SemaphoreType.DMA(()),
        ],
        compiler_params=pltpu.CompilerParams(collective_id=0, has_side_effects=True),
    )(a)


DP = ("dpy", "dpz", "dpc")
SQ = ("sqy", "sqx")


def local(inputs, d_output, loss_mask, queries, keys, values, out_weight, block_mask):
    sizes = {name: lax.axis_size(name) for name in DP + SQ}
    half = lax.axis_index("sqy")
    other = 1 - half
    col = lax.axis_index("sqx")
    head = half * sizes["sqx"] + col
    partner_head = other * sizes["sqx"] + col
    swap = [(0, 1), (1, 0)]
    masked = d_output[0] * loss_mask[0][:, None].astype(jnp.bfloat16)
    own_rows, width = out_weight.shape
    gathered = lax.all_gather(out_weight, ("dpy", "dpc"), axis=0).reshape((2, 2) + out_weight.shape)
    gathered = lax.all_gather(gathered, "dpz", axis=0)
    gathered = jnp.transpose(gathered, (1, 0, 2, 3, 4)).reshape(-1, width)
    head_weight = lax.dynamic_slice_in_dim(gathered, head * HD, HD, 0)
    partner_weight = lax.dynamic_slice_in_dim(gathered, partner_head * HD, HD, 0)
    masked_half = seq_gather(masked, sizes["sqx"]).reshape(-1, width)
    half_len = masked_half.shape[0]
    nt = (((1,), (1,)), ((), ()))
    d_own = lax.dot_general(masked_half, head_weight, nt, preferred_element_type=jnp.float32).astype(jnp.bfloat16)
    d_give = lax.dot_general(masked_half, partner_weight, nt, preferred_element_type=jnp.float32).astype(jnp.bfloat16)
    d_got = lax.ppermute(d_give, "sqy", swap)
    d_attn = jnp.zeros((2 * half_len, HD), jnp.bfloat16)
    d_attn = lax.dynamic_update_slice_in_dim(d_attn, d_own, half * half_len, 0)
    d_attn = lax.dynamic_update_slice_in_dim(d_attn, d_got, other * half_len, 0)
    blocks = block_mask[0, 0]
    live_cols = jnp.repeat(blocks, BLOCK, axis=1)[:, None, :]
    d_query, attended, d_key, d_value, inputs_half = attention_backward(
        queries[0, :, 0], keys[0, :, 0], values[0, :, 0], d_attn, live_cols, inputs[0], sizes["sqx"]
    )
    inputs_half = inputs_half.reshape(-1, width)
    grads = jnp.stack([d_query, d_key, d_value, attended])
    grads_own = lax.dynamic_slice_in_dim(grads, half * half_len, half_len, 1)
    grads_give = lax.dynamic_slice_in_dim(grads, other * half_len, half_len, 1)
    grads_got = lax.ppermute(grads_give, "sqy", swap)
    tn = (((0,), (0,)), ((), ()))

    def terms_of(parts):
        return jnp.stack(
            [
                lax.dot_general(parts[0], inputs_half, tn, preferred_element_type=jnp.float32),
                lax.dot_general(parts[1], inputs_half, tn, preferred_element_type=jnp.float32),
                lax.dot_general(parts[2], inputs_half, tn, preferred_element_type=jnp.float32),
                lax.dot_general(parts[3], masked_half, tn, preferred_element_type=jnp.float32),
            ],
            axis=0,
        )

    terms = jnp.stack([terms_of(grads_own), terms_of(grads_got)])
    ny, nz, nc = sizes["dpy"], sizes["dpz"], sizes["dpc"]
    chunk = terms.shape[2] // (ny * nz * nc)
    terms = terms.reshape(2, 4, ny, nz, nc, chunk, width)
    core = lax.axis_index("dpc")
    kept = lax.dynamic_index_in_dim(terms, core, 4, keepdims=False)
    sent = lax.dynamic_index_in_dim(terms, 1 - core, 4, keepdims=False)
    terms = kept + lax.ppermute(sent, "dpc", swap)
    terms = jnp.transpose(terms, (3, 0, 1, 2, 4, 5))
    terms = lax.psum_scatter(terms.reshape(nz, -1, 128), "dpz", scatter_dimension=0, tiled=True)
    terms = terms.reshape(2, 4, ny, chunk, width)
    row = lax.axis_index("dpy")
    mine = lax.dynamic_index_in_dim(terms, row, 2, keepdims=False)
    theirs = lax.dynamic_index_in_dim(terms, 1 - row, 2, keepdims=False)
    cross = [(0, 3), (3, 0), (1, 2), (2, 1)]
    owned = (
        mine[0]
        + lax.ppermute(theirs[0], "dpy", swap)
        + lax.ppermute(mine[1], "sqy", swap)
        + lax.ppermute(theirs[1], ("dpy", "sqy"), cross)
    )
    owned = jnp.transpose(owned, (1, 0, 2))
    return tuple(owned[:, part][:, None, :] for part in range(4))


def solution(mesh):
    dp, seq = mesh.devices.shape
    devices = mesh.devices.reshape(2, dp // 4, 2, 2, seq // 2)
    fine = jax.sharding.Mesh(devices, DP + SQ)
    in_specs = (
        P(DP, SQ, None),
        P(DP, SQ, None),
        P(DP, SQ),
        P(DP, None, SQ, None),
        P(DP, None, SQ, None),
        P(DP, None, SQ, None),
        P(DP, None),
        P(DP, SQ, None, None),
    )
    out_specs = (
        P(DP, SQ, None),
        P(DP, SQ, None),
        P(DP, SQ, None),
        P(DP, SQ, None),
    )
    return jax.shard_map(local, mesh=fine, in_specs=in_specs, out_specs=out_specs, check_vma=False)
```
